128 devices in a mesh: shot: 4 (over x_lo, core), sub: 32 (over x_hi, z, y).
Axes of the slice: x: 4 (x_hi: 2, x_lo: 2; x = x_hi * 2 + x_lo), y: 4, z: 4, core: 2. Of those that a mesh axis runs over, the one named last changes fastest.
Arguments:
- velocity: float32 [512, 128, 256], P(('shot', 'sub')), may hold values from 1.5 to 4.5
- density: float32 [512, 128, 256], P(('shot', 'sub')), may hold values from 1 to 3
- aperture_start: int32 [4], P('shot'), may hold values from 0 to 96
- source_cell: int32 [4], P('shot'), may hold values from 0 to 4194303
- receiver_cells: int32 [4, 256], P('shot'), may hold values from 0 to 4194303, as said below
- wavelet: float32 [4, 4], P('shot'), may hold values from -6 to 6
- observed: float32 [4, 4, 256], P('shot'), may hold values from -6 to 6
- forward_old: float32 [4, 128, 128, 256], P('shot', 'sub'), may hold values from -6 to 6
- forward_now: float32 [4, 128, 128, 256], P('shot', 'sub'), may hold values from -6 to 6
- adjoint_later: float32 [4, 128, 128, 256], P('shot', 'sub'), may hold values from -6 to 6
- adjoint_now: float32 [4, 128, 128, 256], P('shot', 'sub'), may hold values from -6 to 6
Outputs:
- gradient: float32 [512, 128, 256], P(('shot', 'sub'))
- forward_last: float32 [4, 128, 128, 256], P('shot', 'sub')
- adjoint_first: float32 [4, 128, 128, 256], P('shot', 'sub')
The draws below stay inside these ranges and needn't reach their ends.
Inputs may be any that keep to these rules, and one draw needn't show every extreme that they name: `aperture_start`: the aperture of a shot lies inside the model. `receiver_cells`: several receivers of a shot may share a cell; their injections add up.
All inputs are finite; a program needn't handle non-finite values.
Results may differ from the reference program's by a relative error of at most 0.00002.
Values sent between devices are 32-bit elements; how exact they have to be, the bound alone decides.
No kernel may reach another device: no remote copies, remote signals or barrier semaphores. Data moves between devices by JAX's collectives and lax.ppermute only.
A program may use at most 64 MiB of HBM per device.

```python
import math
import jax
import jax.numpy as jnp
from jax import lax

SLAB = 4
NY = 128
NZ = 256
NREC = 256
STEPS = 4
SHOTS = 4
APERTURE = 128
MODEL_X = 512
N_SHOT = 4
N_SUB = 32


def draw_receiver_cells(key, part):
    cells_key = jax.random.fold_in(key, 17)
    total_cells = APERTURE * NY * NZ
    picked = jax.random.randint(cells_key, (SHOTS, NREC), 0, total_cells, dtype=jnp.int32)
    slot_index = jnp.arange(NREC, dtype=jnp.int32)
    source_slot = jnp.where(slot_index % 8 == 1, slot_index - 1, slot_index)
    picked = picked[:, source_slot]
    picked = picked.at[0, NREC - 1].set(0)
    picked = picked.at[SHOTS - 1, NREC - 2].set(total_cells - 1)
    return picked


def with_ends(array, own_key, least, high):
    longest = array.shape.index(max(array.shape))
    spots = []
    for shift in (0, 1):
        where = [jax.random.randint(jax.random.fold_in(own_key, axis), (), 0, length) for axis, length in enumerate(array.shape)]
        where[longest] = (where[longest] + shift) % array.shape[longest]
        spots.append(tuple(where))
    return array.at[spots[0]].set(least).at[spots[1]].set(high)


def steps_of(own_key, shape, split, low, top_value):
    def one(position, shards_of):
        heights = jax.random.uniform(jax.random.fold_in(jax.random.fold_in(own_key, 6), position), (shards_of,), jnp.float32, low / len(split), top_value / len(split))
        return jnp.repeat(jnp.exp(heights), shape[position] // shards_of).reshape((-1,) + (1,) * (len(shape) - position - 1))

    factor_of = one(*split[0])
    for cut in split[1:]:
        factor_of = factor_of * one(*cut)
    return factor_of


def normal_values(own_key, shape, scale, bound, split=(), kind=jnp.bfloat16):
    result = scale * jax.random.normal(own_key, shape, jnp.float32)
    if split:
        result = result * steps_of(own_key, shape, split, -0.22, 0.18)
    return jnp.clip(result, -bound, bound).astype(kind)


def setup_inputs(seed: int = 0) -> dict:
    streams_of = jax.random.split(jax.random.key(seed), 12)
    return {
        "velocity": jnp.clip(jnp.exp(math.log(4.5) - 1.0986123 * jax.random.uniform(streams_of[0], (MODEL_X, NY, NZ), jnp.float32) ** steps_of(streams_of[0], (MODEL_X, NY, NZ), ((0, 128),), -0.2, 0.2)), 1.5, 4.5),
        "density": jnp.clip(jnp.exp(math.log(3.0) - 1.0986123 * jax.random.uniform(streams_of[1], (MODEL_X, NY, NZ), jnp.float32) ** steps_of(streams_of[1], (MODEL_X, NY, NZ), ((0, 128),), -0.2, 0.2)), 1.0, 3.0),
        "aperture_start": with_ends(jax.random.randint(streams_of[2], (SHOTS,), 0, N_SHOT * N_SUB - N_SUB + 1), jax.random.fold_in(streams_of[2], 1), 0, N_SHOT * N_SUB - N_SUB).astype(jnp.int32),
        "source_cell": with_ends(jax.random.randint(streams_of[3], (SHOTS,), 0, APERTURE * NY * NZ), jax.random.fold_in(streams_of[3], 1), 0, (APERTURE * NY * NZ) - 1).astype(jnp.int32),
        "receiver_cells": draw_receiver_cells(jax.random.fold_in(streams_of[11], 71), 0),
        "wavelet": normal_values(streams_of[5], (SHOTS, STEPS), 1.0, 6.0, ((0, 4),), jnp.float32),
        "observed": normal_values(streams_of[6], (SHOTS, STEPS, NREC), 1.0, 6.0, ((0, 4),), jnp.float32),
        "forward_old": normal_values(streams_of[7], (SHOTS, APERTURE, NY, NZ), 1.0, 6.0, ((0, 4), (1, 32)), jnp.float32),
        "forward_now": normal_values(streams_of[8], (SHOTS, APERTURE, NY, NZ), 1.0, 6.0, ((0, 4), (1, 32)), jnp.float32),
        "adjoint_later": normal_values(streams_of[9], (SHOTS, APERTURE, NY, NZ), 1.0, 6.0, ((0, 4), (1, 32)), jnp.float32),
        "adjoint_now": normal_values(streams_of[10], (SHOTS, APERTURE, NY, NZ), 1.0, 6.0, ((0, 4), (1, 32)), jnp.float32),
    }


lap_coeffs = (-205.0 / 72.0, 8.0 / 5.0, -1.0 / 5.0, 8.0 / 315.0, -1.0 / 560.0)
diff_coeffs = (4.0 / 5.0, -1.0 / 5.0, 4.0 / 105.0, -1.0 / 280.0)
time_step_sq = 0.0088


def offset_view(padded, direction, offset):
    starts = [4, 4, 4]
    starts[direction] = 4 + offset
    extent = [padded.shape[0] - 8, padded.shape[1] - 8, padded.shape[2] - 8]
    return lax.slice(padded, starts, [starts[0] + extent[0], starts[1] + extent[1], starts[2] + extent[2]])


def laplacian(padded):
    summed = 3.0 * lap_coeffs[0] * offset_view(padded, 0, 0)
    for direction in range(3):
        for reach in range(1, 5):
            summed = summed + lap_coeffs[reach] * (offset_view(padded, direction, reach) + offset_view(padded, direction, -reach))
    return summed


def derivative(padded, direction):
    summed = diff_coeffs[0] * (offset_view(padded, direction, 1) - offset_view(padded, direction, -1))
    for reach in range(2, 5):
        summed = summed + diff_coeffs[reach - 1] * (offset_view(padded, direction, reach) - offset_view(padded, direction, -reach))
    return summed


def advance(padded, previous, speed_sq, slopes):
    current = offset_view(padded, 0, 0)
    operator = laplacian(padded)
    for direction in range(3):
        operator = operator - slopes[direction] * derivative(padded, direction)
    return 2.0 * current - previous + speed_sq * operator


def reference(velocity, density, aperture_start, source_cell, receiver_cells, wavelet, observed, forward_old, forward_now, adjoint_later, adjoint_now):
    gradient = jnp.zeros(velocity.shape, jnp.float32)
    forward_outs = []
    adjoint_outs = []
    for shot_index in range(SHOTS):
        first_row = (aperture_start[shot_index] * SLAB).astype(jnp.int32)
        speed = lax.dynamic_slice_in_dim(velocity, first_row, APERTURE, 0)
        mass = lax.dynamic_slice_in_dim(density, first_row, APERTURE, 0)
        speed_sq = time_step_sq * speed * speed
        log_padded = jnp.pad(jnp.log(mass), 4)
        slopes = [derivative(log_padded, direction) for direction in range(3)]
        fields = [forward_old[shot_index], forward_now[shot_index]]
        samples = []
        for step_index in range(STEPS):
            advanced = advance(jnp.pad(fields[-1], 4), fields[-2], speed_sq, slopes)
            flattened = advanced.reshape(-1).at[source_cell[shot_index]].add(wavelet[shot_index, step_index])
            samples.append(flattened[receiver_cells[shot_index]])
            fields.append(flattened.reshape(advanced.shape))
        residual = jnp.stack(samples) - observed[shot_index]
        later_field = adjoint_later[shot_index]
        current = adjoint_now[shot_index]
        summed = jnp.zeros(current.shape, jnp.float32)
        for step_index in reversed(range(STEPS)):
            earlier = advance(jnp.pad(current, 4), later_field, speed_sq, slopes)
            earlier = earlier.reshape(-1).at[receiver_cells[shot_index]].add(residual[step_index]).reshape(current.shape)
            curvature = fields[step_index + 2] - 2.0 * fields[step_index + 1] + fields[step_index]
            summed = summed + earlier * curvature
            later_field = current
            current = earlier
        image_term = (2.0 / speed) * summed
        window = lax.dynamic_slice_in_dim(gradient, first_row, APERTURE, 0)
        gradient = lax.dynamic_update_slice_in_dim(gradient, window + image_term, first_row, 0)
        forward_outs.append(fields[-1])
        adjoint_outs.append(current)
    return gradient, jnp.stack(forward_outs), jnp.stack(adjoint_outs)
```

```python
import functools

import jax
import jax.numpy as jnp
from jax import lax
from jax.experimental import pallas as pl
from jax.experimental.pallas import tpu as pltpu
from jax.sharding import PartitionSpec as P

lap_coeffs = (-205.0 / 72.0, 8.0 / 5.0, -1.0 / 5.0, 8.0 / 315.0, -1.0 / 560.0)
diff_coeffs = (4.0 / 5.0, -1.0 / 5.0, 4.0 / 105.0, -1.0 / 280.0)
time_step_sq = 0.0088

ROWS = 16
CELLS = 32
NZ = 256
F32 = jnp.float32


def pairs_by(move):
    pairs = []
    for shot in range(4):
        for sub in range(32):
            x = 2 * (sub // 16) + shot // 2
            target = move(x, shot % 2, (sub // 4) % 4, sub % 4)
            if target is None:
                continue
            tx, tcore, tz, ty = target
            pairs.append((shot * 32 + sub, ((tx % 2) * 2 + tcore) * 32 + (tx // 2) * 16 + tz * 4 + ty))
    return pairs


def send(value, move):
    return lax.ppermute(value, ("shot", "sub"), pairs_by(move))


def send_x(value, steps):
    return send(value, lambda x, c, z, y: ((x + steps) % 4, c, z, y))


def send_core(value):
    return send(value, lambda x, c, z, y: (x, 1 - c, z, y))


def send_z(value, steps):
    return send(value, lambda x, c, z, y: (x, c, (z + steps) % 4, y))


def send_y(value, steps):
    return send(value, lambda x, c, z, y: (x, c, z, (y + steps) % 4))


def next_rows(x, z, steps):
    group = (x // 2) * 4 + z + steps
    if group < 0 or group > 7:
        return None
    return (2 * (group // 4) + x % 2, group % 4)


def send_group(value, steps):
    def move(x, c, z, y):
        place = next_rows(x, z, steps)
        return None if place is None else (place[0], c, place[1], y)

    return send(value, move)


def send_cells(value, steps):
    return send(value, lambda x, c, z, y: (x, c, z, y + steps) if 0 <= y + steps < 4 else None)


def swap_edges(edges):
    low_rows, high_rows, low_cells, high_cells = edges
    return (
        send_group(high_rows, 1),
        send_group(low_rows, -1),
        send_cells(high_cells, 1),
        send_cells(low_cells, -1),
    )


VMEM = pltpu.VMEM
SMEM = pltpu.SMEM


def block_shape():
    return jax.ShapeDtypeStruct((ROWS, CELLS, NZ), F32)


def edge_shapes():
    rows = jax.ShapeDtypeStruct((4, CELLS, NZ), F32)
    cells = jax.ShapeDtypeStruct((ROWS, 8, NZ), F32)
    return (rows, rows, cells, cells)


def call(body, outs, n_smem, operands, scratch=()):
    specs = [pl.BlockSpec(memory_space=SMEM)] * n_smem
    specs += [pl.BlockSpec(memory_space=VMEM)] * (len(operands) - n_smem)
    return pl.pallas_call(
        body,
        out_shape=outs,
        in_specs=specs,
        out_specs=tuple(pl.BlockSpec(memory_space=VMEM) for _ in outs),
        scratch_shapes=list(scratch),
    )(*operands)


def write_edges(block, edges):
    low_rows, high_rows, low_cells, high_cells = edges
    low_rows[...] = block[0:4]
    high_rows[...] = block[ROWS - 4 : ROWS]
    low_cells[...] = block[:, 0:8, :]
    high_cells[...] = block[:, CELLS - 8 : CELLS, :]


def fill_padded(padded, block, halo):
    below, above, left, right = halo
    padded[0:4, 8 : 8 + CELLS, :] = below[...]
    padded[4 : 4 + ROWS, 8 : 8 + CELLS, :] = block[...]
    padded[4 + ROWS : 8 + ROWS, 8 : 8 + CELLS, :] = above[...]
    padded[4 : 4 + ROWS, 0:8, :] = left[...]
    padded[4 : 4 + ROWS, 8 + CELLS : 16 + CELLS, :] = right[...]


PADDED = pltpu.VMEM((ROWS + 8, CELLS + 16, NZ), F32)


def z_shifted(value, lane, reach):
    ahead = jnp.where(lane < NZ - reach, pltpu.roll(value, NZ - reach, 1), 0.0)
    behind = jnp.where(lane >= reach, pltpu.roll(value, reach, 1), 0.0)
    return ahead, behind


def views(padded, row, direction, reach, lane):
    if direction == 0:
        return (
            padded[row + 4 + reach, 8 : 8 + CELLS, :],
            padded[row + 4 - reach, 8 : 8 + CELLS, :],
        )
    if direction == 1:
        return (
            padded[row + 4, 8 + reach : 8 + CELLS + reach, :],
            padded[row + 4, 8 - reach : 8 + CELLS - reach, :],
        )
    return z_shifted(padded[row + 4, 8 : 8 + CELLS, :], lane, reach)


def operator_row(padded, row, slopes, lane):
    center = padded[row + 4, 8 : 8 + CELLS, :]
    result = (3.0 * lap_coeffs[0]) * center
    for direction in range(3):
        derived = None
        for reach in range(1, 5):
            ahead, behind = views(padded, row, direction, reach, lane)
            result = result + lap_coeffs[reach] * (ahead + behind)
            part = diff_coeffs[reach - 1] * (ahead - behind)
            derived = part if derived is None else derived + part
        result = result - slopes[direction][row] * derived
    return center, result


def lanes():
    return lax.broadcasted_iota(jnp.int32, (CELLS, NZ), 1)


def assemble_body(slots, *refs, fields):
    pieces = refs[:4]
    blocks = refs[4 : 4 + fields]
    edges = refs[4 + fields :]
    for turn in range(4):
        slot = slots[turn]
        for index in range(fields):
            blocks[index][pl.ds(slot * 4, 4)] = pieces[turn][index]
    write_edges(blocks[0], edges)


def assemble(pieces, slots, fields):
    outs = (block_shape(),) * fields + edge_shapes()
    result = call(
        functools.partial(assemble_body, fields=fields), outs, 1, (slots, *pieces)
    )
    return result[:fields], result[fields:]


def model_body(slots, p0, p1, p2, p3, log_mass, h0, h1, h2, h3, speed_sq, twice, s0, s1, s2, padded):
    fill_padded(padded, log_mass, (h0, h1, h2, h3))
    for turn, piece in enumerate((p0, p1, p2, p3)):
        slot = slots[turn]
        speed = piece[0]
        speed_sq[pl.ds(slot * 4, 4)] = time_step_sq * speed * speed
        twice[pl.ds(slot * 4, 4)] = 2.0 / speed
    lane = lanes()

    def step(row, carry):
        for direction, out in enumerate((s0, s1, s2)):
            derived = None
            for reach in range(1, 5):
                ahead, behind = views(padded, row, direction, reach, lane)
                part = diff_coeffs[reach - 1] * (ahead - behind)
                derived = part if derived is None else derived + part
            out[row] = derived
        return carry

    lax.fori_loop(0, ROWS, step, 0)


def forward_body(place, amount, now, h0, h1, h2, h3, old, speed_sq, s0, s1, s2, new, e0, e1, e2, e3, padded, *, index):
    fill_padded(padded, now, (h0, h1, h2, h3))
    lane = lanes()

    def step(row, carry):
        center, result = operator_row(padded, row, (s0, s1, s2), lane)
        new[row] = 2.0 * center - old[row] + speed_sq[row] * result
        return carry

    lax.fori_loop(0, ROWS, step, 0)

    @pl.when(place[0] > 0)
    def _():
        cell = lax.broadcasted_iota(jnp.int32, (CELLS, NZ), 0)
        hit = (cell == place[2]) & (lane == place[3])
        new[place[1]] = new[place[1]] + jnp.where(hit, amount[index], 0.0)

    write_edges(new, (e0, e1, e2, e3))


def adjoint_body(now, h0, h1, h2, h3, later, speed_sq, s0, s1, s2, hits, seen, u_next, u_here, u_before, *rest, first, last):
    rest = list(rest)
    sums = None if first else rest.pop(0)
    twice = rest.pop(0) if last else None
    new, summed = rest.pop(0), rest.pop(0)
    padded = rest.pop()
    fill_padded(padded, now, (h0, h1, h2, h3))
    lane = lanes()

    def step(row, carry):
        center, result = operator_row(padded, row, (s0, s1, s2), lane)
        ahead = u_next[row]
        value = 2.0 * center - later[row] + speed_sq[row] * result
        value = value + (hits[row] * ahead - seen[row])
        new[row] = value
        total = value * (ahead - 2.0 * u_here[row] + u_before[row])
        if sums is not None:
            total = sums[row] + total
        if twice is not None:
            total = twice[row] * total
        summed[row] = total
        return carry

    lax.fori_loop(0, ROWS, step, 0)
    if rest:
        write_edges(new, rest)


def spread_body(chunks, *refs, fields):
    pieces = refs[:4]
    outs = refs[4:]
    for turn in range(4):
        first = pl.multiple_of(chunks[turn] * CELLS, CELLS)
        for index in range(fields):
            outs[index][:, pl.ds(first, CELLS), :] = pieces[turn][index]


def spread(pieces, chunks, fields):
    outs = (jax.ShapeDtypeStruct((4, 4 * CELLS, NZ), F32),) * fields
    return call(functools.partial(spread_body, fields=fields), outs, 1, (chunks, *pieces))


def to_blocks(slabs, y):
    pieces = []
    for turn in range(4):
        first = ((y + turn) % 4) * CELLS
        cut = jnp.stack([lax.dynamic_slice_in_dim(slab, first, CELLS, 1) for slab in slabs])
        pieces.append(send_y(cut, turn) if turn else cut)
    return pieces


def to_slabs(blocks, y, shifts):
    pieces = []
    for turn in range(4):
        cut = jnp.stack(
            [
                lax.dynamic_slice_in_dim(block, ((y + turn - shift) % 4) * 4, 4, 0)
                for block, shift in zip(blocks, shifts)
            ]
        )
        pieces.append(send_y(cut, turn) if turn else cut)
    return pieces


def on_device(
    velocity,
    density,
    aperture_start,
    source_cell,
    receiver_cells,
    wavelet,
    observed,
    forward_old,
    forward_now,
    adjoint_later,
    adjoint_now,
):
    shot = lax.axis_index("shot")
    sub = lax.axis_index("sub")
    core = shot % 2
    x_hi = sub // 16
    x = 2 * x_hi + shot // 2
    z = (sub // 4) % 4
    y = sub % 4
    start = aperture_start[0]
    partner_start = send_core(aperture_start)[0]

    def wanted(first_slab):
        upper = first_slab // 4 + (y < first_slab % 4).astype(jnp.int32)
        block = jnp.clip(x_hi + (upper - z + 3) // 4, 0, 7)
        position = 2 * (block % 2) + block // 4
        return (block // 2) % 2, (position - x) % 4, upper % 4

    own_core, own_step, turn_by = wanted(start)
    pair_core, pair_step, _ = wanted(partner_start)
    low = turn_by % 2 == 1
    high = turn_by // 2 == 1
    high_back = ((turn_by + 1) // 2) % 2 == 1
    high_other = jnp.where(low, high_back, high)
    turns = jnp.arange(4, dtype=jnp.int32)
    plain_slots = (y - turns) % 4
    model_slots = (y - turns - start % 4) % 4

    def gathered(slab):
        from_below = send_x(slab, 1)
        from_above = send_x(slab, -1)
        far = jnp.concatenate([send_x(from_below[0:2], 1), send_x(from_above[2:4], -1)])

        def pick(step):
            return jnp.where(
                step < 2, jnp.where(step == 0, slab, from_above), jnp.where(step == 2, far, from_below)
            )

        other = send_core(pick(pair_step))
        return jnp.where(own_core == core, pick(own_step), other)

    def turned(slab, direction, high_bit):
        slab = jnp.where(low, send_z(slab, direction), slab)
        return jnp.where(high_bit, send_z(slab, 2), slab)

    log_slab = turned(gathered(jnp.log(density)), -1, high)
    speed_slab = turned(gathered(velocity), 1, high_other)

    (u_now, u_old), u_edges = assemble(to_blocks([forward_now[0], forward_old[0]], y), plain_slots, 2)
    (a_now, a_later), a_edges = assemble(to_blocks([adjoint_now[0], adjoint_later[0]], y), plain_slots, 2)
    u_halo = swap_edges(u_edges)
    a_halo = swap_edges(a_edges)

    group = sub // 4

    def local_place(cells):
        rows = cells // (4 * CELLS * NZ) - group * ROWS
        columns = (cells // NZ) % (4 * CELLS) - y * CELLS
        inside = (rows >= 0) & (rows < ROWS) & (columns >= 0) & (columns < CELLS)
        return inside, rows, columns, cells % NZ

    inside, rows, columns, depth = local_place(receiver_cells[0])
    line = jnp.where(inside, rows * CELLS + columns, -1)
    on_line = (jnp.arange(ROWS * CELLS)[:, None] == line[None, :]).astype(F32)
    weights = jnp.concatenate([jnp.ones_like(observed[0, :1]), observed[0]])
    at_depth = jnp.where(depth[None, :, None] == jnp.arange(NZ)[None, None, :], weights[:, :, None], 0.0)
    maps = jnp.einsum("lr,krz->klz", on_line, at_depth, precision=lax.Precision.HIGHEST)
    maps = maps.reshape(5, ROWS, CELLS, NZ)

    s_inside, s_row, s_column, s_depth = local_place(source_cell[0])
    place = jnp.stack(
        [
            s_inside.astype(jnp.int32),
            jnp.clip(s_row, 0, ROWS - 1),
            s_column,
            s_depth,
        ]
    )
    amount = wavelet[0]

    (log_block,), log_edges = assemble(to_blocks([log_slab], y), model_slots, 1)
    log_halo = swap_edges(log_edges)
    speed_pieces = to_blocks([speed_slab], y)
    speed_sq, twice, s0, s1, s2 = call(
        model_body,
        (block_shape(),) * 5,
        1,
        (model_slots, *speed_pieces, log_block, *log_halo),
        (PADDED,),
    )
    model = (speed_sq, s0, s1, s2)

    fields = [u_old, u_now]
    halo = u_halo
    for index in range(4):
        new, *edges = call(
            functools.partial(forward_body, index=index),
            (block_shape(), *edge_shapes()),
            2,
            (place, amount, fields[-1], *halo, fields[-2], *model),
            (PADDED,),
        )
        fields.append(new)
        if index < 3:
            halo = swap_edges(edges)

    current, later = a_now, a_later
    halo = a_halo
    summed = None
    for index in reversed(range(4)):
        first, last = index == 3, index == 0
        operands = (current, *halo, later, *model, maps[0], maps[index + 1])
        operands += (fields[index + 2], fields[index + 1], fields[index])
        if not first:
            operands += (summed,)
        if last:
            operands += (twice,)
        outs = (block_shape(), block_shape()) + (() if last else edge_shapes())
        new, summed, *edges = call(
            functools.partial(adjoint_body, first=first, last=last), outs, 0, operands, (PADDED,)
        )
        later, current = current, new
        if not last:
            halo = swap_edges(edges)

    oy = start % 4
    (forward_last,) = spread(to_slabs([fields[-1]], y, (0,)), plain_slots, 1)
    adjoint_first, image = spread(to_slabs([current, summed], y, (0, oy)), plain_slots, 2)

    def both(first_half, second_half):
        return jnp.concatenate([first_half, second_half])

    image = jnp.where(low, both(send_z(image[0:2], 1), send_z(image[2:4], -1)), image)
    arrived = send_z(image, 2)
    image = both(
        jnp.where(high, arrived[0:2], image[0:2]),
        jnp.where(high_other, arrived[2:4], image[2:4]),
    )
    other = send_core(image)

    def share(step):
        mine = jnp.where((own_core == core) & (own_step == step), image, 0.0)
        return mine + jnp.where((pair_core == core) & (pair_step == step), other, 0.0)

    far = share(2)
    passing_up = send_x(far[0:2], 1)
    passing_down = send_x(far[2:4], -1)
    up = share(1)
    down = share(3)
    up = send_x(both(up[0:2] + passing_up, up[2:4]), 1)
    down = send_x(both(down[0:2], down[2:4] + passing_down), -1)
    gradient = share(0) + up + down
    return (gradient, forward_last[None], adjoint_first[None])


def solution(mesh):
    placed = (
        P(("shot", "sub"), None, None),
        P(("shot", "sub"), None, None),
        P("shot"),
        P("shot"),
        P("shot", None),
        P("shot", None),
        P("shot", None, None),
        P("shot", "sub", None, None),
        P("shot", "sub", None, None),
        P("shot", "sub", None, None),
        P("shot", "sub", None, None),
    )
    return jax.shard_map(
        on_device,
        mesh=mesh,
        in_specs=placed,
        out_specs=(
            P(("shot", "sub"), None, None),
            P("shot", "sub", None, None),
            P("shot", "sub", None, None),
        ),
        check_vma=False,
    )
```

```python
import functools

import jax
import jax.numpy as jnp
from jax import lax
from jax.experimental import pallas as pl
from jax.experimental.pallas import tpu as pltpu
from jax.sharding import PartitionSpec as P

lap_coeffs = (-205.0 / 72.0, 8.0 / 5.0, -1.0 / 5.0, 8.0 / 315.0, -1.0 / 560.0)
diff_coeffs = (4.0 / 5.0, -1.0 / 5.0, 4.0 / 105.0, -1.0 / 280.0)
time_step_sq = 0.0088

ROWS = 16
CELLS = 32
SPAN = CELLS + 16
NY = 128
NZ = 256
F32 = jnp.float32


def pairs_by(move):
    pairs = []
    for shot in range(4):
        for sub in range(32):
            x = 2 * (sub // 16) + shot // 2
            target = move(x, shot % 2, (sub // 4) % 4, sub % 4)
            if target is None:
                continue
            tx, tcore, tz, ty = target
            pairs.append((shot * 32 + sub, ((tx % 2) * 2 + tcore) * 32 + (tx // 2) * 16 + tz * 4 + ty))
    return pairs


def send(value, move):
    return lax.ppermute(value, ("shot", "sub"), pairs_by(move))


def send_x(value, steps):
    return send(value, lambda x, c, z, y: ((x + steps) % 4, c, z, y))


def send_core(value):
    return send(value, lambda x, c, z, y: (x, 1 - c, z, y))


def send_z(value, steps):
    return send(value, lambda x, c, z, y: (x, c, (z + steps) % 4, y))


def send_y(value, steps):
    return send(value, lambda x, c, z, y: (x, c, z, (y + steps) % 4))


def next_rows(x, z, steps):
    group = (x // 2) * 4 + z + steps
    if group < 0 or group > 7:
        return None
    return (2 * (group // 4) + x % 2, group % 4)


def send_group(value, steps):
    def move(x, c, z, y):
        place = next_rows(x, z, steps)
        return None if place is None else (place[0], c, place[1], y)

    return send(value, move)


def send_cells(value, steps):
    return send(value, lambda x, c, z, y: (x, c, z, y + steps) if 0 <= y + steps < 4 else None)


def shape(*sizes):
    return jax.ShapeDtypeStruct(sizes, F32)


def region(rows, cells):
    return shape(rows, 2, cells, 128)


BLOCK = region(ROWS, CELLS)
NEAR = region(ROWS + 8, SPAN)
WIDE = region(ROWS + 16, SPAN)


def call(body, outs, n_smem, operands, scratch=()):
    specs = [pl.BlockSpec(memory_space=pltpu.SMEM)] * n_smem
    specs += [pl.BlockSpec(memory_space=pltpu.VMEM)] * (len(operands) - n_smem)
    return pl.pallas_call(
        body,
        out_shape=tuple(outs),
        in_specs=specs,
        out_specs=tuple(pl.BlockSpec(memory_space=pltpu.VMEM) for _ in outs),
        scratch_shapes=[pltpu.VMEM(s.shape, s.dtype) for s in scratch],
    )(*operands)


def lanes():
    return lax.broadcasted_iota(jnp.int32, (8, 128), 1)


class Stencil:
    def __init__(self, source, row, cell, lane):
        self.source, self.row, self.cell, self.lane = source, row, cell, lane
        self.center = [self.load(0, 0, half) for half in (0, 1)]
        low, high = self.center
        self.deep = []
        for reach in range(1, 5):
            ahead = [pltpu.roll(v, 128 - reach, 1) for v in (low, high)]
            behind = [pltpu.roll(v, reach, 1) for v in (low, high)]
            front = lane < 128 - reach
            back = lane >= reach
            self.deep.append(
                (
                    (jnp.where(front, ahead[0], ahead[1]), jnp.where(front, ahead[1], 0.0)),
                    (jnp.where(back, behind[0], 0.0), jnp.where(back, behind[1], behind[0])),
                )
            )

    def load(self, rows, cells, half):
        first = self.cell + cells
        return self.source[self.row + rows, half, first : first + 8, :]

    def both(self, direction, reach, half):
        if direction == 0:
            return self.load(reach, 0, half), self.load(-reach, 0, half)
        if direction == 1:
            return self.load(0, reach, half), self.load(0, -reach, half)
        ahead, behind = self.deep[reach - 1]
        return ahead[half], behind[half]

    def derivative(self, direction, half):
        total = None
        for reach in range(1, 5):
            ahead, behind = self.both(direction, reach, half)
            part = diff_coeffs[reach - 1] * (ahead - behind)
            total = part if total is None else total + part
        return total

    def advanced(self, half, previous, speed_sq, slopes):
        center = self.center[half]
        lap = (3.0 * lap_coeffs[0]) * center
        derived = [None, None, None]
        for reach in range(1, 5):
            around = None
            for direction in range(3):
                ahead, behind = self.both(direction, reach, half)
                pair = ahead + behind
                around = pair if around is None else around + pair
                part = diff_coeffs[reach - 1] * (ahead - behind)
                derived[direction] = part if reach == 1 else derived[direction] + part
            lap = lap + lap_coeffs[reach] * around
        result = 2.0 * center - previous + speed_sq * lap
        for direction in range(3):
            result = result - slopes[direction] * derived[direction]
        return result


def over_block(visit):
    def step(row, carry):
        for cell in range(0, CELLS, 8):
            visit(row, cell)
        return carry

    lax.fori_loop(0, ROWS, step, 0)


def over_near(visit):
    def side(row, carry):
        for cell in range(8, 8 + CELLS, 8):
            visit(row, cell)
        return carry

    def middle(row, carry):
        for cell in range(4, 12 + CELLS, 8):
            visit(row, cell)
        return carry

    lax.fori_loop(0, 4, side, 0)
    lax.fori_loop(4, 4 + ROWS, middle, 0)
    lax.fori_loop(4 + ROWS, 8 + ROWS, side, 0)


def add_source(place, amount, first, target):
    @pl.when(place[first] > 0)
    def _():
        row, half = place[first + 1], place[first + 2]
        values = target[row, half]
        cell = lax.broadcasted_iota(jnp.int32, values.shape, 0)
        lane = lax.broadcasted_iota(jnp.int32, values.shape, 1)
        hit = (cell == place[first + 3]) & (lane == place[first + 4])
        target[row, half] = values + jnp.where(hit, amount, 0.0)


def near_step(source, old, model, lane, out, extra=None):
    speed_sq, slopes = model[0], model[1:]

    def visit(row, cell):
        stencil = Stencil(source, row + 4, cell, lane)
        cut = slice(cell, cell + 8)
        for half in (0, 1):
            value = stencil.advanced(
                half,
                old[row, half, cut, :],
                speed_sq[row, half, cut, :],
                [s[row, half, cut, :] for s in slopes],
            )
            if extra is not None:
                value = value + extra(row, half, cut)
            out[row, half, cut, :] = value

    over_near(visit)


def block_step(source, old, model, lane, finish):
    speed_sq, slopes = model[0], model[1:]

    def visit(row, cell):
        stencil = Stencil(source, row + 4, cell + 8, lane)
        near = slice(cell + 8, cell + 16)
        for half in (0, 1):
            value = stencil.advanced(
                half,
                old(row, half, slice(cell, cell + 8)),
                speed_sq[row + 4, half, near, :],
                [s[row + 4, half, near, :] for s in slopes],
            )
            finish(row, half, slice(cell, cell + 8), value)

    over_block(visit)


def of_block(ref):
    return lambda row, half, cut: ref[row, half, cut, :]


def of_near(ref):
    return lambda row, half, cut: ref[row + 4, half, cut.start + 8 : cut.stop + 8, :]


def of_wide(ref):
    return lambda row, half, cut: ref[row + 8, half, cut.start + 8 : cut.stop + 8, :]


def injected(maps, index, field):
    def near(row, half, cut):
        hits = maps[row, half, cut, 0:128]
        seen = maps[row, half, cut, 128 * index : 128 * index + 128]
        return hits * field[row, half, cut, :] - seen

    return near


def fill_wide(wide, block, below, above, left, right):
    wide[0:8, :, 8 : 8 + CELLS, :] = below[...]
    wide[8 : 8 + ROWS, :, 8 : 8 + CELLS, :] = block[...]
    wide[8 + ROWS : 16 + ROWS, :, 8 : 8 + CELLS, :] = above[...]
    wide[:, :, 0:8, :] = left[...]
    wide[:, :, 8 + CELLS : SPAN, :] = right[...]


def cut_body(chunks, *refs, margins):
    count = len(margins)
    slabs, pieces = refs[:count], refs[count:]
    for turn in range(4):
        chunk = chunks[turn]
        first = pl.multiple_of(chunk * CELLS, CELLS)
        before = pl.multiple_of(jnp.maximum(first - 8, 0), 8)
        after = pl.multiple_of(jnp.minimum(first + CELLS, NY - 8), 8)
        at = 0
        for slab, margin in zip(slabs, margins):
            if margin:
                pieces[turn][:, at : at + 8, :] = jnp.where(chunk > 0, slab[:, pl.ds(before, 8), :], 0.0)
                at += 8
            pieces[turn][:, at : at + CELLS, :] = slab[:, pl.ds(first, CELLS), :]
            at += CELLS
            if margin:
                pieces[turn][:, at : at + 8, :] = jnp.where(chunk < 3, slab[:, pl.ds(after, 8), :], 0.0)
                at += 8


def to_blocks(slabs, margins, chunks):
    width = sum(SPAN if margin else CELLS for margin in margins)
    pieces = call(functools.partial(cut_body, margins=margins), [shape(4, width, NZ)] * 4, 1, (chunks, *slabs))
    return [pieces[0]] + [send_y(pieces[turn], turn) for turn in (1, 2, 3)]


def place_pieces(slots, pieces, outs):
    for turn in range(4):
        slot = pl.multiple_of(slots[turn] * 4, 4)
        at = 0
        for out in outs:
            width = out.shape[2]
            for half in (0, 1):
                out[pl.ds(slot, 4), half] = pieces[turn][:, at : at + width, 128 * half : 128 * half + 128]
            at += width


def gather_body(slots, *refs, depths):
    pieces, outs = refs[:4], refs[4:]
    low, high = outs[-2:]
    place_pieces(slots, pieces, outs[:-2])
    at = 0
    for out, depth in zip(outs, depths):
        if depth:
            low[at : at + depth] = out[0:depth]
            high[at : at + depth] = out[ROWS - depth : ROWS]
            at += depth


def gather_blocks(pieces, slots, depths):
    outs = [region(ROWS, SPAN if depth else CELLS) for depth in depths]
    outs += [region(sum(depths), SPAN)] * 2
    *blocks, low, high = call(functools.partial(gather_body, depths=depths), outs, 1, (slots, *pieces))
    return blocks, send_group(high, 1), send_group(low, -1)


def stack_rows(out, below, middle, above, at, depth):
    out[0:depth] = below[at : at + depth]
    out[depth : depth + ROWS] = middle[...]
    out[depth + ROWS : 2 * depth + ROWS] = above[at : at + depth]


def fields_body(now, old, adjoint, below, above, wide, old_near, adjoint_near):
    stack_rows(wide, below, now, above, 0, 8)
    stack_rows(old_near, below, old, above, 8, 4)
    stack_rows(adjoint_near, below, adjoint, above, 12, 4)


def model_body(log_mass, speed, below, above, speed_sq, s0, s1, s2, twice, wide, speed_near):
    stack_rows(wide, below, log_mass, above, 0, 8)
    stack_rows(speed_near, below, speed, above, 8, 4)
    twice[...] = 2.0 / speed[:, :, 8 : 8 + CELLS, :]
    lane = lanes()

    def visit(row, cell):
        stencil = Stencil(wide, row + 4, cell, lane)
        cut = slice(cell, cell + 8)
        for half in (0, 1):
            value = speed_near[row, half, cut, :]
            scale = time_step_sq * value * value
            speed_sq[row, half, cut, :] = scale
            for direction, out in enumerate((s0, s1, s2)):
                out[row, half, cut, :] = scale * stencil.derivative(direction, half)

    over_near(visit)


def forward_body(place, amount, wide, old, speed_sq, s0, s1, s2, near, new, low, high):
    model = (speed_sq, s0, s1, s2)
    lane = lanes()
    near_step(wide, old, model, lane, near)
    add_source(place, amount[0], 0, near)

    def finish(row, half, cut, value):
        new[row, half, cut, :] = value

    block_step(near, of_wide(wide), model, lane, finish)
    add_source(place, amount[1], 5, new)
    low[...] = new[0:8]
    high[...] = new[8:ROWS]


def write_pieces(slots, block, pieces, at):
    for turn in range(4):
        slot = pl.multiple_of(slots[turn] * 4, 4)
        for half in (0, 1):
            pieces[turn][:, at : at + CELLS, 128 * half : 128 * half + 128] = block[pl.ds(slot, 4), half]


def turn_body(
    place, amount, slots, block, below, above, left, right, old, speed_sq, s0, s1, s2,
    adjoint, later, maps, near, new, adjoint_new, summed, low, high, p0, p1, p2, p3, wide,
):
    model = (speed_sq, s0, s1, s2)
    lane = lanes()
    fill_wide(wide, block, below, above, left, right)
    near_step(wide, old, model, lane, near)
    add_source(place, amount[2], 0, near)

    def finish(row, half, cut, value):
        new[row, half, cut, :] = value

    block_step(near, of_block(block), model, lane, finish)
    add_source(place, amount[3], 5, new)

    def finish_adjoint(row, half, cut, value):
        hits = of_near(maps)(row, half, cut)
        ahead = new[row, half, cut, :]
        value = value + (hits[:, 0:128] * ahead - hits[:, 4 * 128 : 5 * 128])
        adjoint_new[row, half, cut, :] = value
        summed[row, half, cut, :] = value * (
            ahead - 2.0 * of_near(near)(row, half, cut) + block[row, half, cut, :]
        )

    block_step(adjoint, of_block(later), model, lane, finish_adjoint)
    low[...] = adjoint_new[0:8]
    high[...] = adjoint_new[8:ROWS]
    write_pieces(slots, new, (p0, p1, p2, p3), 0)


def adjoint_body(
    block, below, above, left, right, old, speed_sq, s0, s1, s2, maps, u3, u2, u1, u0, sums,
    near, new, summed, low, high, low_cells, high_cells, wide,
):
    model = (speed_sq, s0, s1, s2)
    lane = lanes()
    fill_wide(wide, block, below, above, left, right)
    near_step(wide, old, model, lane, near, injected(maps, 3, u3))

    def finish(row, half, cut, value):
        hits = of_near(maps)(row, half, cut)
        third = of_near(u3)(row, half, cut)
        second = u2[row, half, cut, :]
        first = of_near(u1)(row, half, cut)
        zeroth = of_wide(u0)(row, half, cut)
        value = value + (hits[:, 0:128] * second - hits[:, 2 * 128 : 3 * 128])
        new[row, half, cut, :] = value
        total = sums[row, half, cut, :]
        total = total + of_near(near)(row, half, cut) * (third - 2.0 * second + first)
        summed[row, half, cut, :] = total + value * (second - 2.0 * first + zeroth)

    block_step(near, of_block(block), model, lane, finish)
    low[...] = new[0:4]
    high[...] = new[ROWS - 4 : ROWS]
    low_cells[...] = new[:, :, 0:8, :]
    high_cells[...] = new[:, :, CELLS - 8 : CELLS, :]


def last_body(
    slots, model_slots, block, below, above, left, right, old, speed_sq, s0, s1, s2, maps,
    u1, u0, u_before, sums, twice, p0, p1, p2, p3, q0, q1, q2, q3, near, new, image,
):
    near[0:4, :, 8 : 8 + CELLS, :] = below[...]
    near[4 : 4 + ROWS, :, 8 : 8 + CELLS, :] = block[...]
    near[4 + ROWS : 8 + ROWS, :, 8 : 8 + CELLS, :] = above[...]
    near[4 : 4 + ROWS, :, 0:8, :] = left[...]
    near[4 : 4 + ROWS, :, 8 + CELLS : SPAN, :] = right[...]
    lane = lanes()

    def finish(row, half, cut, value):
        hits = of_near(maps)(row, half, cut)
        first = of_near(u1)(row, half, cut)
        value = value + (hits[:, 0:128] * first - hits[:, 128:256])
        new[row, half, cut, :] = value
        curvature = first - 2.0 * of_wide(u0)(row, half, cut) + of_near(u_before)(row, half, cut)
        image[row, half, cut, :] = twice[row, half, cut, :] * (sums[row, half, cut, :] + value * curvature)

    block_step(near, of_near(old), (speed_sq, s0, s1, s2), lane, finish)
    write_pieces(model_slots, image, (q0, q1, q2, q3), 0)
    write_pieces(slots, new, (p0, p1, p2, p3), 0)


def rim_body(block, below, above, low, high):
    for out, cut in ((low, slice(0, 8)), (high, slice(CELLS - 8, CELLS))):
        out[0:8] = below[:, :, cut, :]
        out[8 : 8 + ROWS] = block[:, :, cut, :]
        out[8 + ROWS : 16 + ROWS] = above[:, :, cut, :]


def wide_halo(block, low, high):
    below, above = send_group(high, 1), send_group(low, -1)
    low_cells, high_cells = call(rim_body, [region(ROWS + 16, 8)] * 2, 0, (block, below, above))
    return below, above, send_cells(high_cells, 1), send_cells(low_cells, -1)


def spread_body(chunks, p0, p1, p2, p3, out):
    for turn, piece in enumerate((p0, p1, p2, p3)):
        first = pl.multiple_of(chunks[turn] * CELLS, CELLS)
        out[:, pl.ds(first, CELLS), :] = piece[...]


def to_slab(pieces, chunks):
    pieces = [pieces[0]] + [send_y(pieces[turn], turn) for turn in (1, 2, 3)]
    return call(spread_body, [shape(4, NY, NZ)], 1, (chunks, *pieces))[0]


def on_device(
    velocity,
    density,
    aperture_start,
    source_cell,
    receiver_cells,
    wavelet,
    observed,
    forward_old,
    forward_now,
    adjoint_later,
    adjoint_now,
):
    shot = lax.axis_index("shot")
    sub = lax.axis_index("sub")
    core = shot % 2
    x_hi = sub // 16
    x = 2 * x_hi + shot // 2
    z = (sub // 4) % 4
    y = sub % 4
    group = sub // 4
    start = aperture_start[0]
    partner_start = send_core(aperture_start)[0]

    def wanted(first_slab):
        upper = first_slab // 4 + (y < first_slab % 4).astype(jnp.int32)
        block = jnp.clip(x_hi + (upper - z + 3) // 4, 0, 7)
        position = 2 * (block % 2) + block // 4
        return (block // 2) % 2, (position - x) % 4, upper % 4

    own_core, own_step, turn_by = wanted(start)
    pair_core, pair_step, _ = wanted(partner_start)
    low = turn_by % 2 == 1
    high = turn_by // 2 == 1
    high_back = ((turn_by + 1) // 2) % 2 == 1
    high_other = jnp.where(low, high_back, high)
    turns = jnp.arange(4, dtype=jnp.int32)
    chunks_out = (y + turns) % 4
    chunks_in = (y - turns) % 4
    slots_in = (y - turns - start % 4) % 4
    slots_out = (y + turns - start % 4) % 4

    def gathered(slab):
        from_below = send_x(slab, 1)
        from_above = send_x(slab, -1)
        far = jnp.concatenate([send_x(from_below[0:2], 1), send_x(from_above[2:4], -1)])

        def pick(step):
            return jnp.where(
                step < 2, jnp.where(step == 0, slab, from_above), jnp.where(step == 2, far, from_below)
            )

        other = send_core(pick(pair_step))
        return jnp.where(own_core == core, pick(own_step), other)

    def turned(slab, direction, high_bit):
        slab = jnp.where(low, send_z(slab, direction), slab)
        return jnp.where(high_bit, send_z(slab, 2), slab)

    log_slab = turned(gathered(jnp.log(density)), -1, high)
    speed_slab = turned(gathered(velocity), 1, high_other)

    pieces = to_blocks(
        [forward_now[0], forward_old[0], adjoint_now[0], adjoint_later[0]],
        (True, True, True, False),
        chunks_out,
    )
    (now, old, adjoint, a_later), below, above = gather_blocks(pieces, chunks_in, (8, 4, 4, 0))
    u_wide, old_near, a_near = call(
        fields_body, [WIDE, NEAR, NEAR], 0, (now, old, adjoint, below, above)
    )

    def local_place(cells, rows_more, cells_more):
        rows = cells // (NY * NZ) - group * ROWS + rows_more
        columns = (cells // NZ) % NY - y * CELLS + cells_more
        inside = (rows >= 0) & (rows < ROWS + 2 * rows_more)
        inside = inside & (columns >= 0) & (columns < CELLS + 2 * cells_more)
        return inside, rows, (cells // 128) % 2, columns, cells % 128

    inside, rows, half, columns, lane = local_place(receiver_cells[0], 4, 8)
    line = jnp.where(inside, (rows * 2 + half) * SPAN + columns, -1)
    lines = (ROWS + 8) * 2 * SPAN
    on_line = (jnp.arange(lines, dtype=jnp.int32)[:, None] == line[None, :]).astype(F32)
    weights = jnp.concatenate([jnp.ones_like(observed[0, :1]), observed[0]])
    hit = lane[:, None, None] == jnp.arange(128, dtype=jnp.int32)[None, None, :]
    at_lane = jnp.where(hit, weights.T[:, :, None], 0.0).reshape(-1, 5 * 128)
    maps = jnp.dot(on_line, at_lane, precision=lax.Precision.HIGHEST)
    maps = maps.reshape(ROWS + 8, 2, SPAN, 5 * 128)

    def source_place(rows_more, cells_more):
        inside, rows, half, columns, lane = local_place(source_cell[0], rows_more, cells_more)
        rows = jnp.clip(rows, 0, ROWS + 2 * rows_more - 1)
        return [inside.astype(jnp.int32), rows, half, columns, lane]

    place = jnp.stack(source_place(4, 8) + source_place(0, 0))
    amount = wavelet[0]

    pieces = to_blocks([log_slab, speed_slab], (True, True), chunks_out)
    (log_mass, speed), below, above = gather_blocks(pieces, slots_in, (8, 4))
    *model, twice = call(
        model_body, [NEAR] * 4 + [BLOCK], 0, (log_mass, speed, below, above), (WIDE, NEAR)
    )

    edges = [region(8, CELLS)] * 2
    u1, u2, *sides = call(
        forward_body, [NEAR, BLOCK] + edges, 2, (place, amount, u_wide, old_near, *model)
    )
    halo = wide_halo(u2, *sides)
    u3, _, a3, sums, side_low, side_high, *pieces = call(
        turn_body,
        [NEAR, BLOCK, BLOCK, BLOCK] + edges + [shape(4, CELLS, NZ)] * 4,
        3,
        (place, amount, chunks_out, u2, *halo, u1, *model, a_near, a_later, maps),
        (WIDE,),
    )
    halo = wide_halo(a3, side_low, side_high)
    forward_last = to_slab(pieces, chunks_in)
    a2, a1, sums, side_low, side_high, low_cells, high_cells = call(
        adjoint_body,
        [NEAR, BLOCK, BLOCK] + [region(4, CELLS)] * 2 + [region(ROWS, 8)] * 2,
        0,
        (a3, *halo, a_near, *model, maps, u3, u2, u1, u_wide, sums),
        (WIDE,),
    )
    halo = (
        send_group(side_high, 1),
        send_group(side_low, -1),
        send_cells(high_cells, 1),
        send_cells(low_cells, -1),
    )
    pieces = call(
        last_body,
        [shape(4, CELLS, NZ)] * 8,
        2,
        (chunks_out, slots_out, a1, *halo, a2, *model, maps, u1, u_wide, old_near, sums, twice),
        (NEAR, BLOCK, BLOCK),
    )
    image = to_slab(pieces[4:], chunks_in)
    image, *pieces = lax.optimization_barrier((image, *pieces[:4]))
    adjoint_first = to_slab(pieces, chunks_in)

    def both(first_half, second_half):
        return jnp.concatenate([first_half, second_half])

    image = jnp.where(low, both(send_z(image[0:2], 1), send_z(image[2:4], -1)), image)
    arrived = send_z(image, 2)
    image = both(
        jnp.where(high, arrived[0:2], image[0:2]),
        jnp.where(high_other, arrived[2:4], image[2:4]),
    )
    other = send_core(image)

    def share(step):
        mine = jnp.where((own_core == core) & (own_step == step), image, 0.0)
        return mine + jnp.where((pair_core == core) & (pair_step == step), other, 0.0)

    far = share(2)
    passing_up = send_x(far[0:2], 1)
    passing_down = send_x(far[2:4], -1)
    up = share(1)
    down = share(3)
    up = send_x(both(up[0:2] + passing_up, up[2:4]), 1)
    down = send_x(both(down[0:2], down[2:4] + passing_down), -1)
    gradient = share(0) + up + down
    return (gradient, forward_last[None], adjoint_first[None])


def solution(mesh):
    placed = (
        P(("shot", "sub"), None, None),
        P(("shot", "sub"), None, None),
        P("shot"),
        P("shot"),
        P("shot", None),
        P("shot", None),
        P("shot", None, None),
        P("shot", "sub", None, None),
        P("shot", "sub", None, None),
        P("shot", "sub", None, None),
        P("shot", "sub", None, None),
    )
    return jax.shard_map(
        on_device,
        mesh=mesh,
        in_specs=placed,
        out_specs=(
            P(("shot", "sub"), None, None),
            P("shot", "sub", None, None),
            P("shot", "sub", None, None),
        ),
        check_vma=False,
    )
```

```python
import functools

import jax
import jax.numpy as jnp
from jax import lax
from jax.experimental import pallas as pl
from jax.experimental.pallas import tpu as pltpu
from jax.sharding import PartitionSpec as P

lap_coeffs = (-205.0 / 72.0, 8.0 / 5.0, -1.0 / 5.0, 8.0 / 315.0, -1.0 / 560.0)
diff_coeffs = (4.0 / 5.0, -1.0 / 5.0, 4.0 / 105.0, -1.0 / 280.0)
time_step_sq = 0.0088

ROWS = 16
CELLS = 32
SPAN = CELLS + 16
NY = 128
NZ = 256
F32 = jnp.float32


def pairs_by(move):
    pairs = []
    for shot in range(4):
        for sub in range(32):
            x = 2 * (sub // 16) + shot // 2
            target = move(x, shot % 2, (sub // 4) % 4, sub % 4)
            if target is None:
                continue
            tx, tcore, tz, ty = target
            pairs.append((shot * 32 + sub, ((tx % 2) * 2 + tcore) * 32 + (tx // 2) * 16 + tz * 4 + ty))
    return pairs


def send(value, move):
    return lax.ppermute(value, ("shot", "sub"), pairs_by(move))


def send_x(value, steps):
    return send(value, lambda x, c, z, y: ((x + steps) % 4, c, z, y))


def send_core(value):
    return send(value, lambda x, c, z, y: (x, 1 - c, z, y))


def send_z(value, steps):
    return send(value, lambda x, c, z, y: (x, c, (z + steps) % 4, y))


def send_y(value, steps):
    return send(value, lambda x, c, z, y: (x, c, z, (y + steps) % 4))


def next_rows(x, z, steps):
    group = (x // 2) * 4 + z + steps
    if group < 0 or group > 7:
        return None
    return (2 * (group // 4) + x % 2, group % 4)


def send_group(value, steps):
    def move(x, c, z, y):
        place = next_rows(x, z, steps)
        return None if place is None else (place[0], c, place[1], y)

    return send(value, move)


def send_corner(value, steps, cells):
    def move(x, c, z, y):
        place = next_rows(x, z, steps)
        if place is None or not 0 <= y + cells < 4:
            return None
        return (place[0], c, place[1], y + cells)

    return send(value, move)


def send_cells(value, steps):
    return send(value, lambda x, c, z, y: (x, c, z, y + steps) if 0 <= y + steps < 4 else None)


def shape(*sizes):
    return jax.ShapeDtypeStruct(sizes, F32)


def region(rows, cells):
    return shape(rows, 2, cells, 128)


BLOCK = region(ROWS, CELLS)
NEAR = region(ROWS + 8, SPAN)
WIDE = region(ROWS + 16, SPAN)


def call(body, outs, n_smem, operands, scratch=()):
    specs = [pl.BlockSpec(memory_space=pltpu.SMEM)] * n_smem
    specs += [pl.BlockSpec(memory_space=pltpu.VMEM)] * (len(operands) - n_smem)
    return pl.pallas_call(
        body,
        out_shape=tuple(outs),
        in_specs=specs,
        out_specs=tuple(pl.BlockSpec(memory_space=pltpu.VMEM) for _ in outs),
        scratch_shapes=[pltpu.VMEM(s.shape, s.dtype) for s in scratch],
    )(*operands)


def lanes():
    return lax.broadcasted_iota(jnp.int32, (8, 128), 1)


class Stencil:
    def __init__(self, source, row, cell, lane):
        self.source, self.row, self.cell, self.lane = source, row, cell, lane
        self.center = [self.load(0, 0, half) for half in (0, 1)]
        low, high = self.center
        self.deep = []
        for reach in range(1, 5):
            ahead = [pltpu.roll(v, 128 - reach, 1) for v in (low, high)]
            behind = [pltpu.roll(v, reach, 1) for v in (low, high)]
            front = lane < 128 - reach
            back = lane >= reach
            self.deep.append(
                (
                    (jnp.where(front, ahead[0], ahead[1]), jnp.where(front, ahead[1], 0.0)),
                    (jnp.where(back, behind[0], 0.0), jnp.where(back, behind[1], behind[0])),
                )
            )

    def load(self, rows, cells, half):
        first = self.cell + cells
        return self.source[self.row + rows, half, first : first + 8, :]

    def both(self, direction, reach, half):
        if direction == 0:
            return self.load(reach, 0, half), self.load(-reach, 0, half)
        if direction == 1:
            return self.load(0, reach, half), self.load(0, -reach, half)
        ahead, behind = self.deep[reach - 1]
        return ahead[half], behind[half]

    def derivative(self, direction, half):
        ahead, behind = self.both(direction, 1, half)
        total = ahead - behind
        for reach in range(2, 5):
            ahead, behind = self.both(direction, reach, half)
            total = total + (diff_coeffs[reach - 1] / diff_coeffs[0]) * (ahead - behind)
        return total

    def advanced(self, half, previous, speed_sq, slopes):
        center = self.center[half]
        lap = (3.0 * lap_coeffs[0] / lap_coeffs[1]) * center
        derived = [None, None, None]
        for reach in range(1, 5):
            around = None
            for direction in range(3):
                ahead, behind = self.both(direction, reach, half)
                pair = ahead + behind
                around = pair if around is None else around + pair
                part = ahead - behind
                if reach > 1:
                    part = derived[direction] + (diff_coeffs[reach - 1] / diff_coeffs[0]) * part
                derived[direction] = part
            if reach > 1:
                around = (lap_coeffs[reach] / lap_coeffs[1]) * around
            lap = lap + around
        result = 2.0 * center - previous + speed_sq * lap
        for direction in range(3):
            result = result - slopes[direction] * derived[direction]
        return result


def row_pairs(visit, first, last, cells):
    def step(pair, carry):
        for row in (first + 2 * pair, first + 2 * pair + 1):
            for cell in cells:
                visit(row, cell)
        return carry

    lax.fori_loop(0, (last - first) // 2, step, 0)


def over_block(visit):
    row_pairs(visit, 0, ROWS, range(0, CELLS, 8))


def over_near(visit):
    sides, middle = range(8, 8 + CELLS, 8), range(4, 12 + CELLS, 8)
    row_pairs(visit, 0, 4, sides)
    row_pairs(visit, 4, 4 + ROWS, middle)
    row_pairs(visit, 4 + ROWS, 8 + ROWS, sides)


def add_source(place, amount, first, target):
    @pl.when(place[first] > 0)
    def _():
        row, half = place[first + 1], place[first + 2]
        values = target[row, half]
        cell = lax.broadcasted_iota(jnp.int32, values.shape, 0)
        lane = lax.broadcasted_iota(jnp.int32, values.shape, 1)
        hit = (cell == place[first + 3]) & (lane == place[first + 4])
        target[row, half] = values + jnp.where(hit, amount, 0.0)


def near_step(source, old, model, lane, out, extra=None):
    speed_sq, slopes = model[0], model[1:]

    def visit(row, cell):
        stencil = Stencil(source, row + 4, cell, lane)
        cut = slice(cell, cell + 8)
        for half in (0, 1):
            value = stencil.advanced(
                half,
                old[row, half, cut, :],
                speed_sq[row, half, cut, :],
                [s[row, half, cut, :] for s in slopes],
            )
            if extra is not None:
                value = value + extra(row, half, cut)
            out[row, half, cut, :] = value

    over_near(visit)


def block_step(source, old, model, lane, finish):
    speed_sq, slopes = model[0], model[1:]

    def visit(row, cell):
        stencil = Stencil(source, row + 4, cell + 8, lane)
        near = slice(cell + 8, cell + 16)
        for half in (0, 1):
            value = stencil.advanced(
                half,
                old(row, half, slice(cell, cell + 8)),
                speed_sq[row + 4, half, near, :],
                [s[row + 4, half, near, :] for s in slopes],
            )
            finish(row, half, slice(cell, cell + 8), value)

    over_block(visit)


def of_block(ref):
    return lambda row, half, cut: ref[row, half, cut, :]


def of_near(ref):
    return lambda row, half, cut: ref[row + 4, half, cut.start + 8 : cut.stop + 8, :]


def of_wide(ref):
    return lambda row, half, cut: ref[row + 8, half, cut.start + 8 : cut.stop + 8, :]


def injected(maps, index, field):
    def near(row, half, cut):
        hits = maps[row, half, cut, 0:128]
        seen = maps[row, half, cut, 128 * index : 128 * index + 128]
        return hits * field[row, half, cut, :] - seen

    return near


def fill_wide(wide, block, halo):
    below, above, left, right, c0, c1, c2, c3 = halo
    low, high = slice(0, 8), slice(8 + CELLS, SPAN)
    wide[0:8, :, 8 : 8 + CELLS, :] = below[...]
    wide[8 : 8 + ROWS, :, 8 : 8 + CELLS, :] = block[...]
    wide[8 + ROWS : 16 + ROWS, :, 8 : 8 + CELLS, :] = above[...]
    wide[8 : 8 + ROWS, :, low, :] = left[...]
    wide[8 : 8 + ROWS, :, high, :] = right[...]
    wide[4:8, :, low, :] = c0[...]
    wide[4:8, :, high, :] = c1[...]
    wide[8 + ROWS : 12 + ROWS, :, low, :] = c2[...]
    wide[8 + ROWS : 12 + ROWS, :, high, :] = c3[...]


WIDE_EDGES = [region(8, CELLS)] * 2 + [region(ROWS, 8)] * 2 + [region(4, 8)] * 4


def write_wide_edges(block, edges):
    low, high, low_cells, high_cells, c0, c1, c2, c3 = edges
    front, back = slice(0, 8), slice(CELLS - 8, CELLS)
    low[...] = block[0:8]
    high[...] = block[ROWS - 8 : ROWS]
    low_cells[...] = block[:, :, front, :]
    high_cells[...] = block[:, :, back, :]
    c0[...] = block[0:4, :, front, :]
    c1[...] = block[0:4, :, back, :]
    c2[...] = block[ROWS - 4 : ROWS, :, front, :]
    c3[...] = block[ROWS - 4 : ROWS, :, back, :]


def swap_wide_edges(edges):
    low, high, low_cells, high_cells, c0, c1, c2, c3 = edges
    return (
        send_group(high, 1),
        send_group(low, -1),
        send_cells(high_cells, 1),
        send_cells(low_cells, -1),
        send_corner(c3, 1, 1),
        send_corner(c2, 1, -1),
        send_corner(c1, -1, 1),
        send_corner(c0, -1, -1),
    )


def cut_body(chunks, *refs, margins):
    count = len(margins)
    slabs, pieces = refs[:count], refs[count:]
    for turn in range(4):
        chunk = chunks[turn]
        first = pl.multiple_of(chunk * CELLS, CELLS)
        before = pl.multiple_of(jnp.maximum(first - 8, 0), 8)
        after = pl.multiple_of(jnp.minimum(first + CELLS, NY - 8), 8)
        at = 0
        for slab, margin in zip(slabs, margins):
            if margin:
                pieces[turn][:, at : at + 8, :] = jnp.where(chunk > 0, slab[:, pl.ds(before, 8), :], 0.0)
                at += 8
            pieces[turn][:, at : at + CELLS, :] = slab[:, pl.ds(first, CELLS), :]
            at += CELLS
            if margin:
                pieces[turn][:, at : at + 8, :] = jnp.where(chunk < 3, slab[:, pl.ds(after, 8), :], 0.0)
                at += 8


def to_blocks(slabs, margins, chunks):
    width = sum(SPAN if margin else CELLS for margin in margins)
    pieces = call(functools.partial(cut_body, margins=margins), [shape(4, width, NZ)] * 4, 1, (chunks, *slabs))
    return [pieces[0]] + [send_y(pieces[turn], turn) for turn in (1, 2, 3)]


def place_pieces(slots, pieces, outs):
    for turn in range(4):
        slot = pl.multiple_of(slots[turn] * 4, 4)
        at = 0
        for out in outs:
            width = out.shape[2]
            for half in (0, 1):
                out[pl.ds(slot, 4), half] = pieces[turn][:, at : at + width, 128 * half : 128 * half + 128]
            at += width


def gather_body(slots, *refs, depths):
    pieces, outs = refs[:4], refs[4:]
    low, high = outs[-2:]
    place_pieces(slots, pieces, outs[:-2])
    at = 0
    for out, depth in zip(outs, depths):
        if depth:
            low[at : at + depth] = out[0:depth]
            high[at : at + depth] = out[ROWS - depth : ROWS]
            at += depth


def gather_blocks(pieces, slots, depths):
    outs = [region(ROWS, SPAN if depth else CELLS) for depth in depths]
    outs += [region(sum(depths), SPAN)] * 2
    return call(functools.partial(gather_body, depths=depths), outs, 1, (slots, *pieces))


def stack_rows(out, below, middle, above, at, depth):
    out[0:depth] = below[at : at + depth]
    out[depth : depth + ROWS] = middle[...]
    out[depth + ROWS : 2 * depth + ROWS] = above[at : at + depth]


def fields_body(now, old, adjoint, below, above, wide, old_near, adjoint_near):
    stack_rows(wide, below, now, above, 0, 8)
    stack_rows(old_near, below, old, above, 8, 4)
    stack_rows(adjoint_near, below, adjoint, above, 12, 4)


def model_body(log_mass, speed, below, above, speed_sq, s0, s1, s2, twice, wide, speed_near):
    stack_rows(wide, below, log_mass, above, 0, 8)
    stack_rows(speed_near, below, speed, above, 8, 4)
    twice[...] = 2.0 / speed[:, :, 8 : 8 + CELLS, :]
    lane = lanes()

    def visit(row, cell):
        stencil = Stencil(wide, row + 4, cell, lane)
        cut = slice(cell, cell + 8)
        for half in (0, 1):
            value = speed_near[row, half, cut, :]
            scale = time_step_sq * value * value
            speed_sq[row, half, cut, :] = lap_coeffs[1] * scale
            scale = (diff_coeffs[0] * diff_coeffs[0]) * scale
            for direction, out in enumerate((s0, s1, s2)):
                out[row, half, cut, :] = scale * stencil.derivative(direction, half)

    over_near(visit)


def forward_body(place, amount, wide, old, speed_sq, s0, s1, s2, near, new, *edges):
    model = (speed_sq, s0, s1, s2)
    lane = lanes()
    near_step(wide, old, model, lane, near)
    add_source(place, amount[0], 0, near)

    def finish(row, half, cut, value):
        new[row, half, cut, :] = value

    block_step(near, of_wide(wide), model, lane, finish)
    add_source(place, amount[1], 5, new)
    write_wide_edges(new, edges)


def write_pieces(slots, block, pieces, at):
    for turn in range(4):
        slot = pl.multiple_of(slots[turn] * 4, 4)
        for half in (0, 1):
            pieces[turn][:, at : at + CELLS, 128 * half : 128 * half + 128] = block[pl.ds(slot, 4), half]


def turn_body(place, amount, slots, block, *refs):
    halo, refs = refs[:8], refs[8:]
    old, speed_sq, s0, s1, s2, adjoint, later, maps, near, new, adjoint_new, summed = refs[:12]
    edges, pieces, wide = refs[12:20], refs[20:24], refs[24]
    model = (speed_sq, s0, s1, s2)
    lane = lanes()
    fill_wide(wide, block, halo)
    near_step(wide, old, model, lane, near)
    add_source(place, amount[2], 0, near)

    def finish(row, half, cut, value):
        new[row, half, cut, :] = value

    block_step(near, of_block(block), model, lane, finish)
    add_source(place, amount[3], 5, new)

    def finish_adjoint(row, half, cut, value):
        hits = of_near(maps)(row, half, cut)
        ahead = new[row, half, cut, :]
        value = value + (hits[:, 0:128] * ahead - hits[:, 4 * 128 : 5 * 128])
        adjoint_new[row, half, cut, :] = value
        summed[row, half, cut, :] = value * (
            ahead - 2.0 * of_near(near)(row, half, cut) + block[row, half, cut, :]
        )

    block_step(adjoint, of_block(later), model, lane, finish_adjoint)
    write_wide_edges(adjoint_new, edges)
    write_pieces(slots, new, pieces, 0)


def adjoint_body(block, *refs):
    halo, refs = refs[:8], refs[8:]
    old, speed_sq, s0, s1, s2, maps, u3, u2, u1, u0, sums = refs[:11]
    near, new, summed, low, high, low_cells, high_cells, wide = refs[11:]
    model = (speed_sq, s0, s1, s2)
    lane = lanes()
    fill_wide(wide, block, halo)
    near_step(wide, old, model, lane, near, injected(maps, 3, u3))

    def finish(row, half, cut, value):
        hits = of_near(maps)(row, half, cut)
        third = of_near(u3)(row, half, cut)
        second = u2[row, half, cut, :]
        first = of_near(u1)(row, half, cut)
        zeroth = of_wide(u0)(row, half, cut)
        value = value + (hits[:, 0:128] * second - hits[:, 2 * 128 : 3 * 128])
        new[row, half, cut, :] = value
        total = sums[row, half, cut, :]
        total = total + of_near(near)(row, half, cut) * (third - 2.0 * second + first)
        summed[row, half, cut, :] = total + value * (second - 2.0 * first + zeroth)

    block_step(near, of_block(block), model, lane, finish)
    low[...] = new[0:4]
    high[...] = new[ROWS - 4 : ROWS]
    low_cells[...] = new[:, :, 0:8, :]
    high_cells[...] = new[:, :, CELLS - 8 : CELLS, :]


def last_body(
    slots, model_slots, block, below, above, left, right, old, speed_sq, s0, s1, s2, maps,
    u1, u0, u_before, sums, twice, p0, p1, p2, p3, near, new, image,
):
    near[0:4, :, 8 : 8 + CELLS, :] = below[...]
    near[4 : 4 + ROWS, :, 8 : 8 + CELLS, :] = block[...]
    near[4 + ROWS : 8 + ROWS, :, 8 : 8 + CELLS, :] = above[...]
    near[4 : 4 + ROWS, :, 0:8, :] = left[...]
    near[4 : 4 + ROWS, :, 8 + CELLS : SPAN, :] = right[...]
    lane = lanes()

    def finish(row, half, cut, value):
        hits = of_near(maps)(row, half, cut)
        first = of_near(u1)(row, half, cut)
        value = value + (hits[:, 0:128] * first - hits[:, 128:256])
        new[row, half, cut, :] = value
        curvature = first - 2.0 * of_wide(u0)(row, half, cut) + of_near(u_before)(row, half, cut)
        image[row, half, cut, :] = twice[row, half, cut, :] * (sums[row, half, cut, :] + value * curvature)

    block_step(near, of_near(old), (speed_sq, s0, s1, s2), lane, finish)
    write_pieces(model_slots, image, (p0, p1, p2, p3), 0)
    write_pieces(slots, new, (p0, p1, p2, p3), CELLS)


def spread_body(chunks, p0, p1, p2, p3, *outs):
    for turn, piece in enumerate((p0, p1, p2, p3)):
        first = pl.multiple_of(chunks[turn] * CELLS, CELLS)
        for index, out in enumerate(outs):
            out[:, pl.ds(first, CELLS), :] = piece[:, CELLS * index : CELLS * index + CELLS, :]


def to_slabs(pieces, chunks, count):
    pieces = [pieces[0]] + [send_y(pieces[turn], turn) for turn in (1, 2, 3)]
    return call(spread_body, [shape(4, NY, NZ)] * count, 1, (chunks, *pieces))


def on_device(
    velocity,
    density,
    aperture_start,
    source_cell,
    receiver_cells,
    wavelet,
    observed,
    forward_old,
    forward_now,
    adjoint_later,
    adjoint_now,
):
    shot = lax.axis_index("shot")
    sub = lax.axis_index("sub")
    core = shot % 2
    x_hi = sub // 16
    x = 2 * x_hi + shot // 2
    z = (sub // 4) % 4
    y = sub % 4
    group = sub // 4
    start = aperture_start[0]
    partner_start = send_core(aperture_start)[0]

    def wanted(first_slab):
        upper = first_slab // 4 + (y < first_slab % 4).astype(jnp.int32)
        block = jnp.clip(x_hi + (upper - z + 3) // 4, 0, 7)
        position = 2 * (block % 2) + block // 4
        return (block // 2) % 2, (position - x) % 4, upper % 4

    own_core, own_step, turn_by = wanted(start)
    pair_core, pair_step, _ = wanted(partner_start)
    turns = jnp.arange(4, dtype=jnp.int32)
    chunks_out = (y + turns) % 4
    chunks_in = (y - turns) % 4
    slots_in = (y - turns - start % 4) % 4
    slots_out = (y + turns - start % 4) % 4

    def gathered(slab):
        from_below = send_x(slab, 1)
        from_above = send_x(slab, -1)
        far = jnp.concatenate([send_x(from_below[0:2], 1), send_x(from_above[2:4], -1)])

        def pick(step):
            return jnp.where(
                step < 2, jnp.where(step == 0, slab, from_above), jnp.where(step == 2, far, from_below)
            )

        other = send_core(pick(pair_step))
        return jnp.where(own_core == core, pick(own_step), other)

    def turned(arrays, steps):
        def branch(count):
            return lambda *values: tuple(send_z(value, count) if count else value for value in values)

        return lax.switch(steps, [branch(count) for count in (0, 1, 2, -1)], *arrays)

    log_slab = gathered(jnp.log(density))
    speed_slab = gathered(velocity)

    pieces = to_blocks(
        [forward_now[0], forward_old[0], adjoint_now[0], adjoint_later[0]],
        (True, True, True, False),
        chunks_out,
    )
    now, old, adjoint, a_later, side_low, side_high = gather_blocks(pieces, chunks_in, (8, 4, 4, 0))

    def local_place(cells, rows_more, cells_more):
        rows = cells // (NY * NZ) - group * ROWS + rows_more
        columns = (cells // NZ) % NY - y * CELLS + cells_more
        inside = (rows >= 0) & (rows < ROWS + 2 * rows_more)
        inside = inside & (columns >= 0) & (columns < CELLS + 2 * cells_more)
        return inside, rows, (cells // 128) % 2, columns, cells % 128

    inside, rows, half, columns, lane = local_place(receiver_cells[0], 4, 8)
    line = jnp.where(inside, (rows * 2 + half) * SPAN + columns, -1)
    lines = (ROWS + 8) * 2 * SPAN
    on_line = (jnp.arange(lines, dtype=jnp.int32)[:, None] == line[None, :]).astype(F32)
    weights = jnp.concatenate([jnp.ones_like(observed[0, :1]), observed[0]])
    hit = lane[:, None, None] == jnp.arange(128, dtype=jnp.int32)[None, None, :]
    at_lane = jnp.where(hit, weights.T[:, :, None], 0.0).reshape(-1, 5 * 128)
    maps = jnp.dot(on_line, at_lane, precision=lax.Precision.HIGHEST)
    maps = maps.reshape(ROWS + 8, 2, SPAN, 5 * 128)

    def source_place(rows_more, cells_more):
        inside, rows, half, columns, lane = local_place(source_cell[0], rows_more, cells_more)
        rows = jnp.clip(rows, 0, ROWS + 2 * rows_more - 1)
        return [inside.astype(jnp.int32), rows, half, columns, lane]

    place = jnp.stack(source_place(4, 8) + source_place(0, 0))
    amount = wavelet[0]

    log_slab, speed_slab, maps, side_low, side_high = lax.optimization_barrier(
        (log_slab, speed_slab, maps, side_low, side_high)
    )
    log_slab, speed_slab = turned((log_slab, speed_slab), (4 - turn_by) % 4)
    log_slab, speed_slab, side_low, side_high = lax.optimization_barrier(
        (log_slab, speed_slab, side_low, side_high)
    )
    pieces = to_blocks([log_slab, speed_slab], (True, True), chunks_out)
    below, above = send_group(side_high, 1), send_group(side_low, -1)
    u_wide, old_near, a_near = call(
        fields_body, [WIDE, NEAR, NEAR], 0, (now, old, adjoint, below, above)
    )
    log_mass, speed, side_low, side_high = gather_blocks(pieces, slots_in, (8, 4))
    below, above = send_group(side_high, 1), send_group(side_low, -1)
    *model, twice = call(
        model_body, [NEAR] * 4 + [BLOCK], 0, (log_mass, speed, below, above), (WIDE, NEAR)
    )

    u1, u2, *edges = call(
        forward_body, [NEAR, BLOCK] + WIDE_EDGES, 2, (place, amount, u_wide, old_near, *model)
    )
    halo = swap_wide_edges(edges)
    u3, _, a3, sums, *rest = call(
        turn_body,
        [NEAR, BLOCK, BLOCK, BLOCK] + WIDE_EDGES + [shape(4, CELLS, NZ)] * 4,
        3,
        (place, amount, chunks_out, u2, *halo, u1, *model, a_near, a_later, maps),
        (WIDE,),
    )
    halo = swap_wide_edges(rest[:8])
    (forward_last,) = to_slabs(rest[8:], chunks_in, 1)
    a2, a1, sums, side_low, side_high, low_cells, high_cells = call(
        adjoint_body,
        [NEAR, BLOCK, BLOCK] + [region(4, CELLS)] * 2 + [region(ROWS, 8)] * 2,
        0,
        (a3, *halo, a_near, *model, maps, u3, u2, u1, u_wide, sums),
        (WIDE,),
    )
    halo = (
        send_group(side_high, 1),
        send_group(side_low, -1),
        send_cells(high_cells, 1),
        send_cells(low_cells, -1),
    )
    pieces = call(
        last_body,
        [shape(4, 2 * CELLS, NZ)] * 4,
        2,
        (chunks_out, slots_out, a1, *halo, a2, *model, maps, u1, u_wide, old_near, sums, twice),
        (NEAR, BLOCK, BLOCK),
    )
    image, adjoint_first = to_slabs(pieces, chunks_in, 2)

    def both(first_half, second_half):
        return jnp.concatenate([first_half, second_half])

    (image,) = turned((image,), turn_by)
    other = send_core(image)

    def share(step):
        mine = jnp.where((own_core == core) & (own_step == step), image, 0.0)
        return mine + jnp.where((pair_core == core) & (pair_step == step), other, 0.0)

    far = share(2)
    passing_up = send_x(far[0:2], 1)
    passing_down = send_x(far[2:4], -1)
    up = share(1)
    down = share(3)
    up = send_x(both(up[0:2] + passing_up, up[2:4]), 1)
    down = send_x(both(down[0:2], down[2:4] + passing_down), -1)
    gradient = share(0) + up + down
    return (gradient, forward_last[None], adjoint_first[None])


def solution(mesh):
    placed = (
        P(("shot", "sub"), None, None),
        P(("shot", "sub"), None, None),
        P("shot"),
        P("shot"),
        P("shot", None),
        P("shot", None),
        P("shot", None, None),
        P("shot", "sub", None, None),
        P("shot", "sub", None, None),
        P("shot", "sub", None, None),
        P("shot", "sub", None, None),
    )
    return jax.shard_map(
        on_device,
        mesh=mesh,
        in_specs=placed,
        out_specs=(
            P(("shot", "sub"), None, None),
            P("shot", "sub", None, None),
            P("shot", "sub", None, None),
        ),
        check_vma=False,
    )
```

```python
import functools

import jax
import jax.numpy as jnp
from jax import lax
from jax.experimental import pallas as pl
from jax.experimental.pallas import tpu as pltpu
from jax.sharding import PartitionSpec as P

lap_coeffs = (-205.0 / 72.0, 8.0 / 5.0, -1.0 / 5.0, 8.0 / 315.0, -1.0 / 560.0)
diff_coeffs = (4.0 / 5.0, -1.0 / 5.0, 4.0 / 105.0, -1.0 / 280.0)
time_step_sq = 0.0088

ROWS = 16
CELLS = 32
SPAN = CELLS + 16
NY = 128
NZ = 256
F32 = jnp.float32


def pairs_by(move):
    pairs = []
    for shot in range(4):
        for sub in range(32):
            x = 2 * (sub // 16) + shot // 2
            target = move(x, shot % 2, (sub // 4) % 4, sub % 4)
            if target is None:
                continue
            tx, tcore, tz, ty = target
            pairs.append((shot * 32 + sub, ((tx % 2) * 2 + tcore) * 32 + (tx // 2) * 16 + tz * 4 + ty))
    return pairs


def send(value, move):
    return lax.ppermute(value, ("shot", "sub"), pairs_by(move))


def send_x(value, steps):
    return send(value, lambda x, c, z, y: ((x + steps) % 4, c, z, y))


def send_core(value):
    return send(value, lambda x, c, z, y: (x, 1 - c, z, y))


def send_z(value, steps):
    return send(value, lambda x, c, z, y: (x, c, (z + steps) % 4, y))


def send_y(value, steps):
    return send(value, lambda x, c, z, y: (x, c, z, (y + steps) % 4))


def next_rows(x, z, steps):
    group = (x // 2) * 4 + z + steps
    if group < 0 or group > 7:
        return None
    return (2 * (group // 4) + x % 2, group % 4)


def send_group(value, steps):
    def move(x, c, z, y):
        place = next_rows(x, z, steps)
        return None if place is None else (place[0], c, place[1], y)

    return send(value, move)


def send_cells(value, steps):
    return send(value, lambda x, c, z, y: (x, c, z, y + steps) if 0 <= y + steps < 4 else None)


def shape(*sizes):
    return jax.ShapeDtypeStruct(sizes, F32)


def region(rows, cells):
    return shape(rows, 2, cells, 128)


BLOCK = region(ROWS, CELLS)
NEAR = region(ROWS + 8, SPAN)
WIDE = region(ROWS + 16, SPAN)


def call(body, outs, n_smem, operands, scratch=()):
    specs = [pl.BlockSpec(memory_space=pltpu.SMEM)] * n_smem
    specs += [pl.BlockSpec(memory_space=pltpu.VMEM)] * (len(operands) - n_smem)
    return pl.pallas_call(
        body,
        out_shape=tuple(outs),
        in_specs=specs,
        out_specs=tuple(pl.BlockSpec(memory_space=pltpu.VMEM) for _ in outs),
        scratch_shapes=[pltpu.VMEM(s.shape, s.dtype) for s in scratch],
    )(*operands)


def lanes():
    return lax.broadcasted_iota(jnp.int32, (8, 128), 1)


class Stencil:
    def __init__(self, source, row, cell, lane):
        self.source, self.row, self.cell, self.lane = source, row, cell, lane
        self.center = [self.load(0, 0, half) for half in (0, 1)]
        low, high = self.center
        self.deep = []
        for reach in range(1, 5):
            ahead = [pltpu.roll(v, 128 - reach, 1) for v in (low, high)]
            behind = [pltpu.roll(v, reach, 1) for v in (low, high)]
            front = lane < 128 - reach
            back = lane >= reach
            self.deep.append(
                (
                    (jnp.where(front, ahead[0], ahead[1]), jnp.where(front, ahead[1], 0.0)),
                    (jnp.where(back, behind[0], 0.0), jnp.where(back, behind[1], behind[0])),
                )
            )

    def load(self, rows, cells, half):
        first = self.cell + cells
        return self.source[self.row + rows, half, first : first + 8, :]

    def both(self, direction, reach, half):
        if direction == 0:
            return self.load(reach, 0, half), self.load(-reach, 0, half)
        if direction == 1:
            return self.load(0, reach, half), self.load(0, -reach, half)
        ahead, behind = self.deep[reach - 1]
        return ahead[half], behind[half]

    def derivative(self, direction, half):
        ahead, behind = self.both(direction, 1, half)
        total = ahead - behind
        for reach in range(2, 5):
            ahead, behind = self.both(direction, reach, half)
            total = total + (diff_coeffs[reach - 1] / diff_coeffs[0]) * (ahead - behind)
        return total

    def advanced(self, half, previous, speed_sq, slopes):
        center = self.center[half]
        lap = (3.0 * lap_coeffs[0] / lap_coeffs[1]) * center
        derived = [None, None, None]
        for reach in range(1, 5):
            around = None
            for direction in range(3):
                ahead, behind = self.both(direction, reach, half)
                pair = ahead + behind
                around = pair if around is None else around + pair
                part = ahead - behind
                if reach > 1:
                    part = derived[direction] + (diff_coeffs[reach - 1] / diff_coeffs[0]) * part
                derived[direction] = part
            if reach > 1:
                around = (lap_coeffs[reach] / lap_coeffs[1]) * around
            lap = lap + around
        result = 2.0 * center - previous + speed_sq * lap
        for direction in range(3):
            result = result - slopes[direction] * derived[direction]
        return result


def row_pairs(visit, first, last, cells):
    def step(pair, carry):
        for row in (first + 2 * pair, first + 2 * pair + 1):
            for cell in cells:
                visit(row, cell)
        return carry

    lax.fori_loop(0, (last - first) // 2, step, 0)


def over_block(visit):
    row_pairs(visit, 0, ROWS, range(0, CELLS, 8))


def over_near(visit):
    sides, middle = range(8, 8 + CELLS, 8), range(4, 12 + CELLS, 8)
    row_pairs(visit, 0, 4, sides)
    row_pairs(visit, 4, 4 + ROWS, middle)
    row_pairs(visit, 4 + ROWS, 8 + ROWS, sides)


def add_source(place, amount, first, target):
    @pl.when(place[first] > 0)
    def _():
        row, half = place[first + 1], place[first + 2]
        values = target[row, half]
        cell = lax.broadcasted_iota(jnp.int32, values.shape, 0)
        lane = lax.broadcasted_iota(jnp.int32, values.shape, 1)
        hit = (cell == place[first + 3]) & (lane == place[first + 4])
        target[row, half] = values + jnp.where(hit, amount, 0.0)


def near_step(source, old, model, lane, out, extra=None):
    speed_sq, slopes = model[0], model[1:]

    def visit(row, cell):
        stencil = Stencil(source, row + 4, cell, lane)
        cut = slice(cell, cell + 8)
        for half in (0, 1):
            value = stencil.advanced(
                half,
                old[row, half, cut, :],
                speed_sq[row, half, cut, :],
                [s[row, half, cut, :] for s in slopes],
            )
            if extra is not None:
                value = value + extra(row, half, cut)
            out[row, half, cut, :] = value

    over_near(visit)


def block_step(source, old, model, lane, finish):
    speed_sq, slopes = model[0], model[1:]

    def visit(row, cell):
        stencil = Stencil(source, row + 4, cell + 8, lane)
        near = slice(cell + 8, cell + 16)
        for half in (0, 1):
            value = stencil.advanced(
                half,
                old(row, half, slice(cell, cell + 8)),
                speed_sq[row + 4, half, near, :],
                [s[row + 4, half, near, :] for s in slopes],
            )
            finish(row, half, slice(cell, cell + 8), value)

    over_block(visit)


def of_block(ref):
    return lambda row, half, cut: ref[row, half, cut, :]


def of_near(ref):
    return lambda row, half, cut: ref[row + 4, half, cut.start + 8 : cut.stop + 8, :]


def of_wide(ref):
    return lambda row, half, cut: ref[row + 8, half, cut.start + 8 : cut.stop + 8, :]


def injected(maps, index, field):
    def near(row, half, cut):
        hits = maps[row, half, cut, 0:128]
        seen = maps[row, half, cut, 128 * index : 128 * index + 128]
        return hits * field[row, half, cut, :] - seen

    return near


def fill_wide(wide, block, halo):
    below, above, left, right = halo
    wide[0:8, :, 8 : 8 + CELLS, :] = below[...]
    wide[8 : 8 + ROWS, :, 8 : 8 + CELLS, :] = block[...]
    wide[8 + ROWS : 16 + ROWS, :, 8 : 8 + CELLS, :] = above[...]
    wide[4 : 12 + ROWS, :, 0:8, :] = left[...]
    wide[4 : 12 + ROWS, :, 8 + CELLS : SPAN, :] = right[...]


WIDE_EDGES = [region(8, CELLS)] * 2


def write_wide_edges(block, edges):
    low, high = edges
    low[...] = block[0:8]
    high[...] = block[ROWS - 8 : ROWS]


def rim_body(block, below, above, low, high):
    for out, cut in ((low, slice(0, 8)), (high, slice(CELLS - 8, CELLS))):
        out[0:4] = below[4:8, :, cut, :]
        out[4 : 4 + ROWS] = block[:, :, cut, :]
        out[4 + ROWS : 8 + ROWS] = above[0:4, :, cut, :]


def swap_wide_edges(block, edges):
    low, high = edges
    below, above = send_group(high, 1), send_group(low, -1)
    low_cells, high_cells = call(rim_body, [region(ROWS + 8, 8)] * 2, 0, (block, below, above))
    return below, above, send_cells(high_cells, 1), send_cells(low_cells, -1)


def cut_body(chunks, *refs, margins):
    count = len(margins)
    slabs, pieces = refs[:count], refs[count:]
    for turn in range(4):
        chunk = chunks[turn]
        first = pl.multiple_of(chunk * CELLS, CELLS)
        before = pl.multiple_of(jnp.maximum(first - 8, 0), 8)
        after = pl.multiple_of(jnp.minimum(first + CELLS, NY - 8), 8)
        at = 0
        for slab, margin in zip(slabs, margins):
            if margin:
                pieces[turn][:, at : at + 8, :] = jnp.where(chunk > 0, slab[:, pl.ds(before, 8), :], 0.0)
                at += 8
            pieces[turn][:, at : at + CELLS, :] = slab[:, pl.ds(first, CELLS), :]
            at += CELLS
            if margin:
                pieces[turn][:, at : at + 8, :] = jnp.where(chunk < 3, slab[:, pl.ds(after, 8), :], 0.0)
                at += 8


def cut_pieces(slabs, margins, chunks):
    width = sum(SPAN if margin else CELLS for margin in margins)
    pieces = call(functools.partial(cut_body, margins=margins), [shape(4, width, NZ)] * 4, 1, (chunks, *slabs))
    return pieces


def place_pieces(slots, pieces, outs):
    for turn in range(4):
        slot = pl.multiple_of(slots[turn] * 4, 4)
        at = 0
        for out in outs:
            width = out.shape[2]
            for half in (0, 1):
                out[pl.ds(slot, 4), half] = pieces[turn][:, at : at + width, 128 * half : 128 * half + 128]
            at += width


def gather_body(slots, *refs, depths):
    pieces, outs = refs[:4], refs[4:]
    low, high = outs[-2:]
    place_pieces(slots, pieces, outs[:-2])
    at = 0
    for out, depth in zip(outs, depths):
        if depth:
            low[at : at + depth] = out[0:depth]
            high[at : at + depth] = out[ROWS - depth : ROWS]
            at += depth


def gather_blocks(pieces, slots, depths):
    outs = [region(ROWS, SPAN if depth else CELLS) for depth in depths]
    outs += [region(sum(depths), SPAN)] * 2
    return call(functools.partial(gather_body, depths=depths), outs, 1, (slots, *pieces))


def stack_rows(out, below, middle, above, at, depth):
    out[0:depth] = below[at : at + depth]
    out[depth : depth + ROWS] = middle[...]
    out[depth + ROWS : 2 * depth + ROWS] = above[at : at + depth]


def fields_body(now, old, adjoint, below, above, wide, old_near, adjoint_near):
    stack_rows(wide, below, now, above, 0, 8)
    stack_rows(old_near, below, old, above, 8, 4)
    stack_rows(adjoint_near, below, adjoint, above, 12, 4)


def model_body(log_mass, speed, below, above, speed_sq, s0, s1, s2, twice, wide, speed_near):
    stack_rows(wide, below, log_mass, above, 0, 8)
    stack_rows(speed_near, below, speed, above, 8, 4)
    twice[...] = 2.0 / speed[:, :, 8 : 8 + CELLS, :]
    lane = lanes()

    def visit(row, cell):
        stencil = Stencil(wide, row + 4, cell, lane)
        cut = slice(cell, cell + 8)
        for half in (0, 1):
            value = speed_near[row, half, cut, :]
            scale = time_step_sq * value * value
            speed_sq[row, half, cut, :] = lap_coeffs[1] * scale
            scale = (diff_coeffs[0] * diff_coeffs[0]) * scale
            for direction, out in enumerate((s0, s1, s2)):
                out[row, half, cut, :] = scale * stencil.derivative(direction, half)

    over_near(visit)


def forward_body(place, amount, wide, old, speed_sq, s0, s1, s2, near, new, *edges):
    model = (speed_sq, s0, s1, s2)
    lane = lanes()
    near_step(wide, old, model, lane, near)
    add_source(place, amount[0], 0, near)

    def finish(row, half, cut, value):
        new[row, half, cut, :] = value

    block_step(near, of_wide(wide), model, lane, finish)
    add_source(place, amount[1], 5, new)
    write_wide_edges(new, edges)


def write_pieces(slots, block, pieces, at):
    for turn in range(4):
        slot = pl.multiple_of(slots[turn] * 4, 4)
        for half in (0, 1):
            pieces[turn][:, at : at + CELLS, 128 * half : 128 * half + 128] = block[pl.ds(slot, 4), half]


def turn_body(place, amount, slots, block, *refs):
    halo, refs = refs[:4], refs[4:]
    old, speed_sq, s0, s1, s2, adjoint, later, maps, near, new, adjoint_new, summed = refs[:12]
    edges, pieces, wide = refs[12:14], refs[14:18], refs[18]
    model = (speed_sq, s0, s1, s2)
    lane = lanes()
    fill_wide(wide, block, halo)
    near_step(wide, old, model, lane, near)
    add_source(place, amount[2], 0, near)

    def finish(row, half, cut, value):
        new[row, half, cut, :] = value

    block_step(near, of_block(block), model, lane, finish)
    add_source(place, amount[3], 5, new)

    def finish_adjoint(row, half, cut, value):
        hits = of_near(maps)(row, half, cut)
        ahead = new[row, half, cut, :]
        value = value + (hits[:, 0:128] * ahead - hits[:, 4 * 128 : 5 * 128])
        adjoint_new[row, half, cut, :] = value
        summed[row, half, cut, :] = value * (
            ahead - 2.0 * of_near(near)(row, half, cut) + block[row, half, cut, :]
        )

    block_step(adjoint, of_block(later), model, lane, finish_adjoint)
    write_wide_edges(adjoint_new, edges)
    write_pieces(slots, new, pieces, 0)


def adjoint_body(block, *refs):
    halo, refs = refs[:4], refs[4:]
    old, speed_sq, s0, s1, s2, maps, u3, u2, u1, u0, sums = refs[:11]
    near, new, summed, low, high, low_cells, high_cells, wide = refs[11:]
    model = (speed_sq, s0, s1, s2)
    lane = lanes()
    fill_wide(wide, block, halo)
    near_step(wide, old, model, lane, near, injected(maps, 3, u3))

    def finish(row, half, cut, value):
        hits = of_near(maps)(row, half, cut)
        third = of_near(u3)(row, half, cut)
        second = u2[row, half, cut, :]
        first = of_near(u1)(row, half, cut)
        zeroth = of_wide(u0)(row, half, cut)
        value = value + (hits[:, 0:128] * second - hits[:, 2 * 128 : 3 * 128])
        new[row, half, cut, :] = value
        total = sums[row, half, cut, :]
        total = total + of_near(near)(row, half, cut) * (third - 2.0 * second + first)
        summed[row, half, cut, :] = total + value * (second - 2.0 * first + zeroth)

    block_step(near, of_block(block), model, lane, finish)
    low[...] = new[0:4]
    high[...] = new[ROWS - 4 : ROWS]
    low_cells[...] = new[:, :, 0:8, :]
    high_cells[...] = new[:, :, CELLS - 8 : CELLS, :]


def last_body(
    slots, model_slots, block, below, above, left, right, old, speed_sq, s0, s1, s2, maps,
    u1, u0, u_before, sums, twice, p0, p1, p2, p3, near, new, image,
):
    near[0:4, :, 8 : 8 + CELLS, :] = below[...]
    near[4 : 4 + ROWS, :, 8 : 8 + CELLS, :] = block[...]
    near[4 + ROWS : 8 + ROWS, :, 8 : 8 + CELLS, :] = above[...]
    near[4 : 4 + ROWS, :, 0:8, :] = left[...]
    near[4 : 4 + ROWS, :, 8 + CELLS : SPAN, :] = right[...]
    lane = lanes()

    def finish(row, half, cut, value):
        hits = of_near(maps)(row, half, cut)
        first = of_near(u1)(row, half, cut)
        value = value + (hits[:, 0:128] * first - hits[:, 128:256])
        new[row, half, cut, :] = value
        curvature = first - 2.0 * of_wide(u0)(row, half, cut) + of_near(u_before)(row, half, cut)
        image[row, half, cut, :] = twice[row, half, cut, :] * (sums[row, half, cut, :] + value * curvature)

    block_step(near, of_near(old), (speed_sq, s0, s1, s2), lane, finish)
    write_pieces(model_slots, image, (p0, p1, p2, p3), 0)
    write_pieces(slots, new, (p0, p1, p2, p3), CELLS)


def spread_body(chunks, p0, p1, p2, p3, *outs):
    for turn, piece in enumerate((p0, p1, p2, p3)):
        first = pl.multiple_of(chunks[turn] * CELLS, CELLS)
        for index, out in enumerate(outs):
            out[:, pl.ds(first, CELLS), :] = piece[:, CELLS * index : CELLS * index + CELLS, :]


def sent_pieces(pieces):
    return [pieces[0]] + [send_y(pieces[turn], turn) for turn in (1, 2, 3)]


def to_slabs(pieces, chunks, count):
    return call(spread_body, [shape(4, NY, NZ)] * count, 1, (chunks, *pieces))


def on_device(
    velocity,
    density,
    aperture_start,
    source_cell,
    receiver_cells,
    wavelet,
    observed,
    forward_old,
    forward_now,
    adjoint_later,
    adjoint_now,
):
    shot = lax.axis_index("shot")
    sub = lax.axis_index("sub")
    core = shot % 2
    x_hi = sub // 16
    x = 2 * x_hi + shot // 2
    z = (sub // 4) % 4
    y = sub % 4
    group = sub // 4
    start = aperture_start[0]
    partner = send_core(aperture_start)

    def wanted(first_slab):
        upper = first_slab // 4 + (y < first_slab % 4).astype(jnp.int32)
        block = jnp.clip(x_hi + (upper - z + 3) // 4, 0, 7)
        position = 2 * (block % 2) + block // 4
        return (block // 2) % 2, (position - x) % 4, upper % 4

    own_core, own_step, turn_by = wanted(start)
    turns = jnp.arange(4, dtype=jnp.int32)
    chunks_out = (y + turns) % 4
    chunks_in = (y - turns) % 4
    slots_in = (y - turns - start % 4) % 4
    slots_out = (y + turns - start % 4) % 4

    pieces = cut_pieces(
        [forward_now[0], forward_old[0], adjoint_now[0], adjoint_later[0]],
        (True, True, True, False),
        chunks_out,
    )
    density, partner, *pieces = lax.optimization_barrier((density, partner, *pieces))
    pair_core, pair_step, _ = wanted(partner[0])

    def gathered(slab):
        from_below = send_x(slab, 1)
        from_above = send_x(slab, -1)
        far = jnp.concatenate([send_x(from_below[0:2], 1), send_x(from_above[2:4], -1)])

        def pick(step):
            return jnp.where(
                step < 2, jnp.where(step == 0, slab, from_above), jnp.where(step == 2, far, from_below)
            )

        other = send_core(pick(pair_step))
        return jnp.where(own_core == core, pick(own_step), other)

    def turned(arrays, steps):
        def branch(count):
            return lambda *values: tuple(send_z(value, count) if count else value for value in values)

        return lax.switch(steps, [branch(count) for count in (0, 1, 2, -1)], *arrays)

    log_slab = gathered(jnp.log(density))
    speed_slab = gathered(velocity)
    pieces = sent_pieces(pieces)
    now, old, adjoint, a_later, side_low, side_high = gather_blocks(pieces, chunks_in, (8, 4, 4, 0))

    def local_place(cells, rows_more, cells_more):
        rows = cells // (NY * NZ) - group * ROWS + rows_more
        columns = (cells // NZ) % NY - y * CELLS + cells_more
        inside = (rows >= 0) & (rows < ROWS + 2 * rows_more)
        inside = inside & (columns >= 0) & (columns < CELLS + 2 * cells_more)
        return inside, rows, (cells // 128) % 2, columns, cells % 128

    inside, rows, half, columns, lane = local_place(receiver_cells[0], 4, 8)
    line = jnp.where(inside, (rows * 2 + half) * SPAN + columns, -1)
    lines = (ROWS + 8) * 2 * SPAN
    on_line = (jnp.arange(lines, dtype=jnp.int32)[:, None] == line[None, :]).astype(F32)
    weights = jnp.concatenate([jnp.ones_like(observed[0, :1]), observed[0]])
    hit = lane[:, None, None] == jnp.arange(128, dtype=jnp.int32)[None, None, :]
    at_lane = jnp.where(hit, weights.T[:, :, None], 0.0).reshape(-1, 5 * 128)
    maps = jnp.dot(on_line, at_lane, precision=lax.Precision.HIGHEST)
    maps = maps.reshape(ROWS + 8, 2, SPAN, 5 * 128)

    def source_place(rows_more, cells_more):
        inside, rows, half, columns, lane = local_place(source_cell[0], rows_more, cells_more)
        rows = jnp.clip(rows, 0, ROWS + 2 * rows_more - 1)
        return [inside.astype(jnp.int32), rows, half, columns, lane]

    place = jnp.stack(source_place(4, 8) + source_place(0, 0))
    amount = wavelet[0]

    log_slab, speed_slab, maps, side_low, side_high = lax.optimization_barrier(
        (log_slab, speed_slab, maps, side_low, side_high)
    )
    log_slab, speed_slab = turned((log_slab, speed_slab), (4 - turn_by) % 4)
    log_slab, speed_slab, side_low, side_high = lax.optimization_barrier(
        (log_slab, speed_slab, side_low, side_high)
    )
    pieces = sent_pieces(cut_pieces([log_slab, speed_slab], (True, True), chunks_out))
    below, above = send_group(side_high, 1), send_group(side_low, -1)
    u_wide, old_near, a_near = call(
        fields_body, [WIDE, NEAR, NEAR], 0, (now, old, adjoint, below, above)
    )
    log_mass, speed, side_low, side_high = gather_blocks(pieces, slots_in, (8, 4))
    below, above = send_group(side_high, 1), send_group(side_low, -1)
    *model, twice = call(
        model_body, [NEAR] * 4 + [BLOCK], 0, (log_mass, speed, below, above), (WIDE, NEAR)
    )

    u1, u2, *edges = call(
        forward_body, [NEAR, BLOCK] + WIDE_EDGES, 2, (place, amount, u_wide, old_near, *model)
    )
    halo = swap_wide_edges(u2, edges)
    u3, _, a3, sums, *rest = call(
        turn_body,
        [NEAR, BLOCK, BLOCK, BLOCK] + WIDE_EDGES + [shape(4, CELLS, NZ)] * 4,
        3,
        (place, amount, chunks_out, u2, *halo, u1, *model, a_near, a_later, maps),
        (WIDE,),
    )
    halo = swap_wide_edges(a3, rest[:2])
    last_pieces = sent_pieces(rest[2:])
    a2, a1, sums, side_low, side_high, low_cells, high_cells = call(
        adjoint_body,
        [NEAR, BLOCK, BLOCK] + [region(4, CELLS)] * 2 + [region(ROWS, 8)] * 2,
        0,
        (a3, *halo, a_near, *model, maps, u3, u2, u1, u_wide, sums),
        (WIDE,),
    )
    side_low, side_high, low_cells, high_cells, *last_pieces = lax.optimization_barrier(
        (side_low, side_high, low_cells, high_cells, *last_pieces)
    )
    (forward_last,) = to_slabs(last_pieces, chunks_in, 1)
    halo = (
        send_group(side_high, 1),
        send_group(side_low, -1),
        send_cells(high_cells, 1),
        send_cells(low_cells, -1),
    )
    pieces = call(
        last_body,
        [shape(4, 2 * CELLS, NZ)] * 4,
        2,
        (chunks_out, slots_out, a1, *halo, a2, *model, maps, u1, u_wide, old_near, sums, twice),
        (NEAR, BLOCK, BLOCK),
    )
    image, adjoint_first = to_slabs(sent_pieces(pieces), chunks_in, 2)

    def both(first_half, second_half):
        return jnp.concatenate([first_half, second_half])

    (image,) = turned((image,), turn_by)
    other = send_core(image)

    def share(step):
        mine = jnp.where((own_core == core) & (own_step == step), image, 0.0)
        return mine + jnp.where((pair_core == core) & (pair_step == step), other, 0.0)

    far = share(2)
    passing_up = send_x(far[0:2], 1)
    passing_down = send_x(far[2:4], -1)
    up = share(1)
    down = share(3)
    up = send_x(both(up[0:2] + passing_up, up[2:4]), 1)
    down = send_x(both(down[0:2], down[2:4] + passing_down), -1)
    gradient = share(0) + up + down
    return (gradient, forward_last[None], adjoint_first[None])


def solution(mesh):
    placed = (
        P(("shot", "sub"), None, None),
        P(("shot", "sub"), None, None),
        P("shot"),
        P("shot"),
        P("shot", None),
        P("shot", None),
        P("shot", None, None),
        P("shot", "sub", None, None),
        P("shot", "sub", None, None),
        P("shot", "sub", None, None),
        P("shot", "sub", None, None),
    )
    return jax.shard_map(
        on_device,
        mesh=mesh,
        in_specs=placed,
        out_specs=(
            P(("shot", "sub"), None, None),
            P("shot", "sub", None, None),
            P("shot", "sub", None, None),
        ),
        check_vma=False,
    )
```

```python
import functools

import jax
import jax.numpy as jnp
from jax import lax
from jax.experimental import pallas as pl
from jax.experimental.pallas import tpu as pltpu
from jax.sharding import PartitionSpec as P

lap_coeffs = (-205.0 / 72.0, 8.0 / 5.0, -1.0 / 5.0, 8.0 / 315.0, -1.0 / 560.0)
diff_coeffs = (4.0 / 5.0, -1.0 / 5.0, 4.0 / 105.0, -1.0 / 280.0)
time_step_sq = 0.0088

ROWS = 16
CELLS = 32
SPAN = CELLS + 16
NY = 128
NZ = 256
F32 = jnp.float32
LIMIT = 24 * 2**20


def pairs_by(move):
    pairs = []
    for shot in range(4):
        for sub in range(32):
            x = 2 * (sub // 16) + shot // 2
            target = move(x, shot % 2, (sub // 4) % 4, sub % 4)
            if target is None:
                continue
            tx, tcore, tz, ty = target
            pairs.append((shot * 32 + sub, ((tx % 2) * 2 + tcore) * 32 + (tx // 2) * 16 + tz * 4 + ty))
    return pairs


def send(value, move):
    return lax.ppermute(value, ("shot", "sub"), pairs_by(move))


def send_x(value, steps):
    return send(value, lambda x, c, z, y: ((x + steps) % 4, c, z, y))


def send_core(value):
    return send(value, lambda x, c, z, y: (x, 1 - c, z, y))


def send_z(value, steps):
    return send(value, lambda x, c, z, y: (x, c, (z + steps) % 4, y))


def send_y(value, steps):
    return send(value, lambda x, c, z, y: (x, c, z, (y + steps) % 4))


def next_rows(x, z, steps):
    group = (x // 2) * 4 + z + steps
    if group < 0 or group > 7:
        return None
    return (2 * (group // 4) + x % 2, group % 4)


def send_group(value, steps):
    def move(x, c, z, y):
        place = next_rows(x, z, steps)
        return None if place is None else (place[0], c, place[1], y)

    return send(value, move)


def send_cells(value, steps):
    return send(value, lambda x, c, z, y: (x, c, z, y + steps) if 0 <= y + steps < 4 else None)


def shape(*sizes):
    return jax.ShapeDtypeStruct(sizes, F32)


def region(rows, cells):
    return shape(rows, 2, cells, 128)


BLOCK = region(ROWS, CELLS)
NEAR = region(ROWS + 8, SPAN)
WIDE = region(ROWS + 16, SPAN)


def call(body, outs, n_smem, operands, scratch=()):
    specs = [pl.BlockSpec(memory_space=pltpu.SMEM)] * n_smem
    specs += [pl.BlockSpec(memory_space=pltpu.VMEM)] * (len(operands) - n_smem)
    return pl.pallas_call(
        body,
        out_shape=tuple(outs),
        in_specs=specs,
        out_specs=tuple(pl.BlockSpec(memory_space=pltpu.VMEM) for _ in outs),
        scratch_shapes=[pltpu.VMEM(s.shape, s.dtype) for s in scratch],
        compiler_params=pltpu.CompilerParams(vmem_limit_bytes=LIMIT),
    )(*operands)


def lanes():
    return lax.broadcasted_iota(jnp.int32, (8, 128), 1)


class Stencil:
    def __init__(self, source, row, cell, lane):
        self.source, self.row, self.cell, self.lane = source, row, cell, lane
        self.center = [self.load(0, 0, half) for half in (0, 1)]
        low, high = self.center
        self.deep = []
        for reach in range(1, 5):
            ahead = [pltpu.roll(v, 128 - reach, 1) for v in (low, high)]
            behind = [pltpu.roll(v, reach, 1) for v in (low, high)]
            front = lane < 128 - reach
            back = lane >= reach
            self.deep.append(
                (
                    (jnp.where(front, ahead[0], ahead[1]), jnp.where(front, ahead[1], 0.0)),
                    (jnp.where(back, behind[0], 0.0), jnp.where(back, behind[1], behind[0])),
                )
            )

    def load(self, rows, cells, half):
        first = self.cell + cells
        return self.source[self.row + rows, half, first : first + 8, :]

    def both(self, direction, reach, half):
        if direction == 0:
            return self.load(reach, 0, half), self.load(-reach, 0, half)
        if direction == 1:
            return self.load(0, reach, half), self.load(0, -reach, half)
        ahead, behind = self.deep[reach - 1]
        return ahead[half], behind[half]

    def derivative(self, direction, half):
        ahead, behind = self.both(direction, 1, half)
        total = ahead - behind
        for reach in range(2, 5):
            ahead, behind = self.both(direction, reach, half)
            total = total + (diff_coeffs[reach - 1] / diff_coeffs[0]) * (ahead - behind)
        return total

    def advanced(self, half, previous, speed_sq, slopes):
        center = self.center[half]
        lap = (3.0 * lap_coeffs[0] / lap_coeffs[1]) * center
        derived = [None, None, None]
        for reach in range(1, 5):
            around = None
            for direction in range(3):
                ahead, behind = self.both(direction, reach, half)
                pair = ahead + behind
                around = pair if around is None else around + pair
                part = ahead - behind
                if reach > 1:
                    part = derived[direction] + (diff_coeffs[reach - 1] / diff_coeffs[0]) * part
                derived[direction] = part
            if reach > 1:
                around = (lap_coeffs[reach] / lap_coeffs[1]) * around
            lap = lap + around
        result = 2.0 * center - previous + speed_sq * lap
        for direction in range(3):
            result = result - slopes[direction] * derived[direction]
        return result


def row_pairs(visit, first, last, cells):
    def step(pair, carry):
        for row in (first + 2 * pair, first + 2 * pair + 1):
            for cell in cells:
                visit(row, cell)
        return carry

    lax.fori_loop(0, (last - first) // 2, step, 0)


def over_block(visit):
    row_pairs(visit, 0, ROWS, range(0, CELLS, 8))


def over_near(visit):
    sides, middle = range(8, 8 + CELLS, 8), range(4, 12 + CELLS, 8)
    row_pairs(visit, 0, 4, sides)
    row_pairs(visit, 4, 4 + ROWS, middle)
    row_pairs(visit, 4 + ROWS, 8 + ROWS, sides)


def add_source(place, amount, first, target):
    @pl.when(place[first] > 0)
    def _():
        row, half = place[first + 1], place[first + 2]
        values = target[row, half]
        cell = lax.broadcasted_iota(jnp.int32, values.shape, 0)
        lane = lax.broadcasted_iota(jnp.int32, values.shape, 1)
        hit = (cell == place[first + 3]) & (lane == place[first + 4])
        target[row, half] = values + jnp.where(hit, amount, 0.0)


def near_step(source, old, model, lane, out, extra=None):
    speed_sq, slopes = model[0], model[1:]

    def visit(row, cell):
        stencil = Stencil(source, row + 4, cell, lane)
        cut = slice(cell, cell + 8)
        for half in (0, 1):
            value = stencil.advanced(
                half,
                old[row, half, cut, :],
                speed_sq[row, half, cut, :],
                [s[row, half, cut, :] for s in slopes],
            )
            if extra is not None:
                value = value + extra(row, half, cut)
            out[row, half, cut, :] = value

    over_near(visit)


def block_step(source, old, model, lane, finish):
    speed_sq, slopes = model[0], model[1:]

    def visit(row, cell):
        stencil = Stencil(source, row + 4, cell + 8, lane)
        near = slice(cell + 8, cell + 16)
        for half in (0, 1):
            value = stencil.advanced(
                half,
                old(row, half, slice(cell, cell + 8)),
                speed_sq[row + 4, half, near, :],
                [s[row + 4, half, near, :] for s in slopes],
            )
            finish(row, half, slice(cell, cell + 8), value)

    over_block(visit)


def of_block(ref):
    return lambda row, half, cut: ref[row, half, cut, :]


def of_near(ref):
    return lambda row, half, cut: ref[row + 4, half, cut.start + 8 : cut.stop + 8, :]


def of_wide(ref):
    return lambda row, half, cut: ref[row + 8, half, cut.start + 8 : cut.stop + 8, :]


def injected(maps, index, field):
    def near(row, half, cut):
        hits = maps[row, half, cut, 0:128]
        seen = maps[row, half, cut, 128 * index : 128 * index + 128]
        return hits * field[row, half, cut, :] - seen

    return near


def fill_wide(wide, block, halo):
    below, above, left, right = halo
    wide[0:8, :, 8 : 8 + CELLS, :] = below[...]
    wide[8 : 8 + ROWS, :, 8 : 8 + CELLS, :] = block[...]
    wide[8 + ROWS : 16 + ROWS, :, 8 : 8 + CELLS, :] = above[...]
    wide[4 : 12 + ROWS, :, 0:8, :] = left[...]
    wide[4 : 12 + ROWS, :, 8 + CELLS : SPAN, :] = right[...]


WIDE_EDGES = [region(8, CELLS)] * 2


def write_wide_edges(block, edges):
    low, high = edges
    low[...] = block[0:8]
    high[...] = block[ROWS - 8 : ROWS]


def rim_body(block, below, above, low, high):
    for out, cut in ((low, slice(0, 8)), (high, slice(CELLS - 8, CELLS))):
        out[0:4] = below[4:8, :, cut, :]
        out[4 : 4 + ROWS] = block[:, :, cut, :]
        out[4 + ROWS : 8 + ROWS] = above[0:4, :, cut, :]


def swap_wide_edges(block, edges):
    low, high = edges
    below, above = send_group(high, 1), send_group(low, -1)
    low_cells, high_cells = call(rim_body, [region(ROWS + 8, 8)] * 2, 0, (block, below, above))
    return below, above, send_cells(high_cells, 1), send_cells(low_cells, -1)


def cut_body(chunks, *refs, margins):
    count = len(margins)
    slabs, pieces = refs[:count], refs[count:]
    for turn in range(4):
        chunk = chunks[turn]
        first = pl.multiple_of(chunk * CELLS, CELLS)
        before = pl.multiple_of(jnp.maximum(first - 8, 0), 8)
        after = pl.multiple_of(jnp.minimum(first + CELLS, NY - 8), 8)
        at = 0
        for slab, margin in zip(slabs, margins):
            if margin:
                pieces[turn][:, at : at + 8, :] = jnp.where(chunk > 0, slab[:, pl.ds(before, 8), :], 0.0)
                at += 8
            pieces[turn][:, at : at + CELLS, :] = slab[:, pl.ds(first, CELLS), :]
            at += CELLS
            if margin:
                pieces[turn][:, at : at + 8, :] = jnp.where(chunk < 3, slab[:, pl.ds(after, 8), :], 0.0)
                at += 8


def cut_pieces(slabs, margins, chunks):
    width = sum(SPAN if margin else CELLS for margin in margins)
    pieces = call(functools.partial(cut_body, margins=margins), [shape(4, width, NZ)] * 4, 1, (chunks, *slabs))
    return pieces


def place_pieces(slots, pieces, outs):
    for turn in range(4):
        slot = pl.multiple_of(slots[turn] * 4, 4)
        at = 0
        for out in outs:
            width = out.shape[2]
            for half in (0, 1):
                out[pl.ds(slot, 4), half] = pieces[turn][:, at : at + width, 128 * half : 128 * half + 128]
            at += width


def gather_body(slots, *refs, depths):
    pieces, outs = refs[:4], refs[4:]
    low, high = outs[-2:]
    place_pieces(slots, pieces, outs[:-2])
    at = 0
    for out, depth in zip(outs, depths):
        if depth:
            low[at : at + depth] = out[0:depth]
            high[at : at + depth] = out[ROWS - depth : ROWS]
            at += depth


def gather_blocks(pieces, slots, depths):
    outs = [region(ROWS, SPAN if depth else CELLS) for depth in depths]
    outs += [region(sum(depths), SPAN)] * 2
    return call(functools.partial(gather_body, depths=depths), outs, 1, (slots, *pieces))


def stack_rows(out, below, middle, above, at, depth):
    out[0:depth] = below[at : at + depth]
    out[depth : depth + ROWS] = middle[...]
    out[depth + ROWS : 2 * depth + ROWS] = above[at : at + depth]


def fields_body(now, old, adjoint, below, above, wide, old_near, adjoint_near):
    stack_rows(wide, below, now, above, 0, 8)
    stack_rows(old_near, below, old, above, 8, 4)
    stack_rows(adjoint_near, below, adjoint, above, 12, 4)


def model_body(log_mass, speed, below, above, speed_sq, s0, s1, s2, twice, wide, speed_near):
    stack_rows(wide, below, log_mass, above, 0, 8)
    stack_rows(speed_near, below, speed, above, 8, 4)
    twice[...] = 2.0 / speed[:, :, 8 : 8 + CELLS, :]
    lane = lanes()

    def visit(row, cell):
        stencil = Stencil(wide, row + 4, cell, lane)
        cut = slice(cell, cell + 8)
        for half in (0, 1):
            value = speed_near[row, half, cut, :]
            scale = time_step_sq * value * value
            speed_sq[row, half, cut, :] = lap_coeffs[1] * scale
            scale = (diff_coeffs[0] * diff_coeffs[0]) * scale
            for direction, out in enumerate((s0, s1, s2)):
                out[row, half, cut, :] = scale * stencil.derivative(direction, half)

    over_near(visit)


def forward_body(place, amount, wide, old, speed_sq, s0, s1, s2, near, new, *edges):
    model = (speed_sq, s0, s1, s2)
    lane = lanes()
    near_step(wide, old, model, lane, near)
    add_source(place, amount[0], 0, near)

    def finish(row, half, cut, value):
        new[row, half, cut, :] = value

    block_step(near, of_wide(wide), model, lane, finish)
    add_source(place, amount[1], 5, new)
    write_wide_edges(new, edges)


def write_pieces(slots, block, pieces, at):
    for turn in range(4):
        slot = pl.multiple_of(slots[turn] * 4, 4)
        for half in (0, 1):
            pieces[turn][:, at : at + CELLS, 128 * half : 128 * half + 128] = block[pl.ds(slot, 4), half]


def turn_body(place, amount, block, *refs):
    halo, refs = refs[:4], refs[4:]
    old, speed_sq, s0, s1, s2, adjoint, later, maps, near, new, adjoint_new, summed = refs[:12]
    edges, wide = refs[12:14], refs[14]
    model = (speed_sq, s0, s1, s2)
    lane = lanes()
    fill_wide(wide, block, halo)
    near_step(wide, old, model, lane, near)
    add_source(place, amount[2], 0, near)

    def finish(row, half, cut, value):
        new[row, half, cut, :] = value

    block_step(near, of_block(block), model, lane, finish)
    add_source(place, amount[3], 5, new)

    def finish_adjoint(row, half, cut, value):
        hits = of_near(maps)(row, half, cut)
        ahead = new[row, half, cut, :]
        value = value + (hits[:, 0:128] * ahead - hits[:, 4 * 128 : 5 * 128])
        adjoint_new[row, half, cut, :] = value
        summed[row, half, cut, :] = value * (
            ahead - 2.0 * of_near(near)(row, half, cut) + block[row, half, cut, :]
        )

    block_step(adjoint, of_block(later), model, lane, finish_adjoint)
    write_wide_edges(adjoint_new, edges)


def adjoint_body(block, *refs):
    halo, refs = refs[:4], refs[4:]
    old, speed_sq, s0, s1, s2, maps, u3, u2, u1, u0, sums = refs[:11]
    near, new, summed, low, high, low_cells, high_cells, wide = refs[11:]
    model = (speed_sq, s0, s1, s2)
    lane = lanes()
    fill_wide(wide, block, halo)
    near_step(wide, old, model, lane, near, injected(maps, 3, u3))

    def finish(row, half, cut, value):
        hits = of_near(maps)(row, half, cut)
        third = of_near(u3)(row, half, cut)
        second = u2[row, half, cut, :]
        first = of_near(u1)(row, half, cut)
        zeroth = of_wide(u0)(row, half, cut)
        value = value + (hits[:, 0:128] * second - hits[:, 2 * 128 : 3 * 128])
        new[row, half, cut, :] = value
        total = sums[row, half, cut, :]
        total = total + of_near(near)(row, half, cut) * (third - 2.0 * second + first)
        summed[row, half, cut, :] = total + value * (second - 2.0 * first + zeroth)

    block_step(near, of_block(block), model, lane, finish)
    low[...] = new[0:4]
    high[...] = new[ROWS - 4 : ROWS]
    low_cells[...] = new[:, :, 0:8, :]
    high_cells[...] = new[:, :, CELLS - 8 : CELLS, :]


def last_body(
    slots, model_slots, block, below, above, left, right, old, speed_sq, s0, s1, s2, maps,
    u1, u0, u_before, sums, twice, u4, p0, p1, p2, p3, q0, q1, q2, q3, near, new, image,
):
    near[0:4, :, 8 : 8 + CELLS, :] = below[...]
    near[4 : 4 + ROWS, :, 8 : 8 + CELLS, :] = block[...]
    near[4 + ROWS : 8 + ROWS, :, 8 : 8 + CELLS, :] = above[...]
    near[4 : 4 + ROWS, :, 0:8, :] = left[...]
    near[4 : 4 + ROWS, :, 8 + CELLS : SPAN, :] = right[...]
    lane = lanes()

    def finish(row, half, cut, value):
        hits = of_near(maps)(row, half, cut)
        first = of_near(u1)(row, half, cut)
        value = value + (hits[:, 0:128] * first - hits[:, 128:256])
        new[row, half, cut, :] = value
        curvature = first - 2.0 * of_wide(u0)(row, half, cut) + of_near(u_before)(row, half, cut)
        image[row, half, cut, :] = twice[row, half, cut, :] * (sums[row, half, cut, :] + value * curvature)

    block_step(near, of_near(old), (speed_sq, s0, s1, s2), lane, finish)
    write_pieces(model_slots, image, (p0, p1, p2, p3), 0)
    write_pieces(slots, new, (q0, q1, q2, q3), 0)
    write_pieces(slots, u4, (q0, q1, q2, q3), CELLS)


def spread_body(chunks, p0, p1, p2, p3, *outs):
    for turn, piece in enumerate((p0, p1, p2, p3)):
        first = pl.multiple_of(chunks[turn] * CELLS, CELLS)
        for index, out in enumerate(outs):
            out[:, pl.ds(first, CELLS), :] = piece[:, CELLS * index : CELLS * index + CELLS, :]


def sent_pieces(pieces):
    return [pieces[0]] + [send_y(pieces[turn], turn) for turn in (1, 2, 3)]


def to_slabs(pieces, chunks, count):
    return call(spread_body, [shape(4, NY, NZ)] * count, 1, (chunks, *pieces))


def on_device(
    velocity,
    density,
    aperture_start,
    source_cell,
    receiver_cells,
    wavelet,
    observed,
    forward_old,
    forward_now,
    adjoint_later,
    adjoint_now,
):
    shot = lax.axis_index("shot")
    sub = lax.axis_index("sub")
    core = shot % 2
    x_hi = sub // 16
    x = 2 * x_hi + shot // 2
    z = (sub // 4) % 4
    y = sub % 4
    group = sub // 4
    start = aperture_start[0]
    partner = send_core(aperture_start)

    def wanted(first_slab):
        upper = first_slab // 4 + (y < first_slab % 4).astype(jnp.int32)
        block = jnp.clip(x_hi + (upper - z + 3) // 4, 0, 7)
        position = 2 * (block % 2) + block // 4
        return (block // 2) % 2, (position - x) % 4, upper % 4

    own_core, own_step, turn_by = wanted(start)
    turns = jnp.arange(4, dtype=jnp.int32)
    chunks_out = (y + turns) % 4
    chunks_in = (y - turns) % 4
    slots_in = (y - turns - start % 4) % 4
    slots_out = (y + turns - start % 4) % 4

    pieces = cut_pieces(
        [forward_now[0], forward_old[0], adjoint_now[0], adjoint_later[0]],
        (True, True, True, False),
        chunks_out,
    )
    density, partner, *pieces = lax.optimization_barrier((density, partner, *pieces))
    pair_core, pair_step, _ = wanted(partner[0])

    def gathered(slab):
        from_below = send_x(slab, 1)
        from_above = send_x(slab, -1)
        far = jnp.concatenate([send_x(from_below[0:2], 1), send_x(from_above[2:4], -1)])

        def pick(step):
            return jnp.where(
                step < 2, jnp.where(step == 0, slab, from_above), jnp.where(step == 2, far, from_below)
            )

        other = send_core(pick(pair_step))
        return jnp.where(own_core == core, pick(own_step), other)

    def turned(arrays, steps):
        def branch(count):
            return lambda *values: tuple(send_z(value, count) if count else value for value in values)

        return lax.switch(steps, [branch(count) for count in (0, 1, 2, -1)], *arrays)

    log_slab = gathered(jnp.log(density))
    speed_slab = gathered(velocity)
    pieces = sent_pieces(pieces)

    def local_place(cells, rows_more, cells_more):
        rows = cells // (NY * NZ) - group * ROWS + rows_more
        columns = (cells // NZ) % NY - y * CELLS + cells_more
        inside = (rows >= 0) & (rows < ROWS + 2 * rows_more)
        inside = inside & (columns >= 0) & (columns < CELLS + 2 * cells_more)
        return inside, rows, (cells // 128) % 2, columns, cells % 128

    inside, rows, half, columns, lane = local_place(receiver_cells[0], 4, 8)
    line = jnp.where(inside, (rows * 2 + half) * SPAN + columns, -1)
    lines = (ROWS + 8) * 2 * SPAN
    on_line = (jnp.arange(lines, dtype=jnp.int32)[:, None] == line[None, :]).astype(F32)
    weights = jnp.concatenate([jnp.ones_like(observed[0, :1]), observed[0]])
    hit = lane[:, None, None] == jnp.arange(128, dtype=jnp.int32)[None, None, :]
    at_lane = jnp.where(hit, weights.T[:, :, None], 0.0).reshape(-1, 5 * 128)
    maps = jnp.dot(on_line, at_lane, precision=lax.Precision.HIGHEST)
    maps = maps.reshape(ROWS + 8, 2, SPAN, 5 * 128)

    def source_place(rows_more, cells_more):
        inside, rows, half, columns, lane = local_place(source_cell[0], rows_more, cells_more)
        rows = jnp.clip(rows, 0, ROWS + 2 * rows_more - 1)
        return [inside.astype(jnp.int32), rows, half, columns, lane]

    place = jnp.stack(source_place(4, 8) + source_place(0, 0))
    amount = wavelet[0]

    log_slab, speed_slab, maps = lax.optimization_barrier((log_slab, speed_slab, maps))
    log_slab, speed_slab = turned((log_slab, speed_slab), (4 - turn_by) % 4)
    log_slab, speed_slab, *pieces = lax.optimization_barrier((log_slab, speed_slab, *pieces))
    model_pieces = sent_pieces(cut_pieces([log_slab, speed_slab], (True, True), chunks_out))
    now, old, adjoint, a_later, side_low, side_high = gather_blocks(pieces, chunks_in, (8, 4, 4, 0))
    below, above = send_group(side_high, 1), send_group(side_low, -1)
    u_wide, old_near, a_near = call(
        fields_body, [WIDE, NEAR, NEAR], 0, (now, old, adjoint, below, above)
    )
    log_mass, speed, side_low, side_high = gather_blocks(model_pieces, slots_in, (8, 4))
    below, above = send_group(side_high, 1), send_group(side_low, -1)
    *model, twice = call(
        model_body, [NEAR] * 4 + [BLOCK], 0, (log_mass, speed, below, above), (WIDE, NEAR)
    )

    u1, u2, *edges = call(
        forward_body, [NEAR, BLOCK] + WIDE_EDGES, 2, (place, amount, u_wide, old_near, *model)
    )
    halo = swap_wide_edges(u2, edges)
    u3, u4, a3, sums, *edges = call(
        turn_body,
        [NEAR, BLOCK, BLOCK, BLOCK] + WIDE_EDGES,
        2,
        (place, amount, u2, *halo, u1, *model, a_near, a_later, maps),
        (WIDE,),
    )
    halo = swap_wide_edges(a3, edges)
    a2, a1, sums, side_low, side_high, low_cells, high_cells = call(
        adjoint_body,
        [NEAR, BLOCK, BLOCK] + [region(4, CELLS)] * 2 + [region(ROWS, 8)] * 2,
        0,
        (a3, *halo, a_near, *model, maps, u3, u2, u1, u_wide, sums),
        (WIDE,),
    )
    halo = (
        send_group(side_high, 1),
        send_group(side_low, -1),
        send_cells(high_cells, 1),
        send_cells(low_cells, -1),
    )
    pieces = call(
        last_body,
        [shape(4, CELLS, NZ)] * 4 + [shape(4, 2 * CELLS, NZ)] * 4,
        2,
        (chunks_out, slots_out, a1, *halo, a2, *model, maps, u1, u_wide, old_near, sums, twice, u4),
        (NEAR, BLOCK, BLOCK),
    )
    (image,) = to_slabs(sent_pieces(pieces[:4]), chunks_in, 1)

    def both(first_half, second_half):
        return jnp.concatenate([first_half, second_half])

    (image,) = turned((image,), turn_by)
    image, *pieces = lax.optimization_barrier((image, *pieces[4:]))
    adjoint_first, forward_last = to_slabs(sent_pieces(pieces), chunks_in, 2)
    other = send_core(image)

    def share(step):
        mine = jnp.where((own_core == core) & (own_step == step), image, 0.0)
        return mine + jnp.where((pair_core == core) & (pair_step == step), other, 0.0)

    far = share(2)
    passing_up = send_x(far[0:2], 1)
    passing_down = send_x(far[2:4], -1)
    up = share(1)
    down = share(3)
    up = send_x(both(up[0:2] + passing_up, up[2:4]), 1)
    down = send_x(both(down[0:2], down[2:4] + passing_down), -1)
    gradient = share(0) + up + down
    return (gradient, forward_last[None], adjoint_first[None])


def solution(mesh):
    placed = (
        P(("shot", "sub"), None, None),
        P(("shot", "sub"), None, None),
        P("shot"),
        P("shot"),
        P("shot", None),
        P("shot", None),
        P("shot", None, None),
        P("shot", "sub", None, None),
        P("shot", "sub", None, None),
        P("shot", "sub", None, None),
        P("shot", "sub", None, None),
    )
    return jax.shard_map(
        on_device,
        mesh=mesh,
        in_specs=placed,
        out_specs=(
            P(("shot", "sub"), None, None),
            P("shot", "sub", None, None),
            P("shot", "sub", None, None),
        ),
        check_vma=False,
    )
```

```python
import functools

import jax
import jax.numpy as jnp
from jax import lax
from jax.experimental import pallas as pl
from jax.experimental.pallas import tpu as pltpu
from jax.sharding import PartitionSpec as P

lap_coeffs = (-205.0 / 72.0, 8.0 / 5.0, -1.0 / 5.0, 8.0 / 315.0, -1.0 / 560.0)
diff_coeffs = (4.0 / 5.0, -1.0 / 5.0, 4.0 / 105.0, -1.0 / 280.0)
time_step_sq = 0.0088

ROWS = 16
CELLS = 32
SPAN = CELLS + 16
NY = 128
NZ = 256
F32 = jnp.float32
LIMIT = 24 * 2**20


def pairs_by(move):
    pairs = []
    for shot in range(4):
        for sub in range(32):
            x = 2 * (sub // 16) + shot // 2
            target = move(x, shot % 2, (sub // 4) % 4, sub % 4)
            if target is None:
                continue
            tx, tcore, tz, ty = target
            pairs.append((shot * 32 + sub, ((tx % 2) * 2 + tcore) * 32 + (tx // 2) * 16 + tz * 4 + ty))
    return pairs


def send(value, move):
    return lax.ppermute(value, ("shot", "sub"), pairs_by(move))


def send_x(value, steps):
    return send(value, lambda x, c, z, y: ((x + steps) % 4, c, z, y))


def send_core(value):
    return send(value, lambda x, c, z, y: (x, 1 - c, z, y))


def send_z(value, steps):
    return send(value, lambda x, c, z, y: (x, c, (z + steps) % 4, y))


def send_y(value, steps):
    return send(value, lambda x, c, z, y: (x, c, z, (y + steps) % 4))


def next_rows(x, z, steps):
    group = (x // 2) * 4 + z + steps
    if group < 0 or group > 7:
        return None
    return (2 * (group // 4) + x % 2, group % 4)


def send_group(value, steps):
    def move(x, c, z, y):
        place = next_rows(x, z, steps)
        return None if place is None else (place[0], c, place[1], y)

    return send(value, move)


def send_cells(value, steps):
    return send(value, lambda x, c, z, y: (x, c, z, y + steps) if 0 <= y + steps < 4 else None)


def shape(*sizes):
    return jax.ShapeDtypeStruct(sizes, F32)


def region(rows, cells):
    return shape(rows, 2, cells, 128)


BLOCK = region(ROWS, CELLS)
NEAR = region(ROWS + 8, SPAN)
WIDE = region(ROWS + 16, SPAN)


def call(body, outs, n_smem, operands, scratch=()):
    specs = [pl.BlockSpec(memory_space=pltpu.SMEM)] * n_smem
    specs += [pl.BlockSpec(memory_space=pltpu.VMEM)] * (len(operands) - n_smem)
    return pl.pallas_call(
        body,
        out_shape=tuple(outs),
        in_specs=specs,
        out_specs=tuple(pl.BlockSpec(memory_space=pltpu.VMEM) for _ in outs),
        scratch_shapes=[pltpu.VMEM(s.shape, s.dtype) for s in scratch],
        compiler_params=pltpu.CompilerParams(vmem_limit_bytes=LIMIT),
    )(*operands)


def lanes():
    return lax.broadcasted_iota(jnp.int32, (8, 128), 1)


class Stencil:
    def __init__(self, source, row, cell, lane):
        self.source, self.row, self.cell, self.lane = source, row, cell, lane
        self.center = [self.load(0, 0, half) for half in (0, 1)]
        low, high = self.center
        self.deep = []
        for reach in range(1, 5):
            ahead = [pltpu.roll(v, 128 - reach, 1) for v in (low, high)]
            behind = [pltpu.roll(v, reach, 1) for v in (low, high)]
            front = lane < 128 - reach
            back = lane >= reach
            self.deep.append(
                (
                    (jnp.where(front, ahead[0], ahead[1]), jnp.where(front, ahead[1], 0.0)),
                    (jnp.where(back, behind[0], 0.0), jnp.where(back, behind[1], behind[0])),
                )
            )

    def load(self, rows, cells, half):
        first = self.cell + cells
        return self.source[self.row + rows, half, first : first + 8, :]

    def both(self, direction, reach, half):
        if direction == 0:
            return self.load(reach, 0, half), self.load(-reach, 0, half)
        if direction == 1:
            return self.load(0, reach, half), self.load(0, -reach, half)
        ahead, behind = self.deep[reach - 1]
        return ahead[half], behind[half]

    def derivative(self, direction, half):
        ahead, behind = self.both(direction, 1, half)
        total = ahead - behind
        for reach in range(2, 5):
            ahead, behind = self.both(direction, reach, half)
            total = total + (diff_coeffs[reach - 1] / diff_coeffs[0]) * (ahead - behind)
        return total

    def advanced(self, half, previous, speed_sq, slopes):
        center = self.center[half]
        lap = (3.0 * lap_coeffs[0] / lap_coeffs[1]) * center
        derived = [None, None, None]
        for reach in range(1, 5):
            around = None
            for direction in range(3):
                ahead, behind = self.both(direction, reach, half)
                pair = ahead + behind
                around = pair if around is None else around + pair
                part = ahead - behind
                if reach > 1:
                    part = derived[direction] + (diff_coeffs[reach - 1] / diff_coeffs[0]) * part
                derived[direction] = part
            if reach > 1:
                around = (lap_coeffs[reach] / lap_coeffs[1]) * around
            lap = lap + around
        result = 2.0 * center - previous + speed_sq * lap
        for direction in range(3):
            result = result - slopes[direction] * derived[direction]
        return result


def row_pairs(visit, first, last, cells):
    def step(pair, carry):
        for row in (first + 2 * pair, first + 2 * pair + 1):
            for cell in cells:
                visit(row, cell)
        return carry

    lax.fori_loop(0, (last - first) // 2, step, 0)


def over_block(visit):
    row_pairs(visit, 0, ROWS, range(0, CELLS, 8))


def over_near(visit):
    sides, middle = range(8, 8 + CELLS, 8), range(4, 12 + CELLS, 8)
    row_pairs(visit, 0, 4, sides)
    row_pairs(visit, 4, 4 + ROWS, middle)
    row_pairs(visit, 4 + ROWS, 8 + ROWS, sides)


def add_source(place, amount, first, target):
    @pl.when(place[first] > 0)
    def _():
        row, half = place[first + 1], place[first + 2]
        values = target[row, half]
        cell = lax.broadcasted_iota(jnp.int32, values.shape, 0)
        lane = lax.broadcasted_iota(jnp.int32, values.shape, 1)
        hit = (cell == place[first + 3]) & (lane == place[first + 4])
        target[row, half] = values + jnp.where(hit, amount, 0.0)


def near_step(source, old, model, lane, out, extra=None):
    speed_sq, slopes = model[0], model[1:]

    def visit(row, cell):
        stencil = Stencil(source, row + 4, cell, lane)
        cut = slice(cell, cell + 8)
        for half in (0, 1):
            value = stencil.advanced(
                half,
                old[row, half, cut, :],
                speed_sq[row, half, cut, :],
                [s[row, half, cut, :] for s in slopes],
            )
            if extra is not None:
                value = value + extra(row, half, cut)
            out[row, half, cut, :] = value

    over_near(visit)


def block_step(source, old, model, lane, finish):
    speed_sq, slopes = model[0], model[1:]

    def visit(row, cell):
        stencil = Stencil(source, row + 4, cell + 8, lane)
        near = slice(cell + 8, cell + 16)
        for half in (0, 1):
            value = stencil.advanced(
                half,
                old(row, half, slice(cell, cell + 8)),
                speed_sq[row + 4, half, near, :],
                [s[row + 4, half, near, :] for s in slopes],
            )
            finish(row, half, slice(cell, cell + 8), value)

    over_block(visit)


def of_block(ref):
    return lambda row, half, cut: ref[row, half, cut, :]


def of_near(ref):
    return lambda row, half, cut: ref[row + 4, half, cut.start + 8 : cut.stop + 8, :]


def of_wide(ref):
    return lambda row, half, cut: ref[row + 8, half, cut.start + 8 : cut.stop + 8, :]


def injected(maps, index, field):
    def near(row, half, cut):
        hits = maps[row, half, cut, 0:128]
        seen = maps[row, half, cut, 128 * index : 128 * index + 128]
        return hits * field[row, half, cut, :] - seen

    return near


def fill_wide(wide, block, halo):
    below, above, left, right, left_corners, right_corners = halo
    wide[0:8, :, 8 : 8 + CELLS, :] = below[...]
    wide[8 : 8 + ROWS, :, 8 : 8 + CELLS, :] = block[...]
    wide[8 + ROWS : 16 + ROWS, :, 8 : 8 + CELLS, :] = above[...]
    for cells, side, corners in (
        (slice(0, 8), left, left_corners),
        (slice(8 + CELLS, SPAN), right, right_corners),
    ):
        wide[4:8, :, cells, :] = corners[0:4]
        wide[8 : 8 + ROWS, :, cells, :] = side[...]
        wide[8 + ROWS : 12 + ROWS, :, cells, :] = corners[4:8]


WIDE_EDGES = [region(8, CELLS)] * 2 + [region(ROWS, 8)] * 2


def write_wide_edges(block, edges):
    low, high, low_cells, high_cells = edges
    low[...] = block[0:8]
    high[...] = block[ROWS - 8 : ROWS]
    low_cells[...] = block[:, :, 0:8, :]
    high_cells[...] = block[:, :, CELLS - 8 : CELLS, :]


def rim_body(below, above, low, high):
    for out, cut in ((low, slice(0, 8)), (high, slice(CELLS - 8, CELLS))):
        out[0:4] = below[4:8, :, cut, :]
        out[4:8] = above[0:4, :, cut, :]


def swap_wide_edges(edges):
    low, high, low_cells, high_cells = edges
    below, above = send_group(high, 1), send_group(low, -1)
    left, right = send_cells(high_cells, 1), send_cells(low_cells, -1)
    low_corners, high_corners = call(rim_body, [region(8, 8)] * 2, 0, (below, above))
    return below, above, left, right, send_cells(high_corners, 1), send_cells(low_corners, -1)


def cut_body(chunks, *refs, margins):
    count = len(margins)
    slabs, pieces = refs[:count], refs[count:]
    for turn in range(4):
        chunk = chunks[turn]
        first = pl.multiple_of(chunk * CELLS, CELLS)
        before = pl.multiple_of(jnp.maximum(first - 8, 0), 8)
        after = pl.multiple_of(jnp.minimum(first + CELLS, NY - 8), 8)
        at = 0
        for slab, margin in zip(slabs, margins):
            if margin:
                pieces[turn][:, at : at + 8, :] = jnp.where(chunk > 0, slab[:, pl.ds(before, 8), :], 0.0)
                at += 8
            pieces[turn][:, at : at + CELLS, :] = slab[:, pl.ds(first, CELLS), :]
            at += CELLS
            if margin:
                pieces[turn][:, at : at + 8, :] = jnp.where(chunk < 3, slab[:, pl.ds(after, 8), :], 0.0)
                at += 8


def cut_pieces(slabs, margins, chunks):
    width = sum(SPAN if margin else CELLS for margin in margins)
    pieces = call(functools.partial(cut_body, margins=margins), [shape(4, width, NZ)] * 4, 1, (chunks, *slabs))
    return pieces


def place_pieces(slots, pieces, outs):
    for turn in range(4):
        slot = pl.multiple_of(slots[turn] * 4, 4)
        at = 0
        for out in outs:
            width = out.shape[2]
            for half in (0, 1):
                out[pl.ds(slot, 4), half] = pieces[turn][:, at : at + width, 128 * half : 128 * half + 128]
            at += width


def gather_body(slots, *refs, depths):
    pieces, outs = refs[:4], refs[4:]
    low, high = outs[-2:]
    place_pieces(slots, pieces, outs[:-2])
    at = 0
    core = slice(8, 8 + CELLS)
    for out, depth in zip(outs, depths):
        if depth == 8:
            low[:, :, at : at + SPAN, :] = out[0:4]
            high[:, :, at : at + SPAN, :] = out[ROWS - 4 : ROWS]
            at += SPAN
            low[:, :, at : at + CELLS, :] = out[4:8, :, core, :]
            high[:, :, at : at + CELLS, :] = out[ROWS - 8 : ROWS - 4, :, core, :]
            at += CELLS
        elif depth == 4:
            low[:, :, at : at + CELLS, :] = out[0:4, :, core, :]
            high[:, :, at : at + CELLS, :] = out[ROWS - 4 : ROWS, :, core, :]
            at += CELLS


def gather_blocks(pieces, slots, depths):
    outs = [region(ROWS, SPAN if depth else CELLS) for depth in depths]
    packed = sum({8: SPAN + CELLS, 4: CELLS, 0: 0}[depth] for depth in depths)
    outs += [region(4, packed)] * 2
    return call(functools.partial(gather_body, depths=depths), outs, 1, (slots, *pieces))


def stack_wide(out, below, middle, above, at):
    core = slice(8, 8 + CELLS)
    end = at + SPAN + CELLS
    out[0:4, :, core, :] = below[:, :, at + SPAN : end, :]
    out[4:8] = below[:, :, at : at + SPAN, :]
    out[8 : 8 + ROWS] = middle[...]
    out[8 + ROWS : 12 + ROWS] = above[:, :, at : at + SPAN, :]
    out[12 + ROWS : 16 + ROWS, :, core, :] = above[:, :, at + SPAN : end, :]


def stack_near(out, below, middle, above, at):
    core = slice(8, 8 + CELLS)
    out[0:4, :, core, :] = below[:, :, at : at + CELLS, :]
    out[4 : 4 + ROWS] = middle[...]
    out[4 + ROWS : 8 + ROWS, :, core, :] = above[:, :, at : at + CELLS, :]


def fields_body(now, old, adjoint, below, above, wide, old_near, adjoint_near):
    stack_wide(wide, below, now, above, 0)
    stack_near(old_near, below, old, above, SPAN + CELLS)
    stack_near(adjoint_near, below, adjoint, above, SPAN + 2 * CELLS)


def model_body(log_mass, speed, below, above, speed_sq, s0, s1, s2, twice, wide, speed_near):
    stack_wide(wide, below, log_mass, above, 0)
    stack_near(speed_near, below, speed, above, SPAN + CELLS)
    twice[...] = 2.0 / speed[:, :, 8 : 8 + CELLS, :]
    lane = lanes()

    def visit(row, cell):
        stencil = Stencil(wide, row + 4, cell, lane)
        cut = slice(cell, cell + 8)
        for half in (0, 1):
            value = speed_near[row, half, cut, :]
            scale = time_step_sq * value * value
            speed_sq[row, half, cut, :] = lap_coeffs[1] * scale
            scale = (diff_coeffs[0] * diff_coeffs[0]) * scale
            for direction, out in enumerate((s0, s1, s2)):
                out[row, half, cut, :] = scale * stencil.derivative(direction, half)

    over_near(visit)


def forward_body(place, amount, wide, old, speed_sq, s0, s1, s2, near, new, *edges):
    model = (speed_sq, s0, s1, s2)
    lane = lanes()
    near_step(wide, old, model, lane, near)
    add_source(place, amount[0], 0, near)

    def finish(row, half, cut, value):
        new[row, half, cut, :] = value

    block_step(near, of_wide(wide), model, lane, finish)
    add_source(place, amount[1], 5, new)
    write_wide_edges(new, edges)


def write_pieces(slots, block, pieces, at):
    for turn in range(4):
        slot = pl.multiple_of(slots[turn] * 4, 4)
        for half in (0, 1):
            pieces[turn][:, at : at + CELLS, 128 * half : 128 * half + 128] = block[pl.ds(slot, 4), half]


def turn_body(place, amount, block, *refs):
    halo, refs = refs[:6], refs[6:]
    old, speed_sq, s0, s1, s2, adjoint, later, maps, near, new, adjoint_new, summed = refs[:12]
    edges, wide = refs[12:16], refs[16]
    model = (speed_sq, s0, s1, s2)
    lane = lanes()
    fill_wide(wide, block, halo)
    near_step(wide, old, model, lane, near)
    add_source(place, amount[2], 0, near)

    def finish(row, half, cut, value):
        new[row, half, cut, :] = value

    block_step(near, of_block(block), model, lane, finish)
    add_source(place, amount[3], 5, new)

    def finish_adjoint(row, half, cut, value):
        hits = of_near(maps)(row, half, cut)
        ahead = new[row, half, cut, :]
        value = value + (hits[:, 0:128] * ahead - hits[:, 4 * 128 : 5 * 128])
        adjoint_new[row, half, cut, :] = value
        summed[row, half, cut, :] = value * (
            ahead - 2.0 * of_near(near)(row, half, cut) + block[row, half, cut, :]
        )

    block_step(adjoint, of_block(later), model, lane, finish_adjoint)
    write_wide_edges(adjoint_new, edges)


def adjoint_body(block, *refs):
    halo, refs = refs[:6], refs[6:]
    old, speed_sq, s0, s1, s2, maps, u3, u2, u1, u0, sums = refs[:11]
    near, new, summed, low, high, low_cells, high_cells, wide = refs[11:]
    model = (speed_sq, s0, s1, s2)
    lane = lanes()
    fill_wide(wide, block, halo)
    near_step(wide, old, model, lane, near, injected(maps, 3, u3))

    def finish(row, half, cut, value):
        hits = of_near(maps)(row, half, cut)
        third = of_near(u3)(row, half, cut)
        second = u2[row, half, cut, :]
        first = of_near(u1)(row, half, cut)
        zeroth = of_wide(u0)(row, half, cut)
        value = value + (hits[:, 0:128] * second - hits[:, 2 * 128 : 3 * 128])
        new[row, half, cut, :] = value
        total = sums[row, half, cut, :]
        total = total + of_near(near)(row, half, cut) * (third - 2.0 * second + first)
        summed[row, half, cut, :] = total + value * (second - 2.0 * first + zeroth)

    block_step(near, of_block(block), model, lane, finish)
    low[...] = new[0:4]
    high[...] = new[ROWS - 4 : ROWS]
    low_cells[...] = new[:, :, 0:8, :]
    high_cells[...] = new[:, :, CELLS - 8 : CELLS, :]


def last_body(
    slots, model_slots, block, below, above, left, right, old, speed_sq, s0, s1, s2, maps,
    u1, u0, u_before, sums, twice, u4, p0, p1, p2, p3, q0, q1, q2, q3, near, new, image,
):
    near[0:4, :, 8 : 8 + CELLS, :] = below[...]
    near[4 : 4 + ROWS, :, 8 : 8 + CELLS, :] = block[...]
    near[4 + ROWS : 8 + ROWS, :, 8 : 8 + CELLS, :] = above[...]
    near[4 : 4 + ROWS, :, 0:8, :] = left[...]
    near[4 : 4 + ROWS, :, 8 + CELLS : SPAN, :] = right[...]
    lane = lanes()

    def finish(row, half, cut, value):
        hits = of_near(maps)(row, half, cut)
        first = of_near(u1)(row, half, cut)
        value = value + (hits[:, 0:128] * first - hits[:, 128:256])
        new[row, half, cut, :] = value
        curvature = first - 2.0 * of_wide(u0)(row, half, cut) + of_near(u_before)(row, half, cut)
        image[row, half, cut, :] = twice[row, half, cut, :] * (sums[row, half, cut, :] + value * curvature)

    block_step(near, of_near(old), (speed_sq, s0, s1, s2), lane, finish)
    write_pieces(model_slots, image, (p0, p1, p2, p3), 0)
    write_pieces(slots, new, (q0, q1, q2, q3), 0)
    write_pieces(slots, u4, (q0, q1, q2, q3), CELLS)


def spread_body(chunks, p0, p1, p2, p3, *outs):
    for turn, piece in enumerate((p0, p1, p2, p3)):
        first = pl.multiple_of(chunks[turn] * CELLS, CELLS)
        for index, out in enumerate(outs):
            out[:, pl.ds(first, CELLS), :] = piece[:, CELLS * index : CELLS * index + CELLS, :]


def sent_pieces(pieces):
    return [pieces[0]] + [send_y(pieces[turn], turn) for turn in (1, 2, 3)]


def to_slabs(pieces, chunks, count):
    return call(spread_body, [shape(4, NY, NZ)] * count, 1, (chunks, *pieces))


def on_device(
    velocity,
    density,
    aperture_start,
    source_cell,
    receiver_cells,
    wavelet,
    observed,
    forward_old,
    forward_now,
    adjoint_later,
    adjoint_now,
):
    shot = lax.axis_index("shot")
    sub = lax.axis_index("sub")
    core = shot % 2
    x_hi = sub // 16
    x = 2 * x_hi + shot // 2
    z = (sub // 4) % 4
    y = sub % 4
    group = sub // 4
    start = aperture_start[0]
    partner = send_core(aperture_start)

    def wanted(first_slab):
        upper = first_slab // 4 + (y < first_slab % 4).astype(jnp.int32)
        block = jnp.clip(x_hi + (upper - z + 3) // 4, 0, 7)
        position = 2 * (block % 2) + block // 4
        return (block // 2) % 2, (position - x) % 4, upper % 4

    own_core, own_step, turn_by = wanted(start)
    turns = jnp.arange(4, dtype=jnp.int32)
    chunks_out = (y + turns) % 4
    chunks_in = (y - turns) % 4
    slots_in = (y - turns - start % 4) % 4
    slots_out = (y + turns - start % 4) % 4

    pieces = cut_pieces(
        [forward_now[0], forward_old[0], adjoint_now[0], adjoint_later[0]],
        (True, True, True, False),
        chunks_out,
    )
    velocity, partner, *pieces = lax.optimization_barrier((velocity, partner, *pieces))
    pair_core, pair_step, _ = wanted(partner[0])

    def gathered(slab):
        from_below = send_x(slab, 1)
        from_above = send_x(slab, -1)
        far = jnp.concatenate([send_x(from_below[0:2], 1), send_x(from_above[2:4], -1)])

        def pick(step):
            return jnp.where(
                step < 2, jnp.where(step == 0, slab, from_above), jnp.where(step == 2, far, from_below)
            )

        other = send_core(pick(pair_step))
        return jnp.where(own_core == core, pick(own_step), other)

    def turned(arrays, steps):
        def branch(count):
            return lambda *values: tuple(send_z(value, count) if count else value for value in values)

        return lax.switch(steps, [branch(count) for count in (0, 1, 2, -1)], *arrays)

    log_slab = gathered(jnp.log(density))
    speed_slab = gathered(velocity)
    pieces = sent_pieces(pieces)

    def local_place(cells, rows_more, cells_more):
        rows = cells // (NY * NZ) - group * ROWS + rows_more
        columns = (cells // NZ) % NY - y * CELLS + cells_more
        inside = (rows >= 0) & (rows < ROWS + 2 * rows_more)
        inside = inside & (columns >= 0) & (columns < CELLS + 2 * cells_more)
        return inside, rows, (cells // 128) % 2, columns, cells % 128

    inside, rows, half, columns, lane = local_place(receiver_cells[0], 4, 8)
    line = jnp.where(inside, (rows * 2 + half) * SPAN + columns, -1)
    lines = (ROWS + 8) * 2 * SPAN
    on_line = (jnp.arange(lines, dtype=jnp.int32)[:, None] == line[None, :]).astype(F32)
    weights = jnp.concatenate([jnp.ones_like(observed[0, :1]), observed[0]])
    hit = lane[:, None, None] == jnp.arange(128, dtype=jnp.int32)[None, None, :]
    at_lane = jnp.where(hit, weights.T[:, :, None], 0.0).reshape(-1, 5 * 128)
    maps = jnp.dot(on_line, at_lane, precision=lax.Precision.HIGHEST)
    maps = maps.reshape(ROWS + 8, 2, SPAN, 5 * 128)

    def source_place(rows_more, cells_more):
        inside, rows, half, columns, lane = local_place(source_cell[0], rows_more, cells_more)
        rows = jnp.clip(rows, 0, ROWS + 2 * rows_more - 1)
        return [inside.astype(jnp.int32), rows, half, columns, lane]

    place = jnp.stack(source_place(4, 8) + source_place(0, 0))
    amount = wavelet[0]

    log_slab, speed_slab = lax.optimization_barrier((log_slab, speed_slab))
    log_slab, speed_slab = turned((log_slab, speed_slab), (4 - turn_by) % 4)
    log_slab, speed_slab, *pieces = lax.optimization_barrier((log_slab, speed_slab, *pieces))
    model_pieces = sent_pieces(cut_pieces([log_slab, speed_slab], (True, True), chunks_out))
    now, old, adjoint, a_later, side_low, side_high = gather_blocks(pieces, chunks_in, (8, 4, 4, 0))
    below, above = send_group(side_high, 1), send_group(side_low, -1)
    u_wide, old_near, a_near = call(
        fields_body, [WIDE, NEAR, NEAR], 0, (now, old, adjoint, below, above)
    )
    log_mass, speed, side_low, side_high = gather_blocks(model_pieces, slots_in, (8, 4))
    below, above = send_group(side_high, 1), send_group(side_low, -1)
    below, above, maps = lax.optimization_barrier((below, above, maps))
    *model, twice = call(
        model_body, [NEAR] * 4 + [BLOCK], 0, (log_mass, speed, below, above), (WIDE, NEAR)
    )

    u1, u2, *edges = call(
        forward_body, [NEAR, BLOCK] + WIDE_EDGES, 2, (place, amount, u_wide, old_near, *model)
    )
    halo = swap_wide_edges(edges)
    u3, u4, a3, sums, *edges = call(
        turn_body,
        [NEAR, BLOCK, BLOCK, BLOCK] + WIDE_EDGES,
        2,
        (place, amount, u2, *halo, u1, *model, a_near, a_later, maps),
        (WIDE,),
    )
    halo = swap_wide_edges(edges)
    a2, a1, sums, side_low, side_high, low_cells, high_cells = call(
        adjoint_body,
        [NEAR, BLOCK, BLOCK] + [region(4, CELLS)] * 2 + [region(ROWS, 8)] * 2,
        0,
        (a3, *halo, a_near, *model, maps, u3, u2, u1, u_wide, sums),
        (WIDE,),
    )
    halo = (
        send_group(side_high, 1),
        send_group(side_low, -1),
        send_cells(high_cells, 1),
        send_cells(low_cells, -1),
    )
    pieces = call(
        last_body,
        [shape(4, CELLS, NZ)] * 4 + [shape(4, 2 * CELLS, NZ)] * 4,
        2,
        (chunks_out, slots_out, a1, *halo, a2, *model, maps, u1, u_wide, old_near, sums, twice, u4),
        (NEAR, BLOCK, BLOCK),
    )
    (image,) = to_slabs(sent_pieces(pieces[:4]), chunks_in, 1)

    def both(first_half, second_half):
        return jnp.concatenate([first_half, second_half])

    (image,) = turned((image,), turn_by)
    image, *pieces = lax.optimization_barrier((image, *pieces[4:]))
    adjoint_first, forward_last = to_slabs(sent_pieces(pieces), chunks_in, 2)
    other = send_core(image)

    def share(step):
        mine = jnp.where((own_core == core) & (own_step == step), image, 0.0)
        return mine + jnp.where((pair_core == core) & (pair_step == step), other, 0.0)

    far = share(2)
    passing_up = send_x(far[0:2], 1)
    passing_down = send_x(far[2:4], -1)
    up = share(1)
    down = share(3)
    up = send_x(both(up[0:2] + passing_up, up[2:4]), 1)
    down = send_x(both(down[0:2], down[2:4] + passing_down), -1)
    gradient = share(0) + up + down
    return (gradient, forward_last[None], adjoint_first[None])


def solution(mesh):
    placed = (
        P(("shot", "sub"), None, None),
        P(("shot", "sub"), None, None),
        P("shot"),
        P("shot"),
        P("shot", None),
        P("shot", None),
        P("shot", None, None),
        P("shot", "sub", None, None),
        P("shot", "sub", None, None),
        P("shot", "sub", None, None),
        P("shot", "sub", None, None),
    )
    return jax.shard_map(
        on_device,
        mesh=mesh,
        in_specs=placed,
        out_specs=(
            P(("shot", "sub"), None, None),
            P("shot", "sub", None, None),
            P("shot", "sub", None, None),
        ),
        check_vma=False,
    )
```

```python
import functools

import jax
import jax.numpy as jnp
from jax import lax
from jax.experimental import pallas as pl
from jax.experimental.pallas import tpu as pltpu
from jax.sharding import PartitionSpec as P

lap_coeffs = (-205.0 / 72.0, 8.0 / 5.0, -1.0 / 5.0, 8.0 / 315.0, -1.0 / 560.0)
diff_coeffs = (4.0 / 5.0, -1.0 / 5.0, 4.0 / 105.0, -1.0 / 280.0)
time_step_sq = 0.0088

ROWS = 16
CELLS = 32
SPAN = CELLS + 16
NY = 128
NZ = 256
F32 = jnp.float32
LIMIT = 24 * 2**20


def pairs_by(move):
    pairs = []
    for shot in range(4):
        for sub in range(32):
            x = 2 * (sub // 16) + shot // 2
            target = move(x, shot % 2, (sub // 4) % 4, sub % 4)
            if target is None:
                continue
            tx, tcore, tz, ty = target
            pairs.append((shot * 32 + sub, ((tx % 2) * 2 + tcore) * 32 + (tx // 2) * 16 + tz * 4 + ty))
    return pairs


def send(value, move):
    return lax.ppermute(value, ("shot", "sub"), pairs_by(move))


def send_x(value, steps):
    return send(value, lambda x, c, z, y: ((x + steps) % 4, c, z, y))


def send_core(value):
    return send(value, lambda x, c, z, y: (x, 1 - c, z, y))


def send_z(value, steps):
    return send(value, lambda x, c, z, y: (x, c, (z + steps) % 4, y))


def send_y(value, steps):
    return send(value, lambda x, c, z, y: (x, c, z, (y + steps) % 4))


def next_rows(x, z, steps):
    group = (x // 2) * 4 + z + steps
    if group < 0 or group > 7:
        return None
    return (2 * (group // 4) + x % 2, group % 4)


def send_group(value, steps):
    def move(x, c, z, y):
        place = next_rows(x, z, steps)
        return None if place is None else (place[0], c, place[1], y)

    return send(value, move)


def send_cells(value, steps):
    return send(value, lambda x, c, z, y: (x, c, z, y + steps) if 0 <= y + steps < 4 else None)


def shape(*sizes):
    return jax.ShapeDtypeStruct(sizes, F32)


def region(rows, cells):
    return shape(rows, 2, cells, 128)


BLOCK = region(ROWS, CELLS)
NEAR = region(ROWS + 8, SPAN)
WIDE = region(ROWS + 16, SPAN)


def call(body, outs, n_smem, operands, scratch=()):
    specs = [pl.BlockSpec(memory_space=pltpu.SMEM)] * n_smem
    specs += [pl.BlockSpec(memory_space=pltpu.VMEM)] * (len(operands) - n_smem)
    return pl.pallas_call(
        body,
        out_shape=tuple(outs),
        in_specs=specs,
        out_specs=tuple(pl.BlockSpec(memory_space=pltpu.VMEM) for _ in outs),
        scratch_shapes=[pltpu.VMEM(s.shape, s.dtype) for s in scratch],
        compiler_params=pltpu.CompilerParams(vmem_limit_bytes=LIMIT),
    )(*operands)


def lanes():
    return lax.broadcasted_iota(jnp.int32, (8, 128), 1)


class Stencil:
    def __init__(self, source, row, cell, lane):
        self.source, self.row, self.cell, self.lane = source, row, cell, lane
        self.center = [self.load(0, 0, half) for half in (0, 1)]
        low, high = self.center
        self.deep = []
        for reach in range(1, 5):
            ahead = [pltpu.roll(v, 128 - reach, 1) for v in (low, high)]
            behind = [pltpu.roll(v, reach, 1) for v in (low, high)]
            front = lane < 128 - reach
            back = lane >= reach
            self.deep.append(
                (
                    (jnp.where(front, ahead[0], ahead[1]), jnp.where(front, ahead[1], 0.0)),
                    (jnp.where(back, behind[0], 0.0), jnp.where(back, behind[1], behind[0])),
                )
            )

    def load(self, rows, cells, half):
        first = self.cell + cells
        return self.source[self.row + rows, half, first : first + 8, :]

    def both(self, direction, reach, half):
        if direction == 0:
            return self.load(reach, 0, half), self.load(-reach, 0, half)
        if direction == 1:
            return self.load(0, reach, half), self.load(0, -reach, half)
        ahead, behind = self.deep[reach - 1]
        return ahead[half], behind[half]

    def derivative(self, direction, half):
        ahead, behind = self.both(direction, 1, half)
        total = ahead - behind
        for reach in range(2, 5):
            ahead, behind = self.both(direction, reach, half)
            total = total + (diff_coeffs[reach - 1] / diff_coeffs[0]) * (ahead - behind)
        return total

    def advanced(self, half, previous, speed_sq, slopes):
        center = self.center[half]
        lap = (3.0 * lap_coeffs[0] / lap_coeffs[1]) * center
        derived = [None, None, None]
        for reach in range(1, 5):
            around = None
            for direction in range(3):
                ahead, behind = self.both(direction, reach, half)
                pair = ahead + behind
                around = pair if around is None else around + pair
                part = ahead - behind
                if reach > 1:
                    part = derived[direction] + (diff_coeffs[reach - 1] / diff_coeffs[0]) * part
                derived[direction] = part
            if reach > 1:
                around = (lap_coeffs[reach] / lap_coeffs[1]) * around
            lap = lap + around
        result = 2.0 * center - previous + speed_sq * lap
        for direction in range(3):
            result = result - slopes[direction] * derived[direction]
        return result


def row_pairs(visit, first, last, cells):
    def step(pair, carry):
        for row in (first + 2 * pair, first + 2 * pair + 1):
            for cell in cells:
                visit(row, cell)
        return carry

    lax.fori_loop(0, (last - first) // 2, step, 0)


def over_block(visit):
    row_pairs(visit, 0, ROWS, range(0, CELLS, 8))


def over_near(visit):
    sides, middle = range(8, 8 + CELLS, 8), range(4, 12 + CELLS, 8)
    row_pairs(visit, 0, 4, sides)
    row_pairs(visit, 4, 4 + ROWS, middle)
    row_pairs(visit, 4 + ROWS, 8 + ROWS, sides)


def add_source(place, amount, first, target):
    @pl.when(place[first] > 0)
    def _():
        row, half = place[first + 1], place[first + 2]
        values = target[row, half]
        cell = lax.broadcasted_iota(jnp.int32, values.shape, 0)
        lane = lax.broadcasted_iota(jnp.int32, values.shape, 1)
        hit = (cell == place[first + 3]) & (lane == place[first + 4])
        target[row, half] = values + jnp.where(hit, amount, 0.0)


def near_step(source, old, model, lane, out, extra=None):
    speed_sq, slopes = model[0], model[1:]

    def visit(row, cell):
        stencil = Stencil(source, row + 4, cell, lane)
        cut = slice(cell, cell + 8)
        for half in (0, 1):
            value = stencil.advanced(
                half,
                old[row, half, cut, :],
                speed_sq[row, half, cut, :],
                [s[row, half, cut, :] for s in slopes],
            )
            if extra is not None:
                value = value + extra(row, half, cut)
            out[row, half, cut, :] = value

    over_near(visit)


def block_step(source, old, model, lane, finish):
    speed_sq, slopes = model[0], model[1:]

    def visit(row, cell):
        stencil = Stencil(source, row + 4, cell + 8, lane)
        near = slice(cell + 8, cell + 16)
        for half in (0, 1):
            value = stencil.advanced(
                half,
                old(row, half, slice(cell, cell + 8)),
                speed_sq[row + 4, half, near, :],
                [s[row + 4, half, near, :] for s in slopes],
            )
            finish(row, half, slice(cell, cell + 8), value)

    over_block(visit)


def of_block(ref):
    return lambda row, half, cut: ref[row, half, cut, :]


def of_near(ref):
    return lambda row, half, cut: ref[row + 4, half, cut.start + 8 : cut.stop + 8, :]


def of_wide(ref):
    return lambda row, half, cut: ref[row + 8, half, cut.start + 8 : cut.stop + 8, :]


def injected(maps, index, field):
    def near(row, half, cut):
        hits = maps[row, half, cut, 0:128]
        seen = maps[row, half, cut, 128 * index : 128 * index + 128]
        return hits * field[row, half, cut, :] - seen

    return near


def fill_wide(wide, block, halo):
    below, above, left, right, left_corners, right_corners = halo
    wide[0:8, :, 8 : 8 + CELLS, :] = below[...]
    wide[8 : 8 + ROWS, :, 8 : 8 + CELLS, :] = block[...]
    wide[8 + ROWS : 16 + ROWS, :, 8 : 8 + CELLS, :] = above[...]
    for cells, side, corners in (
        (slice(0, 8), left, left_corners),
        (slice(8 + CELLS, SPAN), right, right_corners),
    ):
        wide[4:8, :, cells, :] = corners[0:4]
        wide[8 : 8 + ROWS, :, cells, :] = side[...]
        wide[8 + ROWS : 12 + ROWS, :, cells, :] = corners[4:8]


WIDE_EDGES = [region(8, CELLS)] * 2 + [region(ROWS, 8)] * 2


def write_wide_edges(block, edges):
    low, high, low_cells, high_cells = edges
    low[...] = block[0:8]
    high[...] = block[ROWS - 8 : ROWS]
    low_cells[...] = block[:, :, 0:8, :]
    high_cells[...] = block[:, :, CELLS - 8 : CELLS, :]


def rim_body(below, above, low, high):
    for out, cut in ((low, slice(0, 8)), (high, slice(CELLS - 8, CELLS))):
        out[0:4] = below[4:8, :, cut, :]
        out[4:8] = above[0:4, :, cut, :]


def swap_wide_edges(edges):
    low, high, low_cells, high_cells = edges
    below, above = send_group(high, 1), send_group(low, -1)
    left, right = send_cells(high_cells, 1), send_cells(low_cells, -1)
    low_corners, high_corners = call(rim_body, [region(8, 8)] * 2, 0, (below, above))
    return below, above, left, right, send_cells(high_corners, 1), send_cells(low_corners, -1)


def cut_body(chunks, *refs, margins):
    count = len(margins)
    slabs, pieces = refs[:count], refs[count:]
    for turn in range(4):
        chunk = chunks[turn]
        first = pl.multiple_of(chunk * CELLS, CELLS)
        before = pl.multiple_of(jnp.maximum(first - 8, 0), 8)
        after = pl.multiple_of(jnp.minimum(first + CELLS, NY - 8), 8)
        at = 0
        for slab, margin in zip(slabs, margins):
            if margin:
                pieces[turn][:, at : at + 8, :] = jnp.where(chunk > 0, slab[:, pl.ds(before, 8), :], 0.0)
                at += 8
            pieces[turn][:, at : at + CELLS, :] = slab[:, pl.ds(first, CELLS), :]
            at += CELLS
            if margin:
                pieces[turn][:, at : at + 8, :] = jnp.where(chunk < 3, slab[:, pl.ds(after, 8), :], 0.0)
                at += 8


def cut_pieces(slabs, margins, chunks):
    width = sum(SPAN if margin else CELLS for margin in margins)
    pieces = call(functools.partial(cut_body, margins=margins), [shape(4, width, NZ)] * 4, 1, (chunks, *slabs))
    return pieces


def place_pieces(slots, pieces, outs):
    for turn in range(4):
        slot = pl.multiple_of(slots[turn] * 4, 4)
        at = 0
        for out in outs:
            width = out.shape[2]
            for half in (0, 1):
                out[pl.ds(slot, 4), half] = pieces[turn][:, at : at + width, 128 * half : 128 * half + 128]
            at += width


def gather_body(slots, *refs, depths):
    pieces, outs = refs[:4], refs[4:]
    low, high = outs[-2:]
    place_pieces(slots, pieces, outs[:-2])
    at = 0
    core = slice(8, 8 + CELLS)
    for out, depth in zip(outs, depths):
        if depth == 8:
            low[:, :, at : at + SPAN, :] = out[0:4]
            high[:, :, at : at + SPAN, :] = out[ROWS - 4 : ROWS]
            at += SPAN
            low[:, :, at : at + CELLS, :] = out[4:8, :, core, :]
            high[:, :, at : at + CELLS, :] = out[ROWS - 8 : ROWS - 4, :, core, :]
            at += CELLS
        elif depth == 4:
            low[:, :, at : at + CELLS, :] = out[0:4, :, core, :]
            high[:, :, at : at + CELLS, :] = out[ROWS - 4 : ROWS, :, core, :]
            at += CELLS


def gather_blocks(pieces, slots, depths):
    outs = [region(ROWS, SPAN if depth else CELLS) for depth in depths]
    packed = sum({8: SPAN + CELLS, 4: CELLS, 0: 0}[depth] for depth in depths)
    outs += [region(4, packed)] * 2
    return call(functools.partial(gather_body, depths=depths), outs, 1, (slots, *pieces))


def stack_wide(out, below, middle, above, at):
    core = slice(8, 8 + CELLS)
    end = at + SPAN + CELLS
    out[0:4, :, core, :] = below[:, :, at + SPAN : end, :]
    out[4:8] = below[:, :, at : at + SPAN, :]
    out[8 : 8 + ROWS] = middle[...]
    out[8 + ROWS : 12 + ROWS] = above[:, :, at : at + SPAN, :]
    out[12 + ROWS : 16 + ROWS, :, core, :] = above[:, :, at + SPAN : end, :]


def stack_near(out, below, middle, above, at):
    core = slice(8, 8 + CELLS)
    out[0:4, :, core, :] = below[:, :, at : at + CELLS, :]
    out[4 : 4 + ROWS] = middle[...]
    out[4 + ROWS : 8 + ROWS, :, core, :] = above[:, :, at : at + CELLS, :]


def fields_body(now, old, adjoint, below, above, wide, old_near, adjoint_near):
    stack_wide(wide, below, now, above, 0)
    stack_near(old_near, below, old, above, SPAN + CELLS)
    stack_near(adjoint_near, below, adjoint, above, SPAN + 2 * CELLS)


def model_body(log_mass, speed, below, above, speed_sq, s0, s1, s2, twice, wide, speed_near):
    stack_wide(wide, below, log_mass, above, 0)
    stack_near(speed_near, below, speed, above, SPAN + CELLS)
    twice[...] = 2.0 / speed[:, :, 8 : 8 + CELLS, :]
    lane = lanes()

    def visit(row, cell):
        stencil = Stencil(wide, row + 4, cell, lane)
        cut = slice(cell, cell + 8)
        for half in (0, 1):
            value = speed_near[row, half, cut, :]
            scale = time_step_sq * value * value
            speed_sq[row, half, cut, :] = lap_coeffs[1] * scale
            scale = (diff_coeffs[0] * diff_coeffs[0]) * scale
            for direction, out in enumerate((s0, s1, s2)):
                out[row, half, cut, :] = scale * stencil.derivative(direction, half)

    over_near(visit)


def forward_body(place, amount, wide, old, speed_sq, s0, s1, s2, near, new, *edges):
    model = (speed_sq, s0, s1, s2)
    lane = lanes()
    near_step(wide, old, model, lane, near)
    add_source(place, amount[0], 0, near)

    def finish(row, half, cut, value):
        new[row, half, cut, :] = value

    block_step(near, of_wide(wide), model, lane, finish)
    add_source(place, amount[1], 5, new)
    write_wide_edges(new, edges)


def write_pieces(slots, block, pieces, at):
    for turn in range(4):
        slot = pl.multiple_of(slots[turn] * 4, 4)
        for half in (0, 1):
            pieces[turn][:, at : at + CELLS, 128 * half : 128 * half + 128] = block[pl.ds(slot, 4), half]


def turn_body(place, amount, block, *refs):
    halo, refs = refs[:6], refs[6:]
    old, speed_sq, s0, s1, s2, adjoint, later, maps, near, new, adjoint_new, summed = refs[:12]
    edges, wide = refs[12:16], refs[16]
    model = (speed_sq, s0, s1, s2)
    lane = lanes()
    fill_wide(wide, block, halo)
    near_step(wide, old, model, lane, near)
    add_source(place, amount[2], 0, near)

    def finish(row, half, cut, value):
        new[row, half, cut, :] = value

    block_step(near, of_block(block), model, lane, finish)
    add_source(place, amount[3], 5, new)

    def finish_adjoint(row, half, cut, value):
        hits = of_near(maps)(row, half, cut)
        ahead = new[row, half, cut, :]
        value = value + (hits[:, 0:128] * ahead - hits[:, 4 * 128 : 5 * 128])
        adjoint_new[row, half, cut, :] = value
        summed[row, half, cut, :] = value * (
            ahead - 2.0 * of_near(near)(row, half, cut) + block[row, half, cut, :]
        )

    block_step(adjoint, of_block(later), model, lane, finish_adjoint)
    write_wide_edges(adjoint_new, edges)


def adjoint_body(block, *refs):
    halo, refs = refs[:6], refs[6:]
    old, speed_sq, s0, s1, s2, maps, u3, u2, u1, u0, sums = refs[:11]
    near, new, summed, low, high, low_cells, high_cells, wide = refs[11:]
    model = (speed_sq, s0, s1, s2)
    lane = lanes()
    fill_wide(wide, block, halo)
    near_step(wide, old, model, lane, near, injected(maps, 3, u3))

    def finish(row, half, cut, value):
        hits = of_near(maps)(row, half, cut)
        third = of_near(u3)(row, half, cut)
        second = u2[row, half, cut, :]
        first = of_near(u1)(row, half, cut)
        zeroth = of_wide(u0)(row, half, cut)
        value = value + (hits[:, 0:128] * second - hits[:, 2 * 128 : 3 * 128])
        new[row, half, cut, :] = value
        total = sums[row, half, cut, :]
        total = total + of_near(near)(row, half, cut) * (third - 2.0 * second + first)
        summed[row, half, cut, :] = total + value * (second - 2.0 * first + zeroth)

    block_step(near, of_block(block), model, lane, finish)
    low[...] = new[0:4]
    high[...] = new[ROWS - 4 : ROWS]
    low_cells[...] = new[:, :, 0:8, :]
    high_cells[...] = new[:, :, CELLS - 8 : CELLS, :]


def last_body(
    slots, model_slots, block, below, above, left, right, old, speed_sq, s0, s1, s2, maps,
    u1, u0, u_before, sums, twice, u4, p0, p1, p2, p3, q0, q1, q2, q3, near, new, image,
):
    near[0:4, :, 8 : 8 + CELLS, :] = below[...]
    near[4 : 4 + ROWS, :, 8 : 8 + CELLS, :] = block[...]
    near[4 + ROWS : 8 + ROWS, :, 8 : 8 + CELLS, :] = above[...]
    near[4 : 4 + ROWS, :, 0:8, :] = left[...]
    near[4 : 4 + ROWS, :, 8 + CELLS : SPAN, :] = right[...]
    lane = lanes()

    def finish(row, half, cut, value):
        hits = of_near(maps)(row, half, cut)
        first = of_near(u1)(row, half, cut)
        value = value + (hits[:, 0:128] * first - hits[:, 128:256])
        new[row, half, cut, :] = value
        curvature = first - 2.0 * of_wide(u0)(row, half, cut) + of_near(u_before)(row, half, cut)
        image[row, half, cut, :] = twice[row, half, cut, :] * (sums[row, half, cut, :] + value * curvature)

    block_step(near, of_near(old), (speed_sq, s0, s1, s2), lane, finish)
    write_pieces(model_slots, image, (p0, p1, p2, p3), 0)
    write_pieces(slots, new, (q0, q1, q2, q3), 0)
    write_pieces(slots, u4, (q0, q1, q2, q3), CELLS)


def spread_body(chunks, p0, p1, p2, p3, *outs):
    for turn, piece in enumerate((p0, p1, p2, p3)):
        first = pl.multiple_of(chunks[turn] * CELLS, CELLS)
        for index, out in enumerate(outs):
            out[:, pl.ds(first, CELLS), :] = piece[:, CELLS * index : CELLS * index + CELLS, :]


def sent_pieces(pieces):
    return [pieces[0]] + [send_y(pieces[turn], turn) for turn in (1, 2, 3)]


def to_slabs(pieces, chunks, count):
    return call(spread_body, [shape(4, NY, NZ)] * count, 1, (chunks, *pieces))


def on_device(
    velocity,
    density,
    aperture_start,
    source_cell,
    receiver_cells,
    wavelet,
    observed,
    forward_old,
    forward_now,
    adjoint_later,
    adjoint_now,
):
    shot = lax.axis_index("shot")
    sub = lax.axis_index("sub")
    core = shot % 2
    x_hi = sub // 16
    x = 2 * x_hi + shot // 2
    z = (sub // 4) % 4
    y = sub % 4
    group = sub // 4
    start = aperture_start[0]
    partner = send_core(aperture_start)

    def wanted(first_slab):
        upper = first_slab // 4 + (y < first_slab % 4).astype(jnp.int32)
        block = jnp.clip(x_hi + (upper - z + 3) // 4, 0, 7)
        position = 2 * (block % 2) + block // 4
        return (block // 2) % 2, (position - x) % 4, upper % 4

    own_core, own_step, turn_by = wanted(start)
    turns = jnp.arange(4, dtype=jnp.int32)
    chunks_out = (y + turns) % 4
    chunks_in = (y - turns) % 4
    slots_in = (y - turns - start % 4) % 4
    slots_out = (y + turns - start % 4) % 4

    pieces = cut_pieces(
        [forward_now[0], forward_old[0], adjoint_now[0], adjoint_later[0]],
        (True, True, True, False),
        chunks_out,
    )
    velocity, partner, *pieces = lax.optimization_barrier((velocity, partner, *pieces))
    pair_core, pair_step, _ = wanted(partner[0])

    def gathered(slab):
        from_below = send_x(slab, 1)
        from_above = send_x(slab, -1)
        far = jnp.concatenate([send_x(from_below[0:2], 1), send_x(from_above[2:4], -1)])

        def pick(step):
            return jnp.where(
                step < 2, jnp.where(step == 0, slab, from_above), jnp.where(step == 2, far, from_below)
            )

        other = send_core(pick(pair_step))
        return jnp.where(own_core == core, pick(own_step), other)

    def turned(arrays, steps):
        def branch(count):
            return lambda *values: tuple(send_z(value, count) if count else value for value in values)

        return lax.switch(steps, [branch(count) for count in (0, 1, 2, -1)], *arrays)

    log_slab = gathered(jnp.log(density))
    speed_slab = gathered(velocity)
    pieces = sent_pieces(pieces)

    def local_place(cells, rows_more, cells_more):
        rows = cells // (NY * NZ) - group * ROWS + rows_more
        columns = (cells // NZ) % NY - y * CELLS + cells_more
        inside = (rows >= 0) & (rows < ROWS + 2 * rows_more)
        inside = inside & (columns >= 0) & (columns < CELLS + 2 * cells_more)
        return inside, rows, (cells // 128) % 2, columns, cells % 128

    inside, rows, half, columns, lane = local_place(receiver_cells[0], 4, 8)
    line = jnp.where(inside, (rows * 2 + half) * SPAN + columns, -1)
    lines = (ROWS + 8) * 2 * SPAN
    on_line = (jnp.arange(lines, dtype=jnp.int32)[:, None] == line[None, :]).astype(F32)
    weights = jnp.concatenate([jnp.ones_like(observed[0, :1]), observed[0]])
    hit = lane[:, None, None] == jnp.arange(128, dtype=jnp.int32)[None, None, :]
    at_lane = jnp.where(hit, weights.T[:, :, None], 0.0).reshape(-1, 5 * 128)
    maps = jnp.dot(on_line, at_lane, precision=lax.Precision.HIGHEST)
    maps = maps.reshape(ROWS + 8, 2, SPAN, 5 * 128)

    def source_place(rows_more, cells_more):
        inside, rows, half, columns, lane = local_place(source_cell[0], rows_more, cells_more)
        rows = jnp.clip(rows, 0, ROWS + 2 * rows_more - 1)
        return [inside.astype(jnp.int32), rows, half, columns, lane]

    place = jnp.stack(source_place(4, 8) + source_place(0, 0))
    amount = wavelet[0]

    log_slab, speed_slab = lax.optimization_barrier((log_slab, speed_slab))
    log_slab, speed_slab = turned((log_slab, speed_slab), (4 - turn_by) % 4)
    log_slab, speed_slab, *pieces = lax.optimization_barrier((log_slab, speed_slab, *pieces))
    model_pieces = sent_pieces(cut_pieces([log_slab, speed_slab], (True, True), chunks_out))
    now, old, adjoint, a_later, side_low, side_high = gather_blocks(pieces, chunks_in, (8, 4, 4, 0))
    below, above = send_group(side_high, 1), send_group(side_low, -1)
    u_wide, old_near, a_near = call(
        fields_body, [WIDE, NEAR, NEAR], 0, (now, old, adjoint, below, above)
    )
    log_mass, speed, side_low, side_high = gather_blocks(model_pieces, slots_in, (8, 4))
    below, above = send_group(side_high, 1), send_group(side_low, -1)
    below, above, maps = lax.optimization_barrier((below, above, maps))
    *model, twice = call(
        model_body, [NEAR] * 4 + [BLOCK], 0, (log_mass, speed, below, above), (WIDE, NEAR)
    )

    u1, u2, *edges = call(
        forward_body, [NEAR, BLOCK] + WIDE_EDGES, 2, (place, amount, u_wide, old_near, *model)
    )
    halo = swap_wide_edges(edges)
    u3, u4, a3, sums, *edges = call(
        turn_body,
        [NEAR, BLOCK, BLOCK, BLOCK] + WIDE_EDGES,
        2,
        (place, amount, u2, *halo, u1, *model, a_near, a_later, maps),
        (WIDE,),
    )
    halo = swap_wide_edges(edges)
    a2, a1, sums, side_low, side_high, low_cells, high_cells = call(
        adjoint_body,
        [NEAR, BLOCK, BLOCK] + [region(4, CELLS)] * 2 + [region(ROWS, 8)] * 2,
        0,
        (a3, *halo, a_near, *model, maps, u3, u2, u1, u_wide, sums),
        (WIDE,),
    )
    halo = (
        send_group(side_high, 1),
        send_group(side_low, -1),
        send_cells(high_cells, 1),
        send_cells(low_cells, -1),
    )
    pieces = call(
        last_body,
        [shape(4, CELLS, NZ)] * 4 + [shape(4, 2 * CELLS, NZ)] * 4,
        2,
        (chunks_out, slots_out, a1, *halo, a2, *model, maps, u1, u_wide, old_near, sums, twice, u4),
        (NEAR, BLOCK, BLOCK),
    )
    pieces = lax.optimization_barrier((*sent_pieces(pieces[:4]), *pieces[4:]))
    (image,) = to_slabs(pieces[:4], chunks_in, 1)

    def both(first_half, second_half):
        return jnp.concatenate([first_half, second_half])

    (image,) = turned((image,), turn_by)
    image, *pieces = lax.optimization_barrier((image, *sent_pieces(pieces[4:])))
    adjoint_first, forward_last = to_slabs(pieces, chunks_in, 2)
    other = send_core(image)

    def share(step):
        mine = jnp.where((own_core == core) & (own_step == step), image, 0.0)
        return mine + jnp.where((pair_core == core) & (pair_step == step), other, 0.0)

    far = share(2)
    passing_up = send_x(far[0:2], 1)
    passing_down = send_x(far[2:4], -1)
    up = share(1)
    down = share(3)
    up = send_x(both(up[0:2] + passing_up, up[2:4]), 1)
    down = send_x(both(down[0:2], down[2:4] + passing_down), -1)
    gradient = share(0) + up + down
    return (gradient, forward_last[None], adjoint_first[None])


def solution(mesh):
    placed = (
        P(("shot", "sub"), None, None),
        P(("shot", "sub"), None, None),
        P("shot"),
        P("shot"),
        P("shot", None),
        P("shot", None),
        P("shot", None, None),
        P("shot", "sub", None, None),
        P("shot", "sub", None, None),
        P("shot", "sub", None, None),
        P("shot", "sub", None, None),
    )
    return jax.shard_map(
        on_device,
        mesh=mesh,
        in_specs=placed,
        out_specs=(
            P(("shot", "sub"), None, None),
            P("shot", "sub", None, None),
            P("shot", "sub", None, None),
        ),
        check_vma=False,
    )
```

```python
import functools

import jax
import jax.numpy as jnp
from jax import lax
from jax.experimental import pallas as pl
from jax.experimental.pallas import tpu as pltpu
from jax.sharding import PartitionSpec as P

lap_coeffs = (-205.0 / 72.0, 8.0 / 5.0, -1.0 / 5.0, 8.0 / 315.0, -1.0 / 560.0)
diff_coeffs = (4.0 / 5.0, -1.0 / 5.0, 4.0 / 105.0, -1.0 / 280.0)
time_step_sq = 0.0088

ROWS = 16
CELLS = 32
SPAN = CELLS + 16
NY = 128
NZ = 256
F32 = jnp.float32
LIMIT = 24 * 2**20


def pairs_by(move):
    pairs = []
    for shot in range(4):
        for sub in range(32):
            x = 2 * (sub // 16) + shot // 2
            target = move(x, shot % 2, (sub // 4) % 4, sub % 4)
            if target is None:
                continue
            tx, tcore, tz, ty = target
            pairs.append((shot * 32 + sub, ((tx % 2) * 2 + tcore) * 32 + (tx // 2) * 16 + tz * 4 + ty))
    return pairs


def send(value, move):
    return lax.ppermute(value, ("shot", "sub"), pairs_by(move))


def send_x(value, steps):
    return send(value, lambda x, c, z, y: ((x + steps) % 4, c, z, y))


def send_core(value):
    return send(value, lambda x, c, z, y: (x, 1 - c, z, y))


def send_z(value, steps):
    return send(value, lambda x, c, z, y: (x, c, (z + steps) % 4, y))


def send_column(value, turn):
    def move(x, c, z, y):
        column = (y + turn) % 4
        return (x, column % 2, z, 2 * (column // 2) + c)

    return send(value, move)


def send_slab(value, turn):
    def move(x, c, z, y):
        return (x, y % 2, z, (2 * (y // 2) + c + turn) % 4)

    return send(value, move)


def send_outer(value):
    def move(x, c, z, y):
        if c == 1 and y < 2:
            return (x, 0, z, y + 2)
        if c == 0 and y >= 2:
            return (x, 1, z, y - 2)
        return None

    return send(value, move)


def next_rows(x, z, steps):
    group = (x // 2) * 4 + z + steps
    if group < 0 or group > 7:
        return None
    return (2 * (group // 4) + x % 2, group % 4)


def send_group(value, steps):
    def move(x, c, z, y):
        place = next_rows(x, z, steps)
        return None if place is None else (place[0], c, place[1], y)

    return send(value, move)


def shape(*sizes):
    return jax.ShapeDtypeStruct(sizes, F32)


def region(rows, cells):
    return shape(rows, 2, cells, 128)


BLOCK = region(ROWS, CELLS)
NEAR = region(ROWS + 8, SPAN)
WIDE = region(ROWS + 16, SPAN)


def call(body, outs, n_smem, operands, scratch=()):
    specs = [pl.BlockSpec(memory_space=pltpu.SMEM)] * n_smem
    specs += [pl.BlockSpec(memory_space=pltpu.VMEM)] * (len(operands) - n_smem)
    return pl.pallas_call(
        body,
        out_shape=tuple(outs),
        in_specs=specs,
        out_specs=tuple(pl.BlockSpec(memory_space=pltpu.VMEM) for _ in outs),
        scratch_shapes=[pltpu.VMEM(s.shape, s.dtype) for s in scratch],
        compiler_params=pltpu.CompilerParams(vmem_limit_bytes=LIMIT),
    )(*operands)


def lanes():
    return lax.broadcasted_iota(jnp.int32, (8, 128), 1)


class Stencil:
    def __init__(self, source, row, cell, lane):
        self.source, self.row, self.cell, self.lane = source, row, cell, lane
        self.center = [self.load(0, 0, half) for half in (0, 1)]
        low, high = self.center
        self.deep = []
        for reach in range(1, 5):
            ahead = [pltpu.roll(v, 128 - reach, 1) for v in (low, high)]
            behind = [pltpu.roll(v, reach, 1) for v in (low, high)]
            front = lane < 128 - reach
            back = lane >= reach
            self.deep.append(
                (
                    (jnp.where(front, ahead[0], ahead[1]), jnp.where(front, ahead[1], 0.0)),
                    (jnp.where(back, behind[0], 0.0), jnp.where(back, behind[1], behind[0])),
                )
            )

    def load(self, rows, cells, half):
        first = self.cell + cells
        return self.source[self.row + rows, half, first : first + 8, :]

    def both(self, direction, reach, half):
        if direction == 0:
            return self.load(reach, 0, half), self.load(-reach, 0, half)
        if direction == 1:
            return self.load(0, reach, half), self.load(0, -reach, half)
        ahead, behind = self.deep[reach - 1]
        return ahead[half], behind[half]

    def derivative(self, direction, half):
        ahead, behind = self.both(direction, 1, half)
        total = ahead - behind
        for reach in range(2, 5):
            ahead, behind = self.both(direction, reach, half)
            total = total + (diff_coeffs[reach - 1] / diff_coeffs[0]) * (ahead - behind)
        return total

    def advanced(self, half, previous, speed_sq, slopes):
        center = self.center[half]
        lap = (3.0 * lap_coeffs[0] / lap_coeffs[1]) * center
        derived = [None, None, None]
        for reach in range(1, 5):
            around = None
            for direction in range(3):
                ahead, behind = self.both(direction, reach, half)
                pair = ahead + behind
                around = pair if around is None else around + pair
                part = ahead - behind
                if reach > 1:
                    part = derived[direction] + (diff_coeffs[reach - 1] / diff_coeffs[0]) * part
                derived[direction] = part
            if reach > 1:
                around = (lap_coeffs[reach] / lap_coeffs[1]) * around
            lap = lap + around
        result = 2.0 * center - previous + speed_sq * lap
        for direction in range(3):
            result = result - slopes[direction] * derived[direction]
        return result


def row_pairs(visit, first, last, cells):
    def step(pair, carry):
        for row in (first + 2 * pair, first + 2 * pair + 1):
            for cell in cells:
                visit(row, cell)
        return carry

    lax.fori_loop(0, (last - first) // 2, step, 0)


def over_block(visit):
    row_pairs(visit, 0, ROWS, range(0, CELLS, 8))


def over_near(visit):
    sides, middle = range(8, 8 + CELLS, 8), range(4, 12 + CELLS, 8)
    row_pairs(visit, 0, 4, sides)
    row_pairs(visit, 4, 4 + ROWS, middle)
    row_pairs(visit, 4 + ROWS, 8 + ROWS, sides)


def add_source(place, amount, first, target):
    @pl.when(place[first] > 0)
    def _():
        row, half = place[first + 1], place[first + 2]
        values = target[row, half]
        cell = lax.broadcasted_iota(jnp.int32, values.shape, 0)
        lane = lax.broadcasted_iota(jnp.int32, values.shape, 1)
        hit = (cell == place[first + 3]) & (lane == place[first + 4])
        target[row, half] = values + jnp.where(hit, amount, 0.0)


def near_step(source, old, model, lane, out, extra=None):
    speed_sq, slopes = model[0], model[1:]

    def visit(row, cell):
        stencil = Stencil(source, row + 4, cell, lane)
        cut = slice(cell, cell + 8)
        for half in (0, 1):
            value = stencil.advanced(
                half,
                old[row, half, cut, :],
                speed_sq[row, half, cut, :],
                [s[row, half, cut, :] for s in slopes],
            )
            if extra is not None:
                value = value + extra(row, half, cut)
            out[row, half, cut, :] = value

    over_near(visit)


def block_step(source, old, model, lane, finish):
    speed_sq, slopes = model[0], model[1:]

    def visit(row, cell):
        stencil = Stencil(source, row + 4, cell + 8, lane)
        near = slice(cell + 8, cell + 16)
        for half in (0, 1):
            value = stencil.advanced(
                half,
                old(row, half, slice(cell, cell + 8)),
                speed_sq[row + 4, half, near, :],
                [s[row + 4, half, near, :] for s in slopes],
            )
            finish(row, half, slice(cell, cell + 8), value)

    over_block(visit)


def of_block(ref):
    return lambda row, half, cut: ref[row, half, cut, :]


def of_near(ref):
    return lambda row, half, cut: ref[row + 4, half, cut.start + 8 : cut.stop + 8, :]


def of_wide(ref):
    return lambda row, half, cut: ref[row + 8, half, cut.start + 8 : cut.stop + 8, :]


def injected(maps, index, field):
    def near(row, half, cut):
        hits = maps[row, half, cut, 0:128]
        seen = maps[row, half, cut, 128 * index : 128 * index + 128]
        return hits * field[row, half, cut, :] - seen

    return near


def cells_at(start):
    return pl.ds(pl.multiple_of(start, 8), 8)


def fill_wide(sides, wide, block, halo):
    below, above, inner, outer = halo
    wide[0:8, :, 8 : 8 + CELLS, :] = below[...]
    wide[8 : 8 + ROWS, :, 8 : 8 + CELLS, :] = block[...]
    wide[8 + ROWS : 16 + ROWS, :, 8 : 8 + CELLS, :] = above[...]
    wide[4 : 12 + ROWS, :, cells_at(sides[2]), :] = inner[...]
    wide[4 : 12 + ROWS, :, cells_at(sides[3]), :] = outer[...]


WIDE_EDGES = [region(8, CELLS)] * 2


def write_wide_edges(block, edges):
    low, high = edges
    low[...] = block[0:8]
    high[...] = block[ROWS - 8 : ROWS]


def rim_body(sides, block, below, above, inner, outer):
    for out, side in ((inner, 0), (outer, 1)):
        cut = cells_at(sides[side])
        out[0:4] = below[4:8, :, cut, :]
        out[4 : 4 + ROWS] = block[:, :, cut, :]
        out[4 + ROWS : 8 + ROWS] = above[0:4, :, cut, :]


def swap_wide_edges(sides, block, edges):
    low, high = edges
    below, above = send_group(high, 1), send_group(low, -1)
    inner, outer = call(rim_body, [region(ROWS + 8, 8)] * 2, 1, (sides, block, below, above))
    return below, above, send_core(inner), send_outer(outer)


def cut_body(chunks, *refs, margins):
    count = len(margins)
    slabs, pieces = refs[:count], refs[count:]
    for turn in range(4):
        chunk = chunks[turn]
        first = pl.multiple_of(chunk * CELLS, CELLS)
        before = pl.multiple_of(jnp.maximum(first - 8, 0), 8)
        after = pl.multiple_of(jnp.minimum(first + CELLS, NY - 8), 8)
        at = 0
        for slab, margin in zip(slabs, margins):
            if margin:
                pieces[turn][:, at : at + 8, :] = jnp.where(chunk > 0, slab[:, pl.ds(before, 8), :], 0.0)
                at += 8
            pieces[turn][:, at : at + CELLS, :] = slab[:, pl.ds(first, CELLS), :]
            at += CELLS
            if margin:
                pieces[turn][:, at : at + 8, :] = jnp.where(chunk < 3, slab[:, pl.ds(after, 8), :], 0.0)
                at += 8


def cut_pieces(slabs, margins, chunks):
    width = sum(SPAN if margin else CELLS for margin in margins)
    pieces = call(functools.partial(cut_body, margins=margins), [shape(4, width, NZ)] * 4, 1, (chunks, *slabs))
    return pieces


def place_pieces(slots, pieces, outs):
    for turn in range(4):
        slot = pl.multiple_of(slots[turn] * 4, 4)
        at = 0
        for out in outs:
            width = out.shape[2]
            for half in (0, 1):
                out[pl.ds(slot, 4), half] = pieces[turn][:, at : at + width, 128 * half : 128 * half + 128]
            at += width


def gather_body(slots, *refs, depths):
    pieces, outs = refs[:4], refs[4:]
    low, high = outs[-2:]
    place_pieces(slots, pieces, outs[:-2])
    at = 0
    core = slice(8, 8 + CELLS)
    for out, depth in zip(outs, depths):
        if depth == 8:
            low[:, :, at : at + SPAN, :] = out[0:4]
            high[:, :, at : at + SPAN, :] = out[ROWS - 4 : ROWS]
            at += SPAN
            low[:, :, at : at + CELLS, :] = out[4:8, :, core, :]
            high[:, :, at : at + CELLS, :] = out[ROWS - 8 : ROWS - 4, :, core, :]
            at += CELLS
        elif depth == 4:
            low[:, :, at : at + CELLS, :] = out[0:4, :, core, :]
            high[:, :, at : at + CELLS, :] = out[ROWS - 4 : ROWS, :, core, :]
            at += CELLS


def gather_blocks(pieces, slots, depths):
    outs = [region(ROWS, SPAN if depth else CELLS) for depth in depths]
    packed = sum({8: SPAN + CELLS, 4: CELLS, 0: 0}[depth] for depth in depths)
    outs += [region(4, packed)] * 2
    return call(functools.partial(gather_body, depths=depths), outs, 1, (slots, *pieces))


def stack_wide(out, below, middle, above, at):
    core = slice(8, 8 + CELLS)
    end = at + SPAN + CELLS
    out[0:4, :, core, :] = below[:, :, at + SPAN : end, :]
    out[4:8] = below[:, :, at : at + SPAN, :]
    out[8 : 8 + ROWS] = middle[...]
    out[8 + ROWS : 12 + ROWS] = above[:, :, at : at + SPAN, :]
    out[12 + ROWS : 16 + ROWS, :, core, :] = above[:, :, at + SPAN : end, :]


def stack_near(out, below, middle, above, at):
    core = slice(8, 8 + CELLS)
    out[0:4, :, core, :] = below[:, :, at : at + CELLS, :]
    out[4 : 4 + ROWS] = middle[...]
    out[4 + ROWS : 8 + ROWS, :, core, :] = above[:, :, at : at + CELLS, :]


def fields_body(now, old, adjoint, below, above, wide, old_near, adjoint_near):
    stack_wide(wide, below, now, above, 0)
    stack_near(old_near, below, old, above, SPAN + CELLS)
    stack_near(adjoint_near, below, adjoint, above, SPAN + 2 * CELLS)


def model_body(log_mass, speed, below, above, speed_sq, s0, s1, s2, twice, wide, speed_near):
    stack_wide(wide, below, log_mass, above, 0)
    stack_near(speed_near, below, speed, above, SPAN + CELLS)
    twice[...] = 2.0 / speed[:, :, 8 : 8 + CELLS, :]
    lane = lanes()

    def visit(row, cell):
        stencil = Stencil(wide, row + 4, cell, lane)
        cut = slice(cell, cell + 8)
        for half in (0, 1):
            value = speed_near[row, half, cut, :]
            scale = time_step_sq * value * value
            speed_sq[row, half, cut, :] = lap_coeffs[1] * scale
            scale = (diff_coeffs[0] * diff_coeffs[0]) * scale
            for direction, out in enumerate((s0, s1, s2)):
                out[row, half, cut, :] = scale * stencil.derivative(direction, half)

    over_near(visit)


def forward_body(place, amount, wide, old, speed_sq, s0, s1, s2, near, new, *edges):
    model = (speed_sq, s0, s1, s2)
    lane = lanes()
    near_step(wide, old, model, lane, near)
    add_source(place, amount[0], 0, near)

    def finish(row, half, cut, value):
        new[row, half, cut, :] = value

    block_step(near, of_wide(wide), model, lane, finish)
    add_source(place, amount[1], 5, new)
    write_wide_edges(new, edges)


def write_pieces(slots, block, pieces, at):
    for turn in range(4):
        slot = pl.multiple_of(slots[turn] * 4, 4)
        for half in (0, 1):
            pieces[turn][:, at : at + CELLS, 128 * half : 128 * half + 128] = block[pl.ds(slot, 4), half]


def turn_body(place, amount, sides, block, *refs):
    halo, refs = refs[:4], refs[4:]
    old, speed_sq, s0, s1, s2, adjoint, later, maps, near, new, adjoint_new, summed = refs[:12]
    edges, wide = refs[12:14], refs[14]
    model = (speed_sq, s0, s1, s2)
    lane = lanes()
    fill_wide(sides, wide, block, halo)
    near_step(wide, old, model, lane, near)
    add_source(place, amount[2], 0, near)

    def finish(row, half, cut, value):
        new[row, half, cut, :] = value

    block_step(near, of_block(block), model, lane, finish)
    add_source(place, amount[3], 5, new)

    def finish_adjoint(row, half, cut, value):
        hits = of_near(maps)(row, half, cut)
        ahead = new[row, half, cut, :]
        value = value + (hits[:, 0:128] * ahead - hits[:, 4 * 128 : 5 * 128])
        adjoint_new[row, half, cut, :] = value
        summed[row, half, cut, :] = value * (
            ahead - 2.0 * of_near(near)(row, half, cut) + block[row, half, cut, :]
        )

    block_step(adjoint, of_block(later), model, lane, finish_adjoint)
    write_wide_edges(adjoint_new, edges)


def adjoint_body(sides, block, *refs):
    halo, refs = refs[:4], refs[4:]
    old, speed_sq, s0, s1, s2, maps, u3, u2, u1, u0, sums = refs[:11]
    near, new, summed, low, high, inner, outer, wide = refs[11:]
    model = (speed_sq, s0, s1, s2)
    lane = lanes()
    fill_wide(sides, wide, block, halo)
    near_step(wide, old, model, lane, near, injected(maps, 3, u3))

    def finish(row, half, cut, value):
        hits = of_near(maps)(row, half, cut)
        third = of_near(u3)(row, half, cut)
        second = u2[row, half, cut, :]
        first = of_near(u1)(row, half, cut)
        zeroth = of_wide(u0)(row, half, cut)
        value = value + (hits[:, 0:128] * second - hits[:, 2 * 128 : 3 * 128])
        new[row, half, cut, :] = value
        total = sums[row, half, cut, :]
        total = total + of_near(near)(row, half, cut) * (third - 2.0 * second + first)
        summed[row, half, cut, :] = total + value * (second - 2.0 * first + zeroth)

    block_step(near, of_block(block), model, lane, finish)
    low[...] = new[0:4]
    high[...] = new[ROWS - 4 : ROWS]
    inner[...] = new[:, :, cells_at(sides[0]), :]
    outer[...] = new[:, :, cells_at(sides[1]), :]


def last_body(
    slots, model_slots, sides, block, below, above, inner, outer, old, speed_sq, s0, s1, s2, maps,
    u1, u0, u_before, sums, twice, u4, p0, p1, p2, p3, q0, q1, q2, q3, near, new, image,
):
    near[0:4, :, 8 : 8 + CELLS, :] = below[...]
    near[4 : 4 + ROWS, :, 8 : 8 + CELLS, :] = block[...]
    near[4 + ROWS : 8 + ROWS, :, 8 : 8 + CELLS, :] = above[...]
    near[4 : 4 + ROWS, :, cells_at(sides[2]), :] = inner[...]
    near[4 : 4 + ROWS, :, cells_at(sides[3]), :] = outer[...]
    lane = lanes()

    def finish(row, half, cut, value):
        hits = of_near(maps)(row, half, cut)
        first = of_near(u1)(row, half, cut)
        value = value + (hits[:, 0:128] * first - hits[:, 128:256])
        new[row, half, cut, :] = value
        curvature = first - 2.0 * of_wide(u0)(row, half, cut) + of_near(u_before)(row, half, cut)
        image[row, half, cut, :] = twice[row, half, cut, :] * (sums[row, half, cut, :] + value * curvature)

    block_step(near, of_near(old), (speed_sq, s0, s1, s2), lane, finish)
    write_pieces(model_slots, image, (p0, p1, p2, p3), 0)
    write_pieces(slots, new, (q0, q1, q2, q3), 0)
    write_pieces(slots, u4, (q0, q1, q2, q3), CELLS)


def spread_body(chunks, p0, p1, p2, p3, *outs):
    for turn, piece in enumerate((p0, p1, p2, p3)):
        first = pl.multiple_of(chunks[turn] * CELLS, CELLS)
        for index, out in enumerate(outs):
            out[:, pl.ds(first, CELLS), :] = piece[:, CELLS * index : CELLS * index + CELLS, :]


def sent(pieces, move):
    return [move(piece, turn) for turn, piece in enumerate(pieces)]


def to_slabs(pieces, chunks, count):
    return call(spread_body, [shape(4, NY, NZ)] * count, 1, (chunks, *pieces))


def on_device(
    velocity,
    density,
    aperture_start,
    source_cell,
    receiver_cells,
    wavelet,
    observed,
    forward_old,
    forward_now,
    adjoint_later,
    adjoint_now,
):
    shot = lax.axis_index("shot")
    sub = lax.axis_index("sub")
    core = shot % 2
    x_hi = sub // 16
    x = 2 * x_hi + shot // 2
    z = (sub // 4) % 4
    y = sub % 4
    group = sub // 4
    start = aperture_start[0]
    column = 2 * (y // 2) + core
    own_small = (
        jnp.concatenate([aperture_start, source_cell, receiver_cells[0]]),
        jnp.concatenate([wavelet[0], observed.reshape(-1)]),
    )
    partner_small = tuple(send_core(value) for value in own_small)

    def wanted(first_slab):
        upper = first_slab // 4 + (y < first_slab % 4).astype(jnp.int32)
        block = jnp.clip(x_hi + (upper - z + 3) // 4, 0, 7)
        position = 2 * (block % 2) + block // 4
        return (block // 2) % 2, (position - x) % 4, upper % 4

    own_core, own_step, turn_by = wanted(start)
    turns = jnp.arange(4, dtype=jnp.int32)
    chunks_out = (y + turns) % 4
    chunks_in = (y - turns) % 4

    pieces = cut_pieces(
        [forward_now[0], forward_old[0], adjoint_now[0], adjoint_later[0]],
        (True, True, True, False),
        chunks_out,
    )
    velocity, partner_small, *pieces = lax.optimization_barrier((velocity, partner_small, *pieces))
    pair_core, pair_step, _ = wanted(partner_small[0][0])
    whole, amounts = (
        jnp.where(y % 2 == core, own, partner) for own, partner in zip(own_small, partner_small)
    )
    skip = whole[0] % 4
    source, receivers = whole[1], whole[2:]
    amount, seen = amounts[:4], amounts[4:].reshape(4, -1)
    slots_plain = (column - turns) % 4
    slots_in = (column - turns - skip) % 4
    slots_back = (column + turns) % 4
    slots_out = (column + turns - skip) % 4
    sides = jnp.where(
        core == 0,
        jnp.array([CELLS - 8, 0, 8 + CELLS, 0], jnp.int32),
        jnp.array([0, CELLS - 8, 0, 8 + CELLS], jnp.int32),
    )

    def gathered(slab):
        from_below = send_x(slab, 1)
        from_above = send_x(slab, -1)
        far = jnp.concatenate([send_x(from_below[0:2], 1), send_x(from_above[2:4], -1)])

        def pick(step):
            return jnp.where(
                step < 2, jnp.where(step == 0, slab, from_above), jnp.where(step == 2, far, from_below)
            )

        other = send_core(pick(pair_step))
        return jnp.where(own_core == core, pick(own_step), other)

    def turned(arrays, steps):
        def branch(count):
            return lambda *values: tuple(send_z(value, count) if count else value for value in values)

        return lax.switch(steps, [branch(count) for count in (0, 1, 2, -1)], *arrays)

    log_slab = gathered(jnp.log(density))
    speed_slab = gathered(velocity)
    pieces = sent(pieces, send_column)

    def local_place(cells, rows_more, cells_more):
        rows = cells // (NY * NZ) - group * ROWS + rows_more
        columns = (cells // NZ) % NY - column * CELLS + cells_more
        inside = (rows >= 0) & (rows < ROWS + 2 * rows_more)
        inside = inside & (columns >= 0) & (columns < CELLS + 2 * cells_more)
        return inside, rows, (cells // 128) % 2, columns, cells % 128

    inside, rows, half, columns, lane = local_place(receivers, 4, 8)
    line = jnp.where(inside, (rows * 2 + half) * SPAN + columns, -1)
    lines = (ROWS + 8) * 2 * SPAN
    on_line = (jnp.arange(lines, dtype=jnp.int32)[:, None] == line[None, :]).astype(F32)
    weights = jnp.concatenate([jnp.ones_like(seen[:1]), seen])
    hit = lane[:, None, None] == jnp.arange(128, dtype=jnp.int32)[None, None, :]
    at_lane = jnp.where(hit, weights.T[:, :, None], 0.0).reshape(-1, 5 * 128)
    maps = jnp.dot(on_line, at_lane, precision=lax.Precision.HIGHEST)
    maps = maps.reshape(ROWS + 8, 2, SPAN, 5 * 128)

    def source_place(rows_more, cells_more):
        inside, rows, half, columns, lane = local_place(source, rows_more, cells_more)
        rows = jnp.clip(rows, 0, ROWS + 2 * rows_more - 1)
        return [inside.astype(jnp.int32), rows, half, columns, lane]

    place = jnp.stack(source_place(4, 8) + source_place(0, 0))

    log_slab, speed_slab, *pieces[:2] = lax.optimization_barrier((log_slab, speed_slab, *pieces[:2]))
    log_slab, speed_slab = turned((log_slab, speed_slab), (4 - turn_by) % 4)
    log_slab, speed_slab, *pieces = lax.optimization_barrier((log_slab, speed_slab, *pieces))
    model_pieces = sent(cut_pieces([log_slab, speed_slab], (True, True), chunks_out), send_column)
    now, old, adjoint, a_later, side_low, side_high = gather_blocks(pieces, slots_plain, (8, 4, 4, 0))
    below, above = send_group(side_high, 1), send_group(side_low, -1)
    u_wide, old_near, a_near = call(
        fields_body, [WIDE, NEAR, NEAR], 0, (now, old, adjoint, below, above)
    )
    log_mass, speed, side_low, side_high = gather_blocks(model_pieces, slots_in, (8, 4))
    below, above = send_group(side_high, 1), send_group(side_low, -1)
    below, above, maps = lax.optimization_barrier((below, above, maps))
    *model, twice = call(
        model_body, [NEAR] * 4 + [BLOCK], 0, (log_mass, speed, below, above), (WIDE, NEAR)
    )

    u1, u2, *edges = call(
        forward_body, [NEAR, BLOCK] + WIDE_EDGES, 2, (place, amount, u_wide, old_near, *model)
    )
    halo = swap_wide_edges(sides, u2, edges)
    u3, u4, a3, sums, *edges = call(
        turn_body,
        [NEAR, BLOCK, BLOCK, BLOCK] + WIDE_EDGES,
        3,
        (place, amount, sides, u2, *halo, u1, *model, a_near, a_later, maps),
        (WIDE,),
    )
    halo = swap_wide_edges(sides, a3, edges)
    a2, a1, sums, side_low, side_high, inner, outer = call(
        adjoint_body,
        [NEAR, BLOCK, BLOCK] + [region(4, CELLS)] * 2 + [region(ROWS, 8)] * 2,
        1,
        (sides, a3, *halo, a_near, *model, maps, u3, u2, u1, u_wide, sums),
        (WIDE,),
    )
    halo = (
        send_group(side_high, 1),
        send_group(side_low, -1),
        send_core(inner),
        send_outer(outer),
    )
    pieces = call(
        last_body,
        [shape(4, CELLS, NZ)] * 4 + [shape(4, 2 * CELLS, NZ)] * 4,
        3,
        (slots_back, slots_out, sides, a1, *halo, a2, *model, maps, u1, u_wide, old_near, sums, twice, u4),
        (NEAR, BLOCK, BLOCK),
    )
    pieces = lax.optimization_barrier((*sent(pieces[:4], send_slab), *pieces[4:]))
    (image,) = to_slabs(pieces[:4], chunks_in, 1)

    def both(first_half, second_half):
        return jnp.concatenate([first_half, second_half])

    (image,) = turned((image,), turn_by)
    image, *pieces = lax.optimization_barrier((image, *sent(pieces[4:], send_slab)))
    adjoint_first, forward_last = to_slabs(pieces, chunks_in, 2)
    other = send_core(image)

    def share(step):
        mine = jnp.where((own_core == core) & (own_step == step), image, 0.0)
        return mine + jnp.where((pair_core == core) & (pair_step == step), other, 0.0)

    far = share(2)
    passing_up = send_x(far[0:2], 1)
    passing_down = send_x(far[2:4], -1)
    up = share(1)
    down = share(3)
    up = send_x(both(up[0:2] + passing_up, up[2:4]), 1)
    down = send_x(both(down[0:2], down[2:4] + passing_down), -1)
    gradient = share(0) + up + down
    return (gradient, forward_last[None], adjoint_first[None])


def solution(mesh):
    placed = (
        P(("shot", "sub"), None, None),
        P(("shot", "sub"), None, None),
        P("shot"),
        P("shot"),
        P("shot", None),
        P("shot", None),
        P("shot", None, None),
        P("shot", "sub", None, None),
        P("shot", "sub", None, None),
        P("shot", "sub", None, None),
        P("shot", "sub", None, None),
    )
    return jax.shard_map(
        on_device,
        mesh=mesh,
        in_specs=placed,
        out_specs=(
            P(("shot", "sub"), None, None),
            P("shot", "sub", None, None),
            P("shot", "sub", None, None),
        ),
        check_vma=False,
    )
```

```python
import functools

import jax
import jax.numpy as jnp
from jax import lax
from jax.experimental import pallas as pl
from jax.experimental.pallas import tpu as pltpu
from jax.sharding import PartitionSpec as P

lap_coeffs = (-205.0 / 72.0, 8.0 / 5.0, -1.0 / 5.0, 8.0 / 315.0, -1.0 / 560.0)
diff_coeffs = (4.0 / 5.0, -1.0 / 5.0, 4.0 / 105.0, -1.0 / 280.0)
time_step_sq = 0.0088

ROWS = 16
CELLS = 32
SPAN = CELLS + 16
NY = 128
NZ = 256
F32 = jnp.float32
LIMIT = 24 * 2**20


def pairs_by(move):
    pairs = []
    for shot in range(4):
        for sub in range(32):
            x = 2 * (sub // 16) + shot // 2
            target = move(x, shot % 2, (sub // 4) % 4, sub % 4)
            if target is None:
                continue
            tx, tcore, tz, ty = target
            pairs.append((shot * 32 + sub, ((tx % 2) * 2 + tcore) * 32 + (tx // 2) * 16 + tz * 4 + ty))
    return pairs


def send(value, move):
    return lax.ppermute(value, ("shot", "sub"), pairs_by(move))


def send_x(value, steps):
    return send(value, lambda x, c, z, y: ((x + steps) % 4, c, z, y))


def send_core(value):
    return send(value, lambda x, c, z, y: (x, 1 - c, z, y))


def send_z(value, steps):
    return send(value, lambda x, c, z, y: (x, c, (z + steps) % 4, y))


def send_y(value, steps):
    return send(value, lambda x, c, z, y: (x, c, z, (y + steps) % 4))


def next_rows(x, z, steps):
    group = (x // 2) * 4 + z + steps
    if group < 0 or group > 7:
        return None
    return (2 * (group // 4) + x % 2, group % 4)


def send_group(value, steps):
    def move(x, c, z, y):
        place = next_rows(x, z, steps)
        return None if place is None else (place[0], c, place[1], y)

    return send(value, move)


def send_cells(value, steps):
    return send(value, lambda x, c, z, y: (x, c, z, y + steps) if 0 <= y + steps < 4 else None)


def shape(*sizes):
    return jax.ShapeDtypeStruct(sizes, F32)


def region(rows, cells):
    return shape(rows, 2, cells, 128)


BLOCK = region(ROWS, CELLS)
NEAR = region(ROWS + 8, SPAN)
WIDE = region(ROWS + 16, SPAN)


def call(body, outs, n_smem, operands, scratch=()):
    specs = [pl.BlockSpec(memory_space=pltpu.SMEM)] * n_smem
    specs += [pl.BlockSpec(memory_space=pltpu.VMEM)] * (len(operands) - n_smem)
    return pl.pallas_call(
        body,
        out_shape=tuple(outs),
        in_specs=specs,
        out_specs=tuple(pl.BlockSpec(memory_space=pltpu.VMEM) for _ in outs),
        scratch_shapes=[pltpu.VMEM(s.shape, s.dtype) for s in scratch],
        compiler_params=pltpu.CompilerParams(vmem_limit_bytes=LIMIT),
    )(*operands)


def lanes():
    return lax.broadcasted_iota(jnp.int32, (8, 128), 1)


class Stencil:
    def __init__(self, source, row, cell, lane):
        self.source, self.row, self.cell, self.lane = source, row, cell, lane
        self.center = [self.load(0, 0, half) for half in (0, 1)]
        low, high = self.center
        self.deep = []
        for reach in range(1, 5):
            ahead = [pltpu.roll(v, 128 - reach, 1) for v in (low, high)]
            behind = [pltpu.roll(v, reach, 1) for v in (low, high)]
            front = lane < 128 - reach
            back = lane >= reach
            self.deep.append(
                (
                    (jnp.where(front, ahead[0], ahead[1]), jnp.where(front, ahead[1], 0.0)),
                    (jnp.where(back, behind[0], 0.0), jnp.where(back, behind[1], behind[0])),
                )
            )

    def load(self, rows, cells, half):
        first = self.cell + cells
        return self.source[self.row + rows, half, first : first + 8, :]

    def both(self, direction, reach, half):
        if direction == 0:
            return self.load(reach, 0, half), self.load(-reach, 0, half)
        if direction == 1:
            return self.load(0, reach, half), self.load(0, -reach, half)
        ahead, behind = self.deep[reach - 1]
        return ahead[half], behind[half]

    def derivative(self, direction, half):
        ahead, behind = self.both(direction, 1, half)
        total = ahead - behind
        for reach in range(2, 5):
            ahead, behind = self.both(direction, reach, half)
            total = total + (diff_coeffs[reach - 1] / diff_coeffs[0]) * (ahead - behind)
        return total

    def advanced(self, half, previous, speed_sq, slopes):
        center = self.center[half]
        lap = (3.0 * lap_coeffs[0] / lap_coeffs[1]) * center
        derived = [None, None, None]
        for reach in range(1, 5):
            around = None
            for direction in range(3):
                ahead, behind = self.both(direction, reach, half)
                pair = ahead + behind
                around = pair if around is None else around + pair
                part = ahead - behind
                if reach > 1:
                    part = derived[direction] + (diff_coeffs[reach - 1] / diff_coeffs[0]) * part
                derived[direction] = part
            if reach > 1:
                around = (lap_coeffs[reach] / lap_coeffs[1]) * around
            lap = lap + around
        result = 2.0 * center - previous + speed_sq * lap
        for direction in range(3):
            result = result - slopes[direction] * derived[direction]
        return result


def row_pairs(visit, first, last, cells):
    def step(pair, carry):
        for row in (first + 2 * pair, first + 2 * pair + 1):
            for cell in cells:
                visit(row, cell)
        return carry

    lax.fori_loop(0, (last - first) // 2, step, 0)


def over_block(visit):
    row_pairs(visit, 0, ROWS, range(0, CELLS, 8))


def over_near(visit):
    sides, middle = range(8, 8 + CELLS, 8), range(4, 12 + CELLS, 8)
    row_pairs(visit, 0, 4, sides)
    row_pairs(visit, 4, 4 + ROWS, middle)
    row_pairs(visit, 4 + ROWS, 8 + ROWS, sides)


def add_source(place, amount, first, target):
    @pl.when(place[first] > 0)
    def _():
        row, half = place[first + 1], place[first + 2]
        values = target[row, half]
        cell = lax.broadcasted_iota(jnp.int32, values.shape, 0)
        lane = lax.broadcasted_iota(jnp.int32, values.shape, 1)
        hit = (cell == place[first + 3]) & (lane == place[first + 4])
        target[row, half] = values + jnp.where(hit, amount, 0.0)


def near_step(source, old, model, lane, out, extra=None):
    speed_sq, slopes = model[0], model[1:]

    def visit(row, cell):
        stencil = Stencil(source, row + 4, cell, lane)
        cut = slice(cell, cell + 8)
        for half in (0, 1):
            value = stencil.advanced(
                half,
                old[row, half, cut, :],
                speed_sq[row, half, cut, :],
                [s[row, half, cut, :] for s in slopes],
            )
            if extra is not None:
                value = value + extra(row, half, cut)
            out[row, half, cut, :] = value

    over_near(visit)


def block_step(source, old, model, lane, finish):
    speed_sq, slopes = model[0], model[1:]

    def visit(row, cell):
        stencil = Stencil(source, row + 4, cell + 8, lane)
        near = slice(cell + 8, cell + 16)
        for half in (0, 1):
            value = stencil.advanced(
                half,
                old(row, half, slice(cell, cell + 8)),
                speed_sq[row + 4, half, near, :],
                [s[row + 4, half, near, :] for s in slopes],
            )
            finish(row, half, slice(cell, cell + 8), value)

    over_block(visit)


def of_block(ref):
    return lambda row, half, cut: ref[row, half, cut, :]


def of_near(ref):
    return lambda row, half, cut: ref[row + 4, half, cut.start + 8 : cut.stop + 8, :]


def of_wide(ref):
    return lambda row, half, cut: ref[row + 8, half, cut.start + 8 : cut.stop + 8, :]


def injected(maps, index, field):
    def near(row, half, cut):
        hits = maps[row, half, cut, 0:128]
        seen = maps[row, half, cut, 128 * index : 128 * index + 128]
        return hits * field[row, half, cut, :] - seen

    return near


def fill_wide(wide, block, halo):
    below, above, left, right, left_corners, right_corners = halo
    wide[0:8, :, 8 : 8 + CELLS, :] = below[...]
    wide[8 : 8 + ROWS, :, 8 : 8 + CELLS, :] = block[...]
    wide[8 + ROWS : 16 + ROWS, :, 8 : 8 + CELLS, :] = above[...]
    for cells, side, corners in (
        (slice(0, 8), left, left_corners),
        (slice(8 + CELLS, SPAN), right, right_corners),
    ):
        wide[4:8, :, cells, :] = corners[0:4]
        wide[8 : 8 + ROWS, :, cells, :] = side[...]
        wide[8 + ROWS : 12 + ROWS, :, cells, :] = corners[4:8]


WIDE_EDGES = [region(8, CELLS)] * 2 + [region(ROWS, 8)] * 2


def write_wide_edges(block, edges):
    low, high, low_cells, high_cells = edges
    low[...] = block[0:8]
    high[...] = block[ROWS - 8 : ROWS]
    low_cells[...] = block[:, :, 0:8, :]
    high_cells[...] = block[:, :, CELLS - 8 : CELLS, :]


def rim_body(below, above, low, high):
    for out, cut in ((low, slice(0, 8)), (high, slice(CELLS - 8, CELLS))):
        out[0:4] = below[4:8, :, cut, :]
        out[4:8] = above[0:4, :, cut, :]


def swap_wide_edges(edges):
    low, high, low_cells, high_cells = edges
    below, above = send_group(high, 1), send_group(low, -1)
    left, right = send_cells(high_cells, 1), send_cells(low_cells, -1)
    low_corners, high_corners = call(rim_body, [region(8, 8)] * 2, 0, (below, above))
    return below, above, left, right, send_cells(high_corners, 1), send_cells(low_corners, -1)


def cut_body(chunks, *refs, margins):
    count = len(margins)
    slabs, pieces = refs[:count], refs[count:]
    for turn in range(4):
        chunk = chunks[turn]
        first = pl.multiple_of(chunk * CELLS, CELLS)
        before = pl.multiple_of(jnp.maximum(first - 8, 0), 8)
        after = pl.multiple_of(jnp.minimum(first + CELLS, NY - 8), 8)
        at = 0
        for slab, margin in zip(slabs, margins):
            if margin:
                pieces[turn][:, at : at + 8, :] = jnp.where(chunk > 0, slab[:, pl.ds(before, 8), :], 0.0)
                at += 8
            pieces[turn][:, at : at + CELLS, :] = slab[:, pl.ds(first, CELLS), :]
            at += CELLS
            if margin:
                pieces[turn][:, at : at + 8, :] = jnp.where(chunk < 3, slab[:, pl.ds(after, 8), :], 0.0)
                at += 8


def cut_pieces(slabs, margins, chunks):
    width = sum(SPAN if margin else CELLS for margin in margins)
    pieces = call(functools.partial(cut_body, margins=margins), [shape(4, width, NZ)] * 4, 1, (chunks, *slabs))
    return pieces


def place_pieces(slots, pieces, outs):
    for turn in range(4):
        slot = pl.multiple_of(slots[turn] * 4, 4)
        at = 0
        for out in outs:
            width = out.shape[2]
            for half in (0, 1):
                out[pl.ds(slot, 4), half] = pieces[turn][:, at : at + width, 128 * half : 128 * half + 128]
            at += width


def gather_body(slots, *refs, depths):
    pieces, outs = refs[:4], refs[4:]
    low, high = outs[-2:]
    place_pieces(slots, pieces, outs[:-2])
    at = 0
    core = slice(8, 8 + CELLS)
    for out, depth in zip(outs, depths):
        if depth == 8:
            low[:, :, at : at + SPAN, :] = out[0:4]
            high[:, :, at : at + SPAN, :] = out[ROWS - 4 : ROWS]
            at += SPAN
            low[:, :, at : at + CELLS, :] = out[4:8, :, core, :]
            high[:, :, at : at + CELLS, :] = out[ROWS - 8 : ROWS - 4, :, core, :]
            at += CELLS
        elif depth == 4:
            low[:, :, at : at + CELLS, :] = out[0:4, :, core, :]
            high[:, :, at : at + CELLS, :] = out[ROWS - 4 : ROWS, :, core, :]
            at += CELLS


def gather_blocks(pieces, slots, depths):
    outs = [region(ROWS, SPAN if depth else CELLS) for depth in depths]
    packed = sum({8: SPAN + CELLS, 4: CELLS, 0: 0}[depth] for depth in depths)
    outs += [region(4, packed)] * 2
    return call(functools.partial(gather_body, depths=depths), outs, 1, (slots, *pieces))


def stack_wide(out, below, middle, above, at):
    core = slice(8, 8 + CELLS)
    end = at + SPAN + CELLS
    out[0:4, :, core, :] = below[:, :, at + SPAN : end, :]
    out[4:8] = below[:, :, at : at + SPAN, :]
    out[8 : 8 + ROWS] = middle[...]
    out[8 + ROWS : 12 + ROWS] = above[:, :, at : at + SPAN, :]
    out[12 + ROWS : 16 + ROWS, :, core, :] = above[:, :, at + SPAN : end, :]


def stack_near(out, below, middle, above, at):
    core = slice(8, 8 + CELLS)
    out[0:4, :, core, :] = below[:, :, at : at + CELLS, :]
    out[4 : 4 + ROWS] = middle[...]
    out[4 + ROWS : 8 + ROWS, :, core, :] = above[:, :, at : at + CELLS, :]


def fields_body(now, old, adjoint, below, above, wide, old_near, adjoint_near):
    stack_wide(wide, below, now, above, 0)
    stack_near(old_near, below, old, above, SPAN + CELLS)
    stack_near(adjoint_near, below, adjoint, above, SPAN + 2 * CELLS)


def model_body(log_mass, speed, log_below, log_above, below, above, speed_sq, s0, s1, s2, twice, wide, speed_near):
    stack_wide(wide, log_below, log_mass, log_above, 0)
    stack_near(speed_near, below, speed, above, 0)
    twice[...] = 2.0 / speed[:, :, 8 : 8 + CELLS, :]
    lane = lanes()

    def visit(row, cell):
        stencil = Stencil(wide, row + 4, cell, lane)
        cut = slice(cell, cell + 8)
        for half in (0, 1):
            value = speed_near[row, half, cut, :]
            scale = time_step_sq * value * value
            speed_sq[row, half, cut, :] = lap_coeffs[1] * scale
            scale = (diff_coeffs[0] * diff_coeffs[0]) * scale
            for direction, out in enumerate((s0, s1, s2)):
                out[row, half, cut, :] = scale * stencil.derivative(direction, half)

    over_near(visit)


def forward_body(place, amount, wide, old, speed_sq, s0, s1, s2, near, new, *edges):
    model = (speed_sq, s0, s1, s2)
    lane = lanes()
    near_step(wide, old, model, lane, near)
    add_source(place, amount[0], 0, near)

    def finish(row, half, cut, value):
        new[row, half, cut, :] = value

    block_step(near, of_wide(wide), model, lane, finish)
    add_source(place, amount[1], 5, new)
    write_wide_edges(new, edges)


def write_pieces(slots, block, pieces, at):
    for turn in range(4):
        slot = pl.multiple_of(slots[turn] * 4, 4)
        for half in (0, 1):
            pieces[turn][:, at : at + CELLS, 128 * half : 128 * half + 128] = block[pl.ds(slot, 4), half]


def turn_body(place, amount, block, *refs):
    halo, refs = refs[:6], refs[6:]
    old, speed_sq, s0, s1, s2, adjoint, later, maps, near, new, adjoint_new, summed = refs[:12]
    edges, wide = refs[12:16], refs[16]
    model = (speed_sq, s0, s1, s2)
    lane = lanes()
    fill_wide(wide, block, halo)
    near_step(wide, old, model, lane, near)
    add_source(place, amount[2], 0, near)

    def finish(row, half, cut, value):
        new[row, half, cut, :] = value

    block_step(near, of_block(block), model, lane, finish)
    add_source(place, amount[3], 5, new)

    def finish_adjoint(row, half, cut, value):
        hits = of_near(maps)(row, half, cut)
        ahead = new[row, half, cut, :]
        value = value + (hits[:, 0:128] * ahead - hits[:, 4 * 128 : 5 * 128])
        adjoint_new[row, half, cut, :] = value
        summed[row, half, cut, :] = value * (
            ahead - 2.0 * of_near(near)(row, half, cut) + block[row, half, cut, :]
        )

    block_step(adjoint, of_block(later), model, lane, finish_adjoint)
    write_wide_edges(adjoint_new, edges)


def adjoint_body(block, *refs):
    halo, refs = refs[:6], refs[6:]
    old, speed_sq, s0, s1, s2, maps, u3, u2, u1, u0, sums = refs[:11]
    near, new, summed, low, high, low_cells, high_cells, wide = refs[11:]
    model = (speed_sq, s0, s1, s2)
    lane = lanes()
    fill_wide(wide, block, halo)
    near_step(wide, old, model, lane, near, injected(maps, 3, u3))

    def finish(row, half, cut, value):
        hits = of_near(maps)(row, half, cut)
        third = of_near(u3)(row, half, cut)
        second = u2[row, half, cut, :]
        first = of_near(u1)(row, half, cut)
        zeroth = of_wide(u0)(row, half, cut)
        value = value + (hits[:, 0:128] * second - hits[:, 2 * 128 : 3 * 128])
        new[row, half, cut, :] = value
        total = sums[row, half, cut, :]
        total = total + of_near(near)(row, half, cut) * (third - 2.0 * second + first)
        summed[row, half, cut, :] = total + value * (second - 2.0 * first + zeroth)

    block_step(near, of_block(block), model, lane, finish)
    low[...] = new[0:4]
    high[...] = new[ROWS - 4 : ROWS]
    low_cells[...] = new[:, :, 0:8, :]
    high_cells[...] = new[:, :, CELLS - 8 : CELLS, :]


def last_body(
    slots, model_slots, block, below, above, left, right, old, speed_sq, s0, s1, s2, maps,
    u1, u0, u_before, sums, twice, u4, p0, p1, p2, p3, q0, q1, q2, q3, near, new, image,
):
    near[0:4, :, 8 : 8 + CELLS, :] = below[...]
    near[4 : 4 + ROWS, :, 8 : 8 + CELLS, :] = block[...]
    near[4 + ROWS : 8 + ROWS, :, 8 : 8 + CELLS, :] = above[...]
    near[4 : 4 + ROWS, :, 0:8, :] = left[...]
    near[4 : 4 + ROWS, :, 8 + CELLS : SPAN, :] = right[...]
    lane = lanes()

    def finish(row, half, cut, value):
        hits = of_near(maps)(row, half, cut)
        first = of_near(u1)(row, half, cut)
        value = value + (hits[:, 0:128] * first - hits[:, 128:256])
        new[row, half, cut, :] = value
        curvature = first - 2.0 * of_wide(u0)(row, half, cut) + of_near(u_before)(row, half, cut)
        image[row, half, cut, :] = twice[row, half, cut, :] * (sums[row, half, cut, :] + value * curvature)

    block_step(near, of_near(old), (speed_sq, s0, s1, s2), lane, finish)
    write_pieces(model_slots, image, (p0, p1, p2, p3), 0)
    write_pieces(slots, new, (q0, q1, q2, q3), 0)
    write_pieces(slots, u4, (q0, q1, q2, q3), CELLS)


def spread_body(chunks, p0, p1, p2, p3, *outs):
    for turn, piece in enumerate((p0, p1, p2, p3)):
        first = pl.multiple_of(chunks[turn] * CELLS, CELLS)
        for index, out in enumerate(outs):
            out[:, pl.ds(first, CELLS), :] = piece[:, CELLS * index : CELLS * index + CELLS, :]


def sent_pieces(pieces):
    return [pieces[0]] + [send_y(pieces[turn], turn) for turn in (1, 2, 3)]


def to_slabs(pieces, chunks, count):
    return call(spread_body, [shape(4, NY, NZ)] * count, 1, (chunks, *pieces))


def on_device(
    velocity,
    density,
    aperture_start,
    source_cell,
    receiver_cells,
    wavelet,
    observed,
    forward_old,
    forward_now,
    adjoint_later,
    adjoint_now,
):
    shot = lax.axis_index("shot")
    sub = lax.axis_index("sub")
    core = shot % 2
    x_hi = sub // 16
    x = 2 * x_hi + shot // 2
    z = (sub // 4) % 4
    y = sub % 4
    group = sub // 4
    start = aperture_start[0]
    partner = send_core(aperture_start)

    def wanted(first_slab):
        upper = first_slab // 4 + (y < first_slab % 4).astype(jnp.int32)
        block = jnp.clip(x_hi + (upper - z + 3) // 4, 0, 7)
        position = 2 * (block % 2) + block // 4
        return (block // 2) % 2, (position - x) % 4, upper % 4

    own_core, own_step, turn_by = wanted(start)
    turns = jnp.arange(4, dtype=jnp.int32)
    chunks_out = (y + turns) % 4
    chunks_in = (y - turns) % 4
    slots_in = (y - turns - start % 4) % 4
    slots_out = (y + turns - start % 4) % 4

    pieces = cut_pieces(
        [forward_now[0], forward_old[0], adjoint_now[0], adjoint_later[0]],
        (True, True, True, False),
        chunks_out,
    )
    velocity, partner, *pieces = lax.optimization_barrier((velocity, partner, *pieces))
    pair_core, pair_step, _ = wanted(partner[0])

    def gathered(slab, *others):
        from_below = send_x(slab, 1)
        from_above = send_x(slab, -1)
        far = jnp.concatenate([send_x(from_below[0:2], 1), send_x(from_above[2:4], -1)])
        far, *others = lax.optimization_barrier((far, *others))

        def pick(step):
            return jnp.where(
                step < 2, jnp.where(step == 0, slab, from_above), jnp.where(step == 2, far, from_below)
            )

        other = send_core(pick(pair_step))
        return jnp.where(own_core == core, pick(own_step), other), *others

    def turned(arrays, steps):
        def branch(count):
            return lambda *values: tuple(send_z(value, count) if count else value for value in values)

        return lax.switch(steps, [branch(count) for count in (0, 1, 2, -1)], *arrays)

    log_slab, *pieces = gathered(jnp.log(density), *sent_pieces(pieces))
    (speed_slab,) = gathered(velocity)

    def local_place(cells, rows_more, cells_more):
        rows = cells // (NY * NZ) - group * ROWS + rows_more
        columns = (cells // NZ) % NY - y * CELLS + cells_more
        inside = (rows >= 0) & (rows < ROWS + 2 * rows_more)
        inside = inside & (columns >= 0) & (columns < CELLS + 2 * cells_more)
        return inside, rows, (cells // 128) % 2, columns, cells % 128

    inside, rows, half, columns, lane = local_place(receiver_cells[0], 4, 8)
    line = jnp.where(inside, (rows * 2 + half) * SPAN + columns, -1)
    lines = (ROWS + 8) * 2 * SPAN
    on_line = (jnp.arange(lines, dtype=jnp.int32)[:, None] == line[None, :]).astype(F32)
    weights = jnp.concatenate([jnp.ones_like(observed[0, :1]), observed[0]])
    hit = lane[:, None, None] == jnp.arange(128, dtype=jnp.int32)[None, None, :]
    at_lane = jnp.where(hit, weights.T[:, :, None], 0.0).reshape(-1, 5 * 128)
    maps = jnp.dot(on_line, at_lane, precision=lax.Precision.HIGHEST)
    maps = maps.reshape(ROWS + 8, 2, SPAN, 5 * 128)

    def source_place(rows_more, cells_more):
        inside, rows, half, columns, lane = local_place(source_cell[0], rows_more, cells_more)
        rows = jnp.clip(rows, 0, ROWS + 2 * rows_more - 1)
        return [inside.astype(jnp.int32), rows, half, columns, lane]

    place = jnp.stack(source_place(4, 8) + source_place(0, 0))
    amount = wavelet[0]

    steps = (4 - turn_by) % 4
    log_slab, speed_slab = lax.optimization_barrier((log_slab, speed_slab))
    (log_slab,) = turned((log_slab,), steps)
    log_pieces = cut_pieces([log_slab], (True,), chunks_out)
    speed_slab, *log_pieces = lax.optimization_barrier((speed_slab, *log_pieces))
    log_pieces = sent_pieces(log_pieces)
    (speed_slab,) = turned((speed_slab,), steps)
    speed_slab, *log_pieces = lax.optimization_barrier((speed_slab, *log_pieces))
    speed_pieces = sent_pieces(cut_pieces([speed_slab], (True,), chunks_out))
    log_mass, side_low, side_high = gather_blocks(log_pieces, slots_in, (8,))
    log_halo = send_group(side_high, 1), send_group(side_low, -1)
    now, old, adjoint, a_later, side_low, side_high = gather_blocks(pieces, chunks_in, (8, 4, 4, 0))
    below, above = send_group(side_high, 1), send_group(side_low, -1)
    u_wide, old_near, a_near = call(
        fields_body, [WIDE, NEAR, NEAR], 0, (now, old, adjoint, below, above)
    )
    speed, side_low, side_high = gather_blocks(speed_pieces, slots_in, (4,))
    below, above = send_group(side_high, 1), send_group(side_low, -1)
    below, above, maps = lax.optimization_barrier((below, above, maps))
    *model, twice = call(
        model_body, [NEAR] * 4 + [BLOCK], 0, (log_mass, speed, *log_halo, below, above), (WIDE, NEAR)
    )

    u1, u2, *edges = call(
        forward_body, [NEAR, BLOCK] + WIDE_EDGES, 2, (place, amount, u_wide, old_near, *model)
    )
    halo = swap_wide_edges(edges)
    u3, u4, a3, sums, *edges = call(
        turn_body,
        [NEAR, BLOCK, BLOCK, BLOCK] + WIDE_EDGES,
        2,
        (place, amount, u2, *halo, u1, *model, a_near, a_later, maps),
        (WIDE,),
    )
    halo = swap_wide_edges(edges)
    a2, a1, sums, side_low, side_high, low_cells, high_cells = call(
        adjoint_body,
        [NEAR, BLOCK, BLOCK] + [region(4, CELLS)] * 2 + [region(ROWS, 8)] * 2,
        0,
        (a3, *halo, a_near, *model, maps, u3, u2, u1, u_wide, sums),
        (WIDE,),
    )
    halo = (
        send_group(side_high, 1),
        send_group(side_low, -1),
        send_cells(high_cells, 1),
        send_cells(low_cells, -1),
    )
    pieces = call(
        last_body,
        [shape(4, CELLS, NZ)] * 4 + [shape(4, 2 * CELLS, NZ)] * 4,
        2,
        (chunks_out, slots_out, a1, *halo, a2, *model, maps, u1, u_wide, old_near, sums, twice, u4),
        (NEAR, BLOCK, BLOCK),
    )
    pieces = lax.optimization_barrier((*sent_pieces(pieces[:4]), *pieces[4:]))
    (image,) = to_slabs(pieces[:4], chunks_in, 1)

    def both(first_half, second_half):
        return jnp.concatenate([first_half, second_half])

    (image,) = turned((image,), turn_by)
    image, *pieces = lax.optimization_barrier((image, *sent_pieces(pieces[4:])))
    adjoint_first, forward_last = to_slabs(pieces, chunks_in, 2)
    other = send_core(image)

    def share(step):
        mine = jnp.where((own_core == core) & (own_step == step), image, 0.0)
        return mine + jnp.where((pair_core == core) & (pair_step == step), other, 0.0)

    far = share(2)
    passing_up = send_x(far[0:2], 1)
    passing_down = send_x(far[2:4], -1)
    up = share(1)
    down = share(3)
    up = send_x(both(up[0:2] + passing_up, up[2:4]), 1)
    down = send_x(both(down[0:2], down[2:4] + passing_down), -1)
    gradient = share(0) + up + down
    return (gradient, forward_last[None], adjoint_first[None])


def solution(mesh):
    placed = (
        P(("shot", "sub"), None, None),
        P(("shot", "sub"), None, None),
        P("shot"),
        P("shot"),
        P("shot", None),
        P("shot", None),
        P("shot", None, None),
        P("shot", "sub", None, None),
        P("shot", "sub", None, None),
        P("shot", "sub", None, None),
        P("shot", "sub", None, None),
    )
    return jax.shard_map(
        on_device,
        mesh=mesh,
        in_specs=placed,
        out_specs=(
            P(("shot", "sub"), None, None),
            P("shot", "sub", None, None),
            P("shot", "sub", None, None),
        ),
        check_vma=False,
    )
```

```python
import functools

import jax
import jax.numpy as jnp
from jax import lax
from jax.experimental import pallas as pl
from jax.experimental.pallas import tpu as pltpu
from jax.sharding import PartitionSpec as P

lap_coeffs = (-205.0 / 72.0, 8.0 / 5.0, -1.0 / 5.0, 8.0 / 315.0, -1.0 / 560.0)
diff_coeffs = (4.0 / 5.0, -1.0 / 5.0, 4.0 / 105.0, -1.0 / 280.0)
time_step_sq = 0.0088

ROWS = 16
CELLS = 32
SPAN = CELLS + 16
NY = 128
NZ = 256
F32 = jnp.float32
LIMIT = 24 * 2**20


def pairs_by(move):
    pairs = []
    for shot in range(4):
        for sub in range(32):
            x = 2 * (sub // 16) + shot // 2
            target = move(x, shot % 2, (sub // 4) % 4, sub % 4)
            if target is None:
                continue
            tx, tcore, tz, ty = target
            pairs.append((shot * 32 + sub, ((tx % 2) * 2 + tcore) * 32 + (tx // 2) * 16 + tz * 4 + ty))
    return pairs


def send(value, move):
    return lax.ppermute(value, ("shot", "sub"), pairs_by(move))


def send_x(value, steps):
    return send(value, lambda x, c, z, y: ((x + steps) % 4, c, z, y))


def send_core(value):
    return send(value, lambda x, c, z, y: (x, 1 - c, z, y))


def send_z(value, steps):
    return send(value, lambda x, c, z, y: (x, c, (z + steps) % 4, y))


def send_y(value, steps):
    return send(value, lambda x, c, z, y: (x, c, z, (y + steps) % 4))


def next_rows(x, z, steps):
    group = (x // 2) * 4 + z + steps
    if group < 0 or group > 7:
        return None
    return (2 * (group // 4) + x % 2, group % 4)


def send_group(value, steps):
    def move(x, c, z, y):
        place = next_rows(x, z, steps)
        return None if place is None else (place[0], c, place[1], y)

    return send(value, move)


def send_cells(value, steps):
    return send(value, lambda x, c, z, y: (x, c, z, y + steps) if 0 <= y + steps < 4 else None)


def shape(*sizes):
    return jax.ShapeDtypeStruct(sizes, F32)


def region(rows, cells):
    return shape(rows, 2, cells, 128)


BLOCK = region(ROWS, CELLS)
NEAR = region(ROWS + 8, SPAN)
WIDE = region(ROWS + 16, SPAN)


def call(body, outs, n_smem, operands, scratch=()):
    specs = [pl.BlockSpec(memory_space=pltpu.SMEM)] * n_smem
    specs += [pl.BlockSpec(memory_space=pltpu.VMEM)] * (len(operands) - n_smem)
    return pl.pallas_call(
        body,
        out_shape=tuple(outs),
        in_specs=specs,
        out_specs=tuple(pl.BlockSpec(memory_space=pltpu.VMEM) for _ in outs),
        scratch_shapes=[pltpu.VMEM(s.shape, s.dtype) for s in scratch],
        compiler_params=pltpu.CompilerParams(vmem_limit_bytes=LIMIT),
    )(*operands)


def lanes():
    return lax.broadcasted_iota(jnp.int32, (8, 128), 1)


class Stencil:
    def __init__(self, source, row, cell, lane):
        self.source, self.row, self.cell, self.lane = source, row, cell, lane
        self.center = [self.load(0, 0, half) for half in (0, 1)]
        low, high = self.center
        self.deep = []
        for reach in range(1, 5):
            ahead = [pltpu.roll(v, 128 - reach, 1) for v in (low, high)]
            behind = [pltpu.roll(v, reach, 1) for v in (low, high)]
            front = lane < 128 - reach
            back = lane >= reach
            self.deep.append(
                (
                    (jnp.where(front, ahead[0], ahead[1]), jnp.where(front, ahead[1], 0.0)),
                    (jnp.where(back, behind[0], 0.0), jnp.where(back, behind[1], behind[0])),
                )
            )

    def load(self, rows, cells, half):
        first = self.cell + cells
        return self.source[self.row + rows, half, first : first + 8, :]

    def both(self, direction, reach, half):
        if direction == 0:
            return self.load(reach, 0, half), self.load(-reach, 0, half)
        if direction == 1:
            return self.load(0, reach, half), self.load(0, -reach, half)
        ahead, behind = self.deep[reach - 1]
        return ahead[half], behind[half]

    def derivative(self, direction, half):
        ahead, behind = self.both(direction, 1, half)
        total = ahead - behind
        for reach in range(2, 5):
            ahead, behind = self.both(direction, reach, half)
            total = total + (diff_coeffs[reach - 1] / diff_coeffs[0]) * (ahead - behind)
        return total

    def advanced(self, half, previous, speed_sq, slopes):
        center = self.center[half]
        lap = (3.0 * lap_coeffs[0] / lap_coeffs[1]) * center
        derived = [None, None, None]
        for reach in range(1, 5):
            around = None
            for direction in range(3):
                ahead, behind = self.both(direction, reach, half)
                pair = ahead + behind
                around = pair if around is None else around + pair
                part = ahead - behind
                if reach > 1:
                    part = derived[direction] + (diff_coeffs[reach - 1] / diff_coeffs[0]) * part
                derived[direction] = part
            if reach > 1:
                around = (lap_coeffs[reach] / lap_coeffs[1]) * around
            lap = lap + around
        result = 2.0 * center - previous + speed_sq * lap
        for direction in range(3):
            result = result - slopes[direction] * derived[direction]
        return result


def row_pairs(visit, first, last, cells):
    def step(pair, carry):
        for row in (first + 2 * pair, first + 2 * pair + 1):
            for cell in cells:
                visit(row, cell)
        return carry

    lax.fori_loop(0, (last - first) // 2, step, 0)


def over_block(visit):
    row_pairs(visit, 0, ROWS, range(0, CELLS, 8))


def over_near(visit):
    sides, middle = range(8, 8 + CELLS, 8), range(4, 12 + CELLS, 8)
    row_pairs(visit, 0, 4, sides)
    row_pairs(visit, 4, 4 + ROWS, middle)
    row_pairs(visit, 4 + ROWS, 8 + ROWS, sides)


def add_source(place, amount, first, target):
    @pl.when(place[first] > 0)
    def _():
        row, half = place[first + 1], place[first + 2]
        values = target[row, half]
        cell = lax.broadcasted_iota(jnp.int32, values.shape, 0)
        lane = lax.broadcasted_iota(jnp.int32, values.shape, 1)
        hit = (cell == place[first + 3]) & (lane == place[first + 4])
        target[row, half] = values + jnp.where(hit, amount, 0.0)


def near_step(source, old, model, lane, out, extra=None):
    speed_sq, slopes = model[0], model[1:]

    def visit(row, cell):
        stencil = Stencil(source, row + 4, cell, lane)
        cut = slice(cell, cell + 8)
        for half in (0, 1):
            value = stencil.advanced(
                half,
                old[row, half, cut, :],
                speed_sq[row, half, cut, :],
                [s[row, half, cut, :] for s in slopes],
            )
            if extra is not None:
                value = value + extra(row, half, cut)
            out[row, half, cut, :] = value

    over_near(visit)


def block_step(source, old, model, lane, finish):
    speed_sq, slopes = model[0], model[1:]

    def visit(row, cell):
        stencil = Stencil(source, row + 4, cell + 8, lane)
        near = slice(cell + 8, cell + 16)
        for half in (0, 1):
            value = stencil.advanced(
                half,
                old(row, half, slice(cell, cell + 8)),
                speed_sq[row + 4, half, near, :],
                [s[row + 4, half, near, :] for s in slopes],
            )
            finish(row, half, slice(cell, cell + 8), value)

    over_block(visit)


def of_block(ref):
    return lambda row, half, cut: ref[row, half, cut, :]


def of_near(ref):
    return lambda row, half, cut: ref[row + 4, half, cut.start + 8 : cut.stop + 8, :]


def of_wide(ref):
    return lambda row, half, cut: ref[row + 8, half, cut.start + 8 : cut.stop + 8, :]


def injected(maps, index, field):
    def near(row, half, cut):
        hits = maps[row, half, cut, 0:128]
        seen = maps[row, half, cut, 128 * index : 128 * index + 128]
        return hits * field[row, half, cut, :] - seen

    return near


def fill_wide(wide, block, halo):
    below, above, left, right, left_corners, right_corners = halo
    wide[0:8, :, 8 : 8 + CELLS, :] = below[...]
    wide[8 : 8 + ROWS, :, 8 : 8 + CELLS, :] = block[...]
    wide[8 + ROWS : 16 + ROWS, :, 8 : 8 + CELLS, :] = above[...]
    for cells, side, corners in (
        (slice(0, 8), left, left_corners),
        (slice(8 + CELLS, SPAN), right, right_corners),
    ):
        wide[4:8, :, cells, :] = corners[0:4]
        wide[8 : 8 + ROWS, :, cells, :] = side[...]
        wide[8 + ROWS : 12 + ROWS, :, cells, :] = corners[4:8]


WIDE_EDGES = [region(8, CELLS)] * 2 + [region(ROWS, 8)] * 2


def write_wide_edges(block, edges):
    low, high, low_cells, high_cells = edges
    low[...] = block[0:8]
    high[...] = block[ROWS - 8 : ROWS]
    low_cells[...] = block[:, :, 0:8, :]
    high_cells[...] = block[:, :, CELLS - 8 : CELLS, :]


def rim_body(below, above, low, high):
    for out, cut in ((low, slice(0, 8)), (high, slice(CELLS - 8, CELLS))):
        out[0:4] = below[4:8, :, cut, :]
        out[4:8] = above[0:4, :, cut, :]


def swap_wide_edges(edges):
    low, high, low_cells, high_cells = edges
    below, above = send_group(high, 1), send_group(low, -1)
    left, right = send_cells(high_cells, 1), send_cells(low_cells, -1)
    low_corners, high_corners = call(rim_body, [region(8, 8)] * 2, 0, (below, above))
    return below, above, left, right, send_cells(high_corners, 1), send_cells(low_corners, -1)


def cut_body(chunks, *refs, margins):
    count = len(margins)
    slabs, pieces = refs[:count], refs[count:]
    for turn in range(4):
        chunk = chunks[turn]
        first = pl.multiple_of(chunk * CELLS, CELLS)
        before = pl.multiple_of(jnp.maximum(first - 8, 0), 8)
        after = pl.multiple_of(jnp.minimum(first + CELLS, NY - 8), 8)
        at = 0
        for slab, margin in zip(slabs, margins):
            if margin:
                pieces[turn][:, at : at + 8, :] = jnp.where(chunk > 0, slab[:, pl.ds(before, 8), :], 0.0)
                at += 8
            pieces[turn][:, at : at + CELLS, :] = slab[:, pl.ds(first, CELLS), :]
            at += CELLS
            if margin:
                pieces[turn][:, at : at + 8, :] = jnp.where(chunk < 3, slab[:, pl.ds(after, 8), :], 0.0)
                at += 8


def cut_pieces(slabs, margins, chunks):
    width = sum(SPAN if margin else CELLS for margin in margins)
    pieces = call(functools.partial(cut_body, margins=margins), [shape(4, width, NZ)] * 4, 1, (chunks, *slabs))
    return pieces


def place_pieces(slots, pieces, outs):
    for turn in range(4):
        slot = pl.multiple_of(slots[turn] * 4, 4)
        at = 0
        for out in outs:
            width = out.shape[2]
            for half in (0, 1):
                out[pl.ds(slot, 4), half] = pieces[turn][:, at : at + width, 128 * half : 128 * half + 128]
            at += width


def gather_body(slots, *refs, depths):
    pieces, outs = refs[:4], refs[4:]
    low, high = outs[-2:]
    place_pieces(slots, pieces, outs[:-2])
    at = 0
    core = slice(8, 8 + CELLS)
    for out, depth in zip(outs, depths):
        if depth == 8:
            low[:, :, at : at + SPAN, :] = out[0:4]
            high[:, :, at : at + SPAN, :] = out[ROWS - 4 : ROWS]
            at += SPAN
            low[:, :, at : at + CELLS, :] = out[4:8, :, core, :]
            high[:, :, at : at + CELLS, :] = out[ROWS - 8 : ROWS - 4, :, core, :]
            at += CELLS
        elif depth == 4:
            low[:, :, at : at + CELLS, :] = out[0:4, :, core, :]
            high[:, :, at : at + CELLS, :] = out[ROWS - 4 : ROWS, :, core, :]
            at += CELLS


def gather_blocks(pieces, slots, depths):
    outs = [region(ROWS, SPAN if depth else CELLS) for depth in depths]
    packed = sum({8: SPAN + CELLS, 4: CELLS, 0: 0}[depth] for depth in depths)
    outs += [region(4, packed)] * 2
    return call(functools.partial(gather_body, depths=depths), outs, 1, (slots, *pieces))


def stack_wide(out, below, middle, above, at):
    core = slice(8, 8 + CELLS)
    end = at + SPAN + CELLS
    out[0:4, :, core, :] = below[:, :, at + SPAN : end, :]
    out[4:8] = below[:, :, at : at + SPAN, :]
    out[8 : 8 + ROWS] = middle[...]
    out[8 + ROWS : 12 + ROWS] = above[:, :, at : at + SPAN, :]
    out[12 + ROWS : 16 + ROWS, :, core, :] = above[:, :, at + SPAN : end, :]


def stack_near(out, below, middle, above, at):
    core = slice(8, 8 + CELLS)
    out[0:4, :, core, :] = below[:, :, at : at + CELLS, :]
    out[4 : 4 + ROWS] = middle[...]
    out[4 + ROWS : 8 + ROWS, :, core, :] = above[:, :, at : at + CELLS, :]


def fields_body(now, old, adjoint, below, above, wide, old_near, adjoint_near):
    stack_wide(wide, below, now, above, 0)
    stack_near(old_near, below, old, above, SPAN + CELLS)
    stack_near(adjoint_near, below, adjoint, above, SPAN + 2 * CELLS)


def model_body(log_mass, speed, below, above, speed_sq, s0, s1, s2, twice, wide, speed_near):
    stack_wide(wide, below, log_mass, above, 0)
    stack_near(speed_near, below, speed, above, SPAN + CELLS)
    twice[...] = 2.0 / speed[:, :, 8 : 8 + CELLS, :]
    lane = lanes()

    def visit(row, cell):
        stencil = Stencil(wide, row + 4, cell, lane)
        cut = slice(cell, cell + 8)
        for half in (0, 1):
            value = speed_near[row, half, cut, :]
            scale = time_step_sq * value * value
            speed_sq[row, half, cut, :] = lap_coeffs[1] * scale
            scale = (diff_coeffs[0] * diff_coeffs[0]) * scale
            for direction, out in enumerate((s0, s1, s2)):
                out[row, half, cut, :] = scale * stencil.derivative(direction, half)

    over_near(visit)


def forward_body(place, amount, wide, old, speed_sq, s0, s1, s2, near, new, *edges):
    model = (speed_sq, s0, s1, s2)
    lane = lanes()
    near_step(wide, old, model, lane, near)
    add_source(place, amount[0], 0, near)

    def finish(row, half, cut, value):
        new[row, half, cut, :] = value

    block_step(near, of_wide(wide), model, lane, finish)
    add_source(place, amount[1], 5, new)
    write_wide_edges(new, edges)


def write_pieces(slots, block, pieces, at):
    for turn in range(4):
        slot = pl.multiple_of(slots[turn] * 4, 4)
        for half in (0, 1):
            pieces[turn][:, at : at + CELLS, 128 * half : 128 * half + 128] = block[pl.ds(slot, 4), half]


def turn_body(place, amount, block, *refs):
    halo, refs = refs[:6], refs[6:]
    old, speed_sq, s0, s1, s2, adjoint, later, maps, near, new, adjoint_new, summed = refs[:12]
    edges, wide = refs[12:16], refs[16]
    model = (speed_sq, s0, s1, s2)
    lane = lanes()
    fill_wide(wide, block, halo)
    near_step(wide, old, model, lane, near)
    add_source(place, amount[2], 0, near)

    def finish(row, half, cut, value):
        new[row, half, cut, :] = value

    block_step(near, of_block(block), model, lane, finish)
    add_source(place, amount[3], 5, new)

    def finish_adjoint(row, half, cut, value):
        hits = of_near(maps)(row, half, cut)
        ahead = new[row, half, cut, :]
        value = value + (hits[:, 0:128] * ahead - hits[:, 4 * 128 : 5 * 128])
        adjoint_new[row, half, cut, :] = value
        summed[row, half, cut, :] = value * (
            ahead - 2.0 * of_near(near)(row, half, cut) + block[row, half, cut, :]
        )

    block_step(adjoint, of_block(later), model, lane, finish_adjoint)
    write_wide_edges(adjoint_new, edges)


def adjoint_body(block, *refs):
    halo, refs = refs[:6], refs[6:]
    old, speed_sq, s0, s1, s2, maps, u3, u2, u1, u0, sums = refs[:11]
    near, new, summed, low, high, low_cells, high_cells, wide = refs[11:]
    model = (speed_sq, s0, s1, s2)
    lane = lanes()
    fill_wide(wide, block, halo)
    near_step(wide, old, model, lane, near, injected(maps, 3, u3))

    def finish(row, half, cut, value):
        hits = of_near(maps)(row, half, cut)
        third = of_near(u3)(row, half, cut)
        second = u2[row, half, cut, :]
        first = of_near(u1)(row, half, cut)
        zeroth = of_wide(u0)(row, half, cut)
        value = value + (hits[:, 0:128] * second - hits[:, 2 * 128 : 3 * 128])
        new[row, half, cut, :] = value
        total = sums[row, half, cut, :]
        total = total + of_near(near)(row, half, cut) * (third - 2.0 * second + first)
        summed[row, half, cut, :] = total + value * (second - 2.0 * first + zeroth)

    block_step(near, of_block(block), model, lane, finish)
    low[...] = new[0:4]
    high[...] = new[ROWS - 4 : ROWS]
    low_cells[...] = new[:, :, 0:8, :]
    high_cells[...] = new[:, :, CELLS - 8 : CELLS, :]


def last_body(
    slots, model_slots, block, below, above, left, right, old, speed_sq, s0, s1, s2, maps,
    u1, u0, u_before, sums, twice, u4, p0, p1, p2, p3, q0, q1, q2, q3, near, new, image,
):
    near[0:4, :, 8 : 8 + CELLS, :] = below[...]
    near[4 : 4 + ROWS, :, 8 : 8 + CELLS, :] = block[...]
    near[4 + ROWS : 8 + ROWS, :, 8 : 8 + CELLS, :] = above[...]
    near[4 : 4 + ROWS, :, 0:8, :] = left[...]
    near[4 : 4 + ROWS, :, 8 + CELLS : SPAN, :] = right[...]
    lane = lanes()

    def finish(row, half, cut, value):
        hits = of_near(maps)(row, half, cut)
        first = of_near(u1)(row, half, cut)
        value = value + (hits[:, 0:128] * first - hits[:, 128:256])
        new[row, half, cut, :] = value
        curvature = first - 2.0 * of_wide(u0)(row, half, cut) + of_near(u_before)(row, half, cut)
        image[row, half, cut, :] = twice[row, half, cut, :] * (sums[row, half, cut, :] + value * curvature)

    block_step(near, of_near(old), (speed_sq, s0, s1, s2), lane, finish)
    write_pieces(model_slots, image, (p0, p1, p2, p3), 0)
    write_pieces(slots, new, (q0, q1, q2, q3), 0)
    write_pieces(slots, u4, (q0, q1, q2, q3), CELLS)


def spread_body(chunks, p0, p1, p2, p3, *outs):
    for turn, piece in enumerate((p0, p1, p2, p3)):
        first = pl.multiple_of(chunks[turn] * CELLS, CELLS)
        for index, out in enumerate(outs):
            out[:, pl.ds(first, CELLS), :] = piece[:, CELLS * index : CELLS * index + CELLS, :]


def sent_pieces(pieces):
    return [pieces[0]] + [send_y(pieces[turn], turn) for turn in (1, 2, 3)]


def to_slabs(pieces, chunks, count):
    return call(spread_body, [shape(4, NY, NZ)] * count, 1, (chunks, *pieces))


def on_device(
    velocity,
    density,
    aperture_start,
    source_cell,
    receiver_cells,
    wavelet,
    observed,
    forward_old,
    forward_now,
    adjoint_later,
    adjoint_now,
):
    shot = lax.axis_index("shot")
    sub = lax.axis_index("sub")
    core = shot % 2
    x_hi = sub // 16
    x = 2 * x_hi + shot // 2
    z = (sub // 4) % 4
    y = sub % 4
    group = sub // 4
    start = aperture_start[0]
    partner = send_core(aperture_start)

    def wanted(first_slab):
        upper = first_slab // 4 + (y < first_slab % 4).astype(jnp.int32)
        block = jnp.clip(x_hi + (upper - z + 3) // 4, 0, 7)
        position = 2 * (block % 2) + block // 4
        return (block // 2) % 2, (position - x) % 4, upper % 4

    own_core, own_step, turn_by = wanted(start)
    turns = jnp.arange(4, dtype=jnp.int32)
    chunks_out = (y + turns) % 4
    chunks_in = (y - turns) % 4
    slots_in = (y - turns - start % 4) % 4
    slots_out = (y + turns - start % 4) % 4

    pieces = cut_pieces(
        [forward_now[0], forward_old[0], adjoint_now[0], adjoint_later[0]],
        (True, True, True, False),
        chunks_out,
    )
    pair_core, pair_step, _ = wanted(partner[0])

    def gathered(slab, *others):
        from_below = send_x(slab, 1)
        from_above = send_x(slab, -1)
        passing = from_below[0:2], from_above[2:4]
        if others:
            first, second, from_below, from_above, *others = lax.optimization_barrier(
                (*passing, from_below, from_above, *others)
            )
            passing = first, second
        far = jnp.concatenate([send_x(passing[0], 1), send_x(passing[1], -1)])

        def pick(step):
            return jnp.where(
                step < 2, jnp.where(step == 0, slab, from_above), jnp.where(step == 2, far, from_below)
            )

        other = send_core(pick(pair_step))
        return jnp.where(own_core == core, pick(own_step), other), *others

    def turned(arrays, steps):
        def branch(count):
            return lambda *values: tuple(send_z(value, count) if count else value for value in values)

        return lax.switch(steps, [branch(count) for count in (0, 1, 2, -1)], *arrays)

    log_slab, *pieces = gathered(jnp.log(density), *pieces)
    (speed_slab,) = gathered(velocity)
    pieces = sent_pieces(pieces)

    def local_place(cells, rows_more, cells_more):
        rows = cells // (NY * NZ) - group * ROWS + rows_more
        columns = (cells // NZ) % NY - y * CELLS + cells_more
        inside = (rows >= 0) & (rows < ROWS + 2 * rows_more)
        inside = inside & (columns >= 0) & (columns < CELLS + 2 * cells_more)
        return inside, rows, (cells // 128) % 2, columns, cells % 128

    inside, rows, half, columns, lane = local_place(receiver_cells[0], 4, 8)
    line = jnp.where(inside, (rows * 2 + half) * SPAN + columns, -1)
    lines = (ROWS + 8) * 2 * SPAN
    on_line = (jnp.arange(lines, dtype=jnp.int32)[:, None] == line[None, :]).astype(F32)
    weights = jnp.concatenate([jnp.ones_like(observed[0, :1]), observed[0]])
    hit = lane[:, None, None] == jnp.arange(128, dtype=jnp.int32)[None, None, :]
    at_lane = jnp.where(hit, weights.T[:, :, None], 0.0).reshape(-1, 5 * 128)
    maps = jnp.dot(on_line, at_lane, precision=lax.Precision.HIGHEST)
    maps = maps.reshape(ROWS + 8, 2, SPAN, 5 * 128)

    def source_place(rows_more, cells_more):
        inside, rows, half, columns, lane = local_place(source_cell[0], rows_more, cells_more)
        rows = jnp.clip(rows, 0, ROWS + 2 * rows_more - 1)
        return [inside.astype(jnp.int32), rows, half, columns, lane]

    place = jnp.stack(source_place(4, 8) + source_place(0, 0))
    amount = wavelet[0]

    log_slab, speed_slab = lax.optimization_barrier((log_slab, speed_slab))
    log_slab, speed_slab = turned((log_slab, speed_slab), (4 - turn_by) % 4)
    log_slab, speed_slab, *pieces = lax.optimization_barrier((log_slab, speed_slab, *pieces))
    model_pieces = sent_pieces(cut_pieces([log_slab, speed_slab], (True, True), chunks_out))
    now, old, adjoint, a_later, side_low, side_high = gather_blocks(pieces, chunks_in, (8, 4, 4, 0))
    below, above = send_group(side_high, 1), send_group(side_low, -1)
    u_wide, old_near, a_near = call(
        fields_body, [WIDE, NEAR, NEAR], 0, (now, old, adjoint, below, above)
    )
    log_mass, speed, side_low, side_high = gather_blocks(model_pieces, slots_in, (8, 4))
    below, above = send_group(side_high, 1), send_group(side_low, -1)
    below, above, maps = lax.optimization_barrier((below, above, maps))
    *model, twice = call(
        model_body, [NEAR] * 4 + [BLOCK], 0, (log_mass, speed, below, above), (WIDE, NEAR)
    )

    u1, u2, *edges = call(
        forward_body, [NEAR, BLOCK] + WIDE_EDGES, 2, (place, amount, u_wide, old_near, *model)
    )
    halo = swap_wide_edges(edges)
    u3, u4, a3, sums, *edges = call(
        turn_body,
        [NEAR, BLOCK, BLOCK, BLOCK] + WIDE_EDGES,
        2,
        (place, amount, u2, *halo, u1, *model, a_near, a_later, maps),
        (WIDE,),
    )
    halo = swap_wide_edges(edges)
    a2, a1, sums, side_low, side_high, low_cells, high_cells = call(
        adjoint_body,
        [NEAR, BLOCK, BLOCK] + [region(4, CELLS)] * 2 + [region(ROWS, 8)] * 2,
        0,
        (a3, *halo, a_near, *model, maps, u3, u2, u1, u_wide, sums),
        (WIDE,),
    )
    halo = (
        send_group(side_high, 1),
        send_group(side_low, -1),
        send_cells(high_cells, 1),
        send_cells(low_cells, -1),
    )
    pieces = call(
        last_body,
        [shape(4, CELLS, NZ)] * 4 + [shape(4, 2 * CELLS, NZ)] * 4,
        2,
        (chunks_out, slots_out, a1, *halo, a2, *model, maps, u1, u_wide, old_near, sums, twice, u4),
        (NEAR, BLOCK, BLOCK),
    )
    pieces = lax.optimization_barrier((*sent_pieces(pieces[:4]), *pieces[4:]))
    (image,) = to_slabs(pieces[:4], chunks_in, 1)

    def both(first_half, second_half):
        return jnp.concatenate([first_half, second_half])

    (image,) = turned((image,), turn_by)
    image, *pieces = lax.optimization_barrier((image, *sent_pieces(pieces[4:])))
    adjoint_first, forward_last = to_slabs(pieces, chunks_in, 2)
    other = send_core(image)

    def share(step):
        mine = jnp.where((own_core == core) & (own_step == step), image, 0.0)
        return mine + jnp.where((pair_core == core) & (pair_step == step), other, 0.0)

    far = share(2)
    passing_up = send_x(far[0:2], 1)
    passing_down = send_x(far[2:4], -1)
    up = share(1)
    down = share(3)
    up = send_x(both(up[0:2] + passing_up, up[2:4]), 1)
    down = send_x(both(down[0:2], down[2:4] + passing_down), -1)
    gradient = share(0) + up + down
    return (gradient, forward_last[None], adjoint_first[None])


def solution(mesh):
    placed = (
        P(("shot", "sub"), None, None),
        P(("shot", "sub"), None, None),
        P("shot"),
        P("shot"),
        P("shot", None),
        P("shot", None),
        P("shot", None, None),
        P("shot", "sub", None, None),
        P("shot", "sub", None, None),
        P("shot", "sub", None, None),
        P("shot", "sub", None, None),
    )
    return jax.shard_map(
        on_device,
        mesh=mesh,
        in_specs=placed,
        out_specs=(
            P(("shot", "sub"), None, None),
            P("shot", "sub", None, None),
            P("shot", "sub", None, None),
        ),
        check_vma=False,
    )
```

```python
import functools

import jax
import jax.numpy as jnp
from jax import lax
from jax.experimental import pallas as pl
from jax.experimental.pallas import tpu as pltpu
from jax.sharding import PartitionSpec as P

lap_coeffs = (-205.0 / 72.0, 8.0 / 5.0, -1.0 / 5.0, 8.0 / 315.0, -1.0 / 560.0)
diff_coeffs = (4.0 / 5.0, -1.0 / 5.0, 4.0 / 105.0, -1.0 / 280.0)
time_step_sq = 0.0088

ROWS = 16
CELLS = 32
SPAN = CELLS + 16
NY = 128
NZ = 256
F32 = jnp.float32
LIMIT = 24 * 2**20


def pairs_by(move):
    pairs = []
    for shot in range(4):
        for sub in range(32):
            x = 2 * (sub // 16) + shot // 2
            target = move(x, shot % 2, (sub // 4) % 4, sub % 4)
            if target is None:
                continue
            tx, tcore, tz, ty = target
            pairs.append((shot * 32 + sub, ((tx % 2) * 2 + tcore) * 32 + (tx // 2) * 16 + tz * 4 + ty))
    return pairs


def send(value, move):
    return lax.ppermute(value, ("shot", "sub"), pairs_by(move))


def send_x(value, steps):
    return send(value, lambda x, c, z, y: ((x + steps) % 4, c, z, y))


def send_core(value):
    return send(value, lambda x, c, z, y: (x, 1 - c, z, y))


def send_z(value, steps):
    return send(value, lambda x, c, z, y: (x, c, (z + steps) % 4, y))


def send_y(value, steps):
    return send(value, lambda x, c, z, y: (x, c, z, (y + steps) % 4))


def next_rows(x, z, steps):
    group = (x // 2) * 4 + z + steps
    if group < 0 or group > 7:
        return None
    return (2 * (group // 4) + x % 2, group % 4)


def send_group(value, steps):
    def move(x, c, z, y):
        place = next_rows(x, z, steps)
        return None if place is None else (place[0], c, place[1], y)

    return send(value, move)


def send_cells(value, steps):
    return send(value, lambda x, c, z, y: (x, c, z, y + steps) if 0 <= y + steps < 4 else None)


def shape(*sizes):
    return jax.ShapeDtypeStruct(sizes, F32)


def region(rows, cells):
    return shape(rows, 2, cells, 128)


BLOCK = region(ROWS, CELLS)
NEAR = region(ROWS + 8, SPAN)
WIDE = region(ROWS + 16, SPAN)


def call(body, outs, n_smem, operands, scratch=()):
    specs = [pl.BlockSpec(memory_space=pltpu.SMEM)] * n_smem
    specs += [pl.BlockSpec(memory_space=pltpu.VMEM)] * (len(operands) - n_smem)
    return pl.pallas_call(
        body,
        out_shape=tuple(outs),
        in_specs=specs,
        out_specs=tuple(pl.BlockSpec(memory_space=pltpu.VMEM) for _ in outs),
        scratch_shapes=[pltpu.VMEM(s.shape, s.dtype) for s in scratch],
        compiler_params=pltpu.CompilerParams(vmem_limit_bytes=LIMIT),
    )(*operands)


def lanes():
    return lax.broadcasted_iota(jnp.int32, (8, 128), 1)


class Stencil:
    def __init__(self, source, row, cell, lane):
        self.source, self.row, self.cell, self.lane = source, row, cell, lane
        self.center = [self.load(0, 0, half) for half in (0, 1)]
        low, high = self.center
        self.deep = []
        for reach in range(1, 5):
            ahead = [pltpu.roll(v, 128 - reach, 1) for v in (low, high)]
            behind = [pltpu.roll(v, reach, 1) for v in (low, high)]
            front = lane < 128 - reach
            back = lane >= reach
            self.deep.append(
                (
                    (jnp.where(front, ahead[0], ahead[1]), jnp.where(front, ahead[1], 0.0)),
                    (jnp.where(back, behind[0], 0.0), jnp.where(back, behind[1], behind[0])),
                )
            )

    def load(self, rows, cells, half):
        first = self.cell + cells
        return self.source[self.row + rows, half, first : first + 8, :]

    def both(self, direction, reach, half):
        if direction == 0:
            return self.load(reach, 0, half), self.load(-reach, 0, half)
        if direction == 1:
            return self.load(0, reach, half), self.load(0, -reach, half)
        ahead, behind = self.deep[reach - 1]
        return ahead[half], behind[half]

    def derivative(self, direction, half):
        ahead, behind = self.both(direction, 1, half)
        total = ahead - behind
        for reach in range(2, 5):
            ahead, behind = self.both(direction, reach, half)
            total = total + (diff_coeffs[reach - 1] / diff_coeffs[0]) * (ahead - behind)
        return total

    def advanced(self, half, previous, speed_sq, slopes):
        center = self.center[half]
        lap = (3.0 * lap_coeffs[0] / lap_coeffs[1]) * center
        derived = [None, None, None]
        for reach in range(1, 5):
            around = None
            for direction in range(3):
                ahead, behind = self.both(direction, reach, half)
                pair = ahead + behind
                around = pair if around is None else around + pair
                part = ahead - behind
                if reach > 1:
                    part = derived[direction] + (diff_coeffs[reach - 1] / diff_coeffs[0]) * part
                derived[direction] = part
            if reach > 1:
                around = (lap_coeffs[reach] / lap_coeffs[1]) * around
            lap = lap + around
        result = 2.0 * center - previous + speed_sq * lap
        for direction in range(3):
            result = result - slopes[direction] * derived[direction]
        return result


def row_pairs(visit, first, last, cells):
    def step(pair, carry):
        for row in (first + 2 * pair, first + 2 * pair + 1):
            for cell in cells:
                visit(row, cell)
        return carry

    lax.fori_loop(0, (last - first) // 2, step, 0)


def over_block(visit):
    row_pairs(visit, 0, ROWS, range(0, CELLS, 8))


def over_near(visit):
    sides, middle = range(8, 8 + CELLS, 8), range(4, 12 + CELLS, 8)
    row_pairs(visit, 0, 4, sides)
    row_pairs(visit, 4, 4 + ROWS, middle)
    row_pairs(visit, 4 + ROWS, 8 + ROWS, sides)


def add_source(place, amount, first, target):
    @pl.when(place[first] > 0)
    def _():
        row, half = place[first + 1], place[first + 2]
        values = target[row, half]
        cell = lax.broadcasted_iota(jnp.int32, values.shape, 0)
        lane = lax.broadcasted_iota(jnp.int32, values.shape, 1)
        hit = (cell == place[first + 3]) & (lane == place[first + 4])
        target[row, half] = values + jnp.where(hit, amount, 0.0)


def near_step(source, old, model, lane, out, extra=None):
    speed_sq, slopes = model[0], model[1:]

    def visit(row, cell):
        stencil = Stencil(source, row + 4, cell, lane)
        cut = slice(cell, cell + 8)
        for half in (0, 1):
            value = stencil.advanced(
                half,
                old[row, half, cut, :],
                speed_sq[row, half, cut, :],
                [s[row, half, cut, :] for s in slopes],
            )
            if extra is not None:
                value = value + extra(row, half, cut)
            out[row, half, cut, :] = value

    over_near(visit)


def block_step(source, old, model, lane, finish):
    speed_sq, slopes = model[0], model[1:]

    def visit(row, cell):
        stencil = Stencil(source, row + 4, cell + 8, lane)
        near = slice(cell + 8, cell + 16)
        for half in (0, 1):
            value = stencil.advanced(
                half,
                old(row, half, slice(cell, cell + 8)),
                speed_sq[row + 4, half, near, :],
                [s[row + 4, half, near, :] for s in slopes],
            )
            finish(row, half, slice(cell, cell + 8), value)

    over_block(visit)


def of_block(ref):
    return lambda row, half, cut: ref[row, half, cut, :]


def of_near(ref):
    return lambda row, half, cut: ref[row + 4, half, cut.start + 8 : cut.stop + 8, :]


def of_wide(ref):
    return lambda row, half, cut: ref[row + 8, half, cut.start + 8 : cut.stop + 8, :]


def injected(maps, index, field):
    def near(row, half, cut):
        hits = maps[row, half, cut, 0:128]
        seen = maps[row, half, cut, 128 * index : 128 * index + 128]
        return hits * field[row, half, cut, :] - seen

    return near


def fill_wide(wide, block, halo):
    below, above, left, right, left_corners, right_corners = halo
    wide[0:8, :, 8 : 8 + CELLS, :] = below[...]
    wide[8 : 8 + ROWS, :, 8 : 8 + CELLS, :] = block[...]
    wide[8 + ROWS : 16 + ROWS, :, 8 : 8 + CELLS, :] = above[...]
    for cells, side, corners in (
        (slice(0, 8), left, left_corners),
        (slice(8 + CELLS, SPAN), right, right_corners),
    ):
        wide[4:8, :, cells, :] = corners[0:4]
        wide[8 : 8 + ROWS, :, cells, :] = side[...]
        wide[8 + ROWS : 12 + ROWS, :, cells, :] = corners[4:8]


WIDE_EDGES = [region(8, CELLS)] * 2 + [region(ROWS, 8)] * 2


def write_wide_edges(block, edges):
    low, high, low_cells, high_cells = edges
    low[...] = block[0:8]
    high[...] = block[ROWS - 8 : ROWS]
    low_cells[...] = block[:, :, 0:8, :]
    high_cells[...] = block[:, :, CELLS - 8 : CELLS, :]


def rim_body(below, above, low, high):
    for out, cut in ((low, slice(0, 8)), (high, slice(CELLS - 8, CELLS))):
        out[0:4] = below[4:8, :, cut, :]
        out[4:8] = above[0:4, :, cut, :]


def swap_wide_edges(edges):
    low, high, low_cells, high_cells = edges
    below, above = send_group(high, 1), send_group(low, -1)
    left, right = send_cells(high_cells, 1), send_cells(low_cells, -1)
    low_corners, high_corners = call(rim_body, [region(8, 8)] * 2, 0, (below, above))
    return below, above, left, right, send_cells(high_corners, 1), send_cells(low_corners, -1)


def cut_body(chunks, *refs, margins):
    count = len(margins)
    slabs, pieces = refs[:count], refs[count:]
    for turn in range(4):
        chunk = chunks[turn]
        first = pl.multiple_of(chunk * CELLS, CELLS)
        before = pl.multiple_of(jnp.maximum(first - 8, 0), 8)
        after = pl.multiple_of(jnp.minimum(first + CELLS, NY - 8), 8)
        at = 0
        for slab, margin in zip(slabs, margins):
            if margin:
                pieces[turn][:, at : at + 8, :] = jnp.where(chunk > 0, slab[:, pl.ds(before, 8), :], 0.0)
                at += 8
            pieces[turn][:, at : at + CELLS, :] = slab[:, pl.ds(first, CELLS), :]
            at += CELLS
            if margin:
                pieces[turn][:, at : at + 8, :] = jnp.where(chunk < 3, slab[:, pl.ds(after, 8), :], 0.0)
                at += 8


def cut_pieces(slabs, margins, chunks):
    width = sum(SPAN if margin else CELLS for margin in margins)
    pieces = call(functools.partial(cut_body, margins=margins), [shape(4, width, NZ)] * 4, 1, (chunks, *slabs))
    return pieces


def place_pieces(slots, pieces, outs):
    for turn in range(4):
        slot = pl.multiple_of(slots[turn] * 4, 4)
        at = 0
        for out in outs:
            width = out.shape[2]
            for half in (0, 1):
                out[pl.ds(slot, 4), half] = pieces[turn][:, at : at + width, 128 * half : 128 * half + 128]
            at += width


def gather_body(slots, *refs, depths):
    pieces, outs = refs[:4], refs[4:]
    low, high = outs[-2:]
    place_pieces(slots, pieces, outs[:-2])
    at = 0
    core = slice(8, 8 + CELLS)
    for out, depth in zip(outs, depths):
        if depth == 8:
            low[:, :, at : at + SPAN, :] = out[0:4]
            high[:, :, at : at + SPAN, :] = out[ROWS - 4 : ROWS]
            at += SPAN
            low[:, :, at : at + CELLS, :] = out[4:8, :, core, :]
            high[:, :, at : at + CELLS, :] = out[ROWS - 8 : ROWS - 4, :, core, :]
            at += CELLS
        elif depth == 4:
            low[:, :, at : at + CELLS, :] = out[0:4, :, core, :]
            high[:, :, at : at + CELLS, :] = out[ROWS - 4 : ROWS, :, core, :]
            at += CELLS


def gather_blocks(pieces, slots, depths):
    outs = [region(ROWS, SPAN if depth else CELLS) for depth in depths]
    packed = sum({8: SPAN + CELLS, 4: CELLS, 0: 0}[depth] for depth in depths)
    outs += [region(4, packed)] * 2
    return call(functools.partial(gather_body, depths=depths), outs, 1, (slots, *pieces))


def stack_wide(out, below, middle, above, at):
    core = slice(8, 8 + CELLS)
    end = at + SPAN + CELLS
    out[0:4, :, core, :] = below[:, :, at + SPAN : end, :]
    out[4:8] = below[:, :, at : at + SPAN, :]
    out[8 : 8 + ROWS] = middle[...]
    out[8 + ROWS : 12 + ROWS] = above[:, :, at : at + SPAN, :]
    out[12 + ROWS : 16 + ROWS, :, core, :] = above[:, :, at + SPAN : end, :]


def stack_near(out, below, middle, above, at):
    core = slice(8, 8 + CELLS)
    out[0:4, :, core, :] = below[:, :, at : at + CELLS, :]
    out[4 : 4 + ROWS] = middle[...]
    out[4 + ROWS : 8 + ROWS, :, core, :] = above[:, :, at : at + CELLS, :]


def fields_body(now, old, adjoint, below, above, wide, old_near, adjoint_near):
    stack_wide(wide, below, now, above, 0)
    stack_near(old_near, below, old, above, SPAN + CELLS)
    stack_near(adjoint_near, below, adjoint, above, SPAN + 2 * CELLS)


def model_body(log_mass, speed, below, above, speed_sq, s0, s1, s2, twice, wide, speed_near):
    stack_wide(wide, below, log_mass, above, 0)
    stack_near(speed_near, below, speed, above, SPAN + CELLS)
    twice[...] = 2.0 / speed[:, :, 8 : 8 + CELLS, :]
    lane = lanes()

    def visit(row, cell):
        stencil = Stencil(wide, row + 4, cell, lane)
        cut = slice(cell, cell + 8)
        for half in (0, 1):
            value = speed_near[row, half, cut, :]
            scale = time_step_sq * value * value
            speed_sq[row, half, cut, :] = lap_coeffs[1] * scale
            scale = (diff_coeffs[0] * diff_coeffs[0]) * scale
            for direction, out in enumerate((s0, s1, s2)):
                out[row, half, cut, :] = scale * stencil.derivative(direction, half)

    over_near(visit)


def forward_body(place, amount, wide, old, speed_sq, s0, s1, s2, near, new, *edges):
    model = (speed_sq, s0, s1, s2)
    lane = lanes()
    near_step(wide, old, model, lane, near)
    add_source(place, amount[0], 0, near)

    def finish(row, half, cut, value):
        new[row, half, cut, :] = value

    block_step(near, of_wide(wide), model, lane, finish)
    add_source(place, amount[1], 5, new)
    write_wide_edges(new, edges)


def write_pieces(slots, block, pieces, at):
    for turn in range(4):
        slot = pl.multiple_of(slots[turn] * 4, 4)
        for half in (0, 1):
            pieces[turn][:, at : at + CELLS, 128 * half : 128 * half + 128] = block[pl.ds(slot, 4), half]


def turn_body(place, amount, block, *refs):
    halo, refs = refs[:6], refs[6:]
    old, speed_sq, s0, s1, s2, adjoint, later, maps, near, new, adjoint_new, summed = refs[:12]
    edges, wide = refs[12:16], refs[16]
    model = (speed_sq, s0, s1, s2)
    lane = lanes()
    fill_wide(wide, block, halo)
    near_step(wide, old, model, lane, near)
    add_source(place, amount[2], 0, near)

    def finish(row, half, cut, value):
        new[row, half, cut, :] = value

    block_step(near, of_block(block), model, lane, finish)
    add_source(place, amount[3], 5, new)

    def finish_adjoint(row, half, cut, value):
        hits = of_near(maps)(row, half, cut)
        ahead = new[row, half, cut, :]
        value = value + (hits[:, 0:128] * ahead - hits[:, 4 * 128 : 5 * 128])
        adjoint_new[row, half, cut, :] = value
        summed[row, half, cut, :] = value * (
            ahead - 2.0 * of_near(near)(row, half, cut) + block[row, half, cut, :]
        )

    block_step(adjoint, of_block(later), model, lane, finish_adjoint)
    write_wide_edges(adjoint_new, edges)


def adjoint_body(block, *refs):
    halo, refs = refs[:6], refs[6:]
    old, speed_sq, s0, s1, s2, maps, u3, u2, u1, u0, sums = refs[:11]
    near, new, summed, low, high, low_cells, high_cells, wide = refs[11:]
    model = (speed_sq, s0, s1, s2)
    lane = lanes()
    fill_wide(wide, block, halo)
    near_step(wide, old, model, lane, near, injected(maps, 3, u3))

    def finish(row, half, cut, value):
        hits = of_near(maps)(row, half, cut)
        third = of_near(u3)(row, half, cut)
        second = u2[row, half, cut, :]
        first = of_near(u1)(row, half, cut)
        zeroth = of_wide(u0)(row, half, cut)
        value = value + (hits[:, 0:128] * second - hits[:, 2 * 128 : 3 * 128])
        new[row, half, cut, :] = value
        total = sums[row, half, cut, :]
        total = total + of_near(near)(row, half, cut) * (third - 2.0 * second + first)
        summed[row, half, cut, :] = total + value * (second - 2.0 * first + zeroth)

    block_step(near, of_block(block), model, lane, finish)
    low[...] = new[0:4]
    high[...] = new[ROWS - 4 : ROWS]
    low_cells[...] = new[:, :, 0:8, :]
    high_cells[...] = new[:, :, CELLS - 8 : CELLS, :]


def last_body(
    slots, model_slots, block, below, above, left, right, old, speed_sq, s0, s1, s2, maps,
    u1, u0, u_before, sums, twice, u4, p0, p1, p2, p3, q0, q1, q2, q3, near, new, image,
):
    near[0:4, :, 8 : 8 + CELLS, :] = below[...]
    near[4 : 4 + ROWS, :, 8 : 8 + CELLS, :] = block[...]
    near[4 + ROWS : 8 + ROWS, :, 8 : 8 + CELLS, :] = above[...]
    near[4 : 4 + ROWS, :, 0:8, :] = left[...]
    near[4 : 4 + ROWS, :, 8 + CELLS : SPAN, :] = right[...]
    lane = lanes()

    def finish(row, half, cut, value):
        hits = of_near(maps)(row, half, cut)
        first = of_near(u1)(row, half, cut)
        value = value + (hits[:, 0:128] * first - hits[:, 128:256])
        new[row, half, cut, :] = value
        curvature = first - 2.0 * of_wide(u0)(row, half, cut) + of_near(u_before)(row, half, cut)
        image[row, half, cut, :] = twice[row, half, cut, :] * (sums[row, half, cut, :] + value * curvature)

    block_step(near, of_near(old), (speed_sq, s0, s1, s2), lane, finish)
    write_pieces(model_slots, image, (p0, p1, p2, p3), 0)
    write_pieces(slots, new, (q0, q1, q2, q3), 0)
    write_pieces(slots, u4, (q0, q1, q2, q3), CELLS)


def spread_body(chunks, p0, p1, p2, p3, *outs):
    for turn, piece in enumerate((p0, p1, p2, p3)):
        first = pl.multiple_of(chunks[turn] * CELLS, CELLS)
        for index, out in enumerate(outs):
            out[:, pl.ds(first, CELLS), :] = piece[:, CELLS * index : CELLS * index + CELLS, :]


def sent_pieces(pieces):
    return [pieces[0]] + [send_y(pieces[turn], turn) for turn in (1, 2, 3)]


def to_slabs(pieces, chunks, count):
    return call(spread_body, [shape(4, NY, NZ)] * count, 1, (chunks, *pieces))


def on_device(
    velocity,
    density,
    aperture_start,
    source_cell,
    receiver_cells,
    wavelet,
    observed,
    forward_old,
    forward_now,
    adjoint_later,
    adjoint_now,
):
    shot = lax.axis_index("shot")
    sub = lax.axis_index("sub")
    core = shot % 2
    x_hi = sub // 16
    x = 2 * x_hi + shot // 2
    z = (sub // 4) % 4
    y = sub % 4
    group = sub // 4
    start = aperture_start[0]
    partner = send_core(aperture_start)

    def wanted(first_slab):
        upper = first_slab // 4 + (y < first_slab % 4).astype(jnp.int32)
        block = jnp.clip(x_hi + (upper - z + 3) // 4, 0, 7)
        position = 2 * (block % 2) + block // 4
        return (block // 2) % 2, (position - x) % 4, upper % 4

    own_core, own_step, turn_by = wanted(start)
    turns = jnp.arange(4, dtype=jnp.int32)
    chunks_out = (y + turns) % 4
    chunks_in = (y - turns) % 4
    slots_in = (y - turns - start % 4) % 4
    slots_out = (y + turns - start % 4) % 4

    pieces = cut_pieces(
        [forward_now[0], forward_old[0], adjoint_now[0], adjoint_later[0]],
        (True, True, True, False),
        chunks_out,
    )
    pair_core, pair_step, _ = wanted(partner[0])

    def gathered(slab, *others):
        from_below = send_x(slab, 1)
        from_above = send_x(slab, -1)
        passing = from_below[0:2], from_above[2:4]
        if others:
            first, second, from_below, from_above, *others = lax.optimization_barrier(
                (*passing, from_below, from_above, *others)
            )
            passing = first, second
        far = jnp.concatenate([send_x(passing[0], 1), send_x(passing[1], -1)])

        def pick(step):
            return jnp.where(
                step < 2, jnp.where(step == 0, slab, from_above), jnp.where(step == 2, far, from_below)
            )

        other = send_core(pick(pair_step))
        return jnp.where(own_core == core, pick(own_step), other), *others

    def turned(arrays, steps, then=tuple):
        def branch(count):
            return lambda *values: then([send_z(value, count) if count else value for value in values])

        return lax.switch(steps, [branch(count) for count in (0, 1, 2, -1)], *arrays)

    log_slab, *pieces = gathered(jnp.log(density), *pieces)
    (speed_slab,) = gathered(velocity)
    pieces = sent_pieces(pieces)

    def local_place(cells, rows_more, cells_more):
        rows = cells // (NY * NZ) - group * ROWS + rows_more
        columns = (cells // NZ) % NY - y * CELLS + cells_more
        inside = (rows >= 0) & (rows < ROWS + 2 * rows_more)
        inside = inside & (columns >= 0) & (columns < CELLS + 2 * cells_more)
        return inside, rows, (cells // 128) % 2, columns, cells % 128

    inside, rows, half, columns, lane = local_place(receiver_cells[0], 4, 8)
    line = jnp.where(inside, (rows * 2 + half) * SPAN + columns, -1)
    lines = (ROWS + 8) * 2 * SPAN
    on_line = (jnp.arange(lines, dtype=jnp.int32)[:, None] == line[None, :]).astype(F32)
    weights = jnp.concatenate([jnp.ones_like(observed[0, :1]), observed[0]])
    hit = lane[:, None, None] == jnp.arange(128, dtype=jnp.int32)[None, None, :]
    at_lane = jnp.where(hit, weights.T[:, :, None], 0.0).reshape(-1, 5 * 128)
    maps = jnp.dot(on_line, at_lane, precision=lax.Precision.HIGHEST)
    maps = maps.reshape(ROWS + 8, 2, SPAN, 5 * 128)

    def source_place(rows_more, cells_more):
        inside, rows, half, columns, lane = local_place(source_cell[0], rows_more, cells_more)
        rows = jnp.clip(rows, 0, ROWS + 2 * rows_more - 1)
        return [inside.astype(jnp.int32), rows, half, columns, lane]

    place = jnp.stack(source_place(4, 8) + source_place(0, 0))
    amount = wavelet[0]

    log_slab, speed_slab = lax.optimization_barrier((log_slab, speed_slab))
    model_pieces = turned(
        (log_slab, speed_slab),
        (4 - turn_by) % 4,
        lambda slabs: tuple(cut_pieces(slabs, (True, True), chunks_out)),
    )
    rest = lax.optimization_barrier((*model_pieces, *pieces))
    model_pieces, pieces = sent_pieces(rest[:4]), rest[4:]
    now, old, adjoint, a_later, side_low, side_high = gather_blocks(pieces, chunks_in, (8, 4, 4, 0))
    below, above = send_group(side_high, 1), send_group(side_low, -1)
    u_wide, old_near, a_near = call(
        fields_body, [WIDE, NEAR, NEAR], 0, (now, old, adjoint, below, above)
    )
    log_mass, speed, side_low, side_high = gather_blocks(model_pieces, slots_in, (8, 4))
    below, above = send_group(side_high, 1), send_group(side_low, -1)
    below, above, maps = lax.optimization_barrier((below, above, maps))
    *model, twice = call(
        model_body, [NEAR] * 4 + [BLOCK], 0, (log_mass, speed, below, above), (WIDE, NEAR)
    )

    u1, u2, *edges = call(
        forward_body, [NEAR, BLOCK] + WIDE_EDGES, 2, (place, amount, u_wide, old_near, *model)
    )
    halo = swap_wide_edges(edges)
    u3, u4, a3, sums, *edges = call(
        turn_body,
        [NEAR, BLOCK, BLOCK, BLOCK] + WIDE_EDGES,
        2,
        (place, amount, u2, *halo, u1, *model, a_near, a_later, maps),
        (WIDE,),
    )
    halo = swap_wide_edges(edges)
    a2, a1, sums, side_low, side_high, low_cells, high_cells = call(
        adjoint_body,
        [NEAR, BLOCK, BLOCK] + [region(4, CELLS)] * 2 + [region(ROWS, 8)] * 2,
        0,
        (a3, *halo, a_near, *model, maps, u3, u2, u1, u_wide, sums),
        (WIDE,),
    )
    halo = (
        send_group(side_high, 1),
        send_group(side_low, -1),
        send_cells(high_cells, 1),
        send_cells(low_cells, -1),
    )
    pieces = call(
        last_body,
        [shape(4, CELLS, NZ)] * 4 + [shape(4, 2 * CELLS, NZ)] * 4,
        2,
        (chunks_out, slots_out, a1, *halo, a2, *model, maps, u1, u_wide, old_near, sums, twice, u4),
        (NEAR, BLOCK, BLOCK),
    )
    pieces = lax.optimization_barrier((*sent_pieces(pieces[:4]), *pieces[4:]))
    (image,) = to_slabs(pieces[:4], chunks_in, 1)

    def both(first_half, second_half):
        return jnp.concatenate([first_half, second_half])

    (image,) = turned((image,), turn_by)
    image, *pieces = lax.optimization_barrier((image, *sent_pieces(pieces[4:])))
    adjoint_first, forward_last = to_slabs(pieces, chunks_in, 2)
    other = send_core(image)

    def share(step):
        mine = jnp.where((own_core == core) & (own_step == step), image, 0.0)
        return mine + jnp.where((pair_core == core) & (pair_step == step), other, 0.0)

    far = share(2)
    passing_up = send_x(far[0:2], 1)
    passing_down = send_x(far[2:4], -1)
    up = share(1)
    down = share(3)
    up = send_x(both(up[0:2] + passing_up, up[2:4]), 1)
    down = send_x(both(down[0:2], down[2:4] + passing_down), -1)
    gradient = share(0) + up + down
    return (gradient, forward_last[None], adjoint_first[None])


def solution(mesh):
    placed = (
        P(("shot", "sub"), None, None),
        P(("shot", "sub"), None, None),
        P("shot"),
        P("shot"),
        P("shot", None),
        P("shot", None),
        P("shot", None, None),
        P("shot", "sub", None, None),
        P("shot", "sub", None, None),
        P("shot", "sub", None, None),
        P("shot", "sub", None, None),
    )
    return jax.shard_map(
        on_device,
        mesh=mesh,
        in_specs=placed,
        out_specs=(
            P(("shot", "sub"), None, None),
            P("shot", "sub", None, None),
            P("shot", "sub", None, None),
        ),
        check_vma=False,
    )
```

```python
import functools

import jax
import jax.numpy as jnp
from jax import lax
from jax.experimental import pallas as pl
from jax.experimental.pallas import tpu as pltpu
from jax.sharding import PartitionSpec as P

lap_coeffs = (-205.0 / 72.0, 8.0 / 5.0, -1.0 / 5.0, 8.0 / 315.0, -1.0 / 560.0)
diff_coeffs = (4.0 / 5.0, -1.0 / 5.0, 4.0 / 105.0, -1.0 / 280.0)
time_step_sq = 0.0088

ROWS = 16
CELLS = 32
SPAN = CELLS + 16
NY = 128
NZ = 256
F32 = jnp.float32
LIMIT = 24 * 2**20


def pairs_by(move):
    pairs = []
    for shot in range(4):
        for sub in range(32):
            x = 2 * (sub // 16) + shot // 2
            target = move(x, shot % 2, (sub // 4) % 4, sub % 4)
            if target is None:
                continue
            tx, tcore, tz, ty = target
            pairs.append((shot * 32 + sub, ((tx % 2) * 2 + tcore) * 32 + (tx // 2) * 16 + tz * 4 + ty))
    return pairs


def send(value, move):
    return lax.ppermute(value, ("shot", "sub"), pairs_by(move))


def send_x(value, steps):
    return send(value, lambda x, c, z, y: ((x + steps) % 4, c, z, y))


def send_core(value):
    return send(value, lambda x, c, z, y: (x, 1 - c, z, y))


def send_z(value, steps):
    return send(value, lambda x, c, z, y: (x, c, (z + steps) % 4, y))


def send_y(value, steps):
    return send(value, lambda x, c, z, y: (x, c, z, (y + steps) % 4))


def next_rows(x, z, steps):
    group = (x // 2) * 4 + z + steps
    if group < 0 or group > 7:
        return None
    return (2 * (group // 4) + x % 2, group % 4)


def send_group(value, steps):
    def move(x, c, z, y):
        place = next_rows(x, z, steps)
        return None if place is None else (place[0], c, place[1], y)

    return send(value, move)


def send_cells(value, steps):
    return send(value, lambda x, c, z, y: (x, c, z, y + steps) if 0 <= y + steps < 4 else None)


def shape(*sizes):
    return jax.ShapeDtypeStruct(sizes, F32)


def region(rows, cells):
    return shape(rows, 2, cells, 128)


BLOCK = region(ROWS, CELLS)
NEAR = region(ROWS + 8, SPAN)
WIDE = region(ROWS + 16, SPAN)


def call(body, outs, n_smem, operands, scratch=()):
    specs = [pl.BlockSpec(memory_space=pltpu.SMEM)] * n_smem
    specs += [pl.BlockSpec(memory_space=pltpu.VMEM)] * (len(operands) - n_smem)
    return pl.pallas_call(
        body,
        out_shape=tuple(outs),
        in_specs=specs,
        out_specs=tuple(pl.BlockSpec(memory_space=pltpu.VMEM) for _ in outs),
        scratch_shapes=[pltpu.VMEM(s.shape, s.dtype) for s in scratch],
        compiler_params=pltpu.CompilerParams(vmem_limit_bytes=LIMIT),
    )(*operands)


def lanes():
    return lax.broadcasted_iota(jnp.int32, (8, 128), 1)


class Stencil:
    def __init__(self, source, row, cell, lane):
        self.source, self.row, self.cell, self.lane = source, row, cell, lane
        self.center = [self.load(0, 0, half) for half in (0, 1)]
        low, high = self.center
        self.deep = []
        for reach in range(1, 5):
            ahead = [pltpu.roll(v, 128 - reach, 1) for v in (low, high)]
            behind = [pltpu.roll(v, reach, 1) for v in (low, high)]
            front = lane < 128 - reach
            back = lane >= reach
            self.deep.append(
                (
                    (jnp.where(front, ahead[0], ahead[1]), jnp.where(front, ahead[1], 0.0)),
                    (jnp.where(back, behind[0], 0.0), jnp.where(back, behind[1], behind[0])),
                )
            )

    def load(self, rows, cells, half):
        first = self.cell + cells
        return self.source[self.row + rows, half, first : first + 8, :]

    def both(self, direction, reach, half):
        if direction == 0:
            return self.load(reach, 0, half), self.load(-reach, 0, half)
        if direction == 1:
            return self.load(0, reach, half), self.load(0, -reach, half)
        ahead, behind = self.deep[reach - 1]
        return ahead[half], behind[half]

    def derivative(self, direction, half):
        ahead, behind = self.both(direction, 1, half)
        total = ahead - behind
        for reach in range(2, 5):
            ahead, behind = self.both(direction, reach, half)
            total = total + (diff_coeffs[reach - 1] / diff_coeffs[0]) * (ahead - behind)
        return total

    def advanced(self, half, previous, speed_sq, slopes):
        center = self.center[half]
        lap = (3.0 * lap_coeffs[0] / lap_coeffs[1]) * center
        derived = [None, None, None]
        for reach in range(1, 5):
            around = None
            for direction in range(3):
                ahead, behind = self.both(direction, reach, half)
                pair = ahead + behind
                around = pair if around is None else around + pair
                part = ahead - behind
                if reach > 1:
                    part = derived[direction] + (diff_coeffs[reach - 1] / diff_coeffs[0]) * part
                derived[direction] = part
            if reach > 1:
                around = (lap_coeffs[reach] / lap_coeffs[1]) * around
            lap = lap + around
        result = 2.0 * center - previous + speed_sq * lap
        for direction in range(3):
            result = result - slopes[direction] * derived[direction]
        return result


def row_pairs(visit, first, last, cells):
    def step(pair, carry):
        for row in (first + 2 * pair, first + 2 * pair + 1):
            for cell in cells:
                visit(row, cell)
        return carry

    lax.fori_loop(0, (last - first) // 2, step, 0)


def over_block(visit):
    row_pairs(visit, 0, ROWS, range(0, CELLS, 8))


def over_near(visit):
    sides, middle = range(8, 8 + CELLS, 8), range(4, 12 + CELLS, 8)
    row_pairs(visit, 0, 4, sides)
    row_pairs(visit, 4, 4 + ROWS, middle)
    row_pairs(visit, 4 + ROWS, 8 + ROWS, sides)


def add_source(place, amount, first, target):
    @pl.when(place[first] > 0)
    def _():
        row, half = place[first + 1], place[first + 2]
        values = target[row, half]
        cell = lax.broadcasted_iota(jnp.int32, values.shape, 0)
        lane = lax.broadcasted_iota(jnp.int32, values.shape, 1)
        hit = (cell == place[first + 3]) & (lane == place[first + 4])
        target[row, half] = values + jnp.where(hit, amount, 0.0)


def near_step(source, old, model, lane, out, extra=None):
    speed_sq, slopes = model[0], model[1:]

    def visit(row, cell):
        stencil = Stencil(source, row + 4, cell, lane)
        cut = slice(cell, cell + 8)
        for half in (0, 1):
            value = stencil.advanced(
                half,
                old[row, half, cut, :],
                speed_sq[row, half, cut, :],
                [s[row, half, cut, :] for s in slopes],
            )
            if extra is not None:
                value = value + extra(row, half, cut)
            out[row, half, cut, :] = value

    over_near(visit)


def block_step(source, old, model, lane, finish):
    speed_sq, slopes = model[0], model[1:]

    def visit(row, cell):
        stencil = Stencil(source, row + 4, cell + 8, lane)
        near = slice(cell + 8, cell + 16)
        for half in (0, 1):
            value = stencil.advanced(
                half,
                old(row, half, slice(cell, cell + 8)),
                speed_sq[row + 4, half, near, :],
                [s[row + 4, half, near, :] for s in slopes],
            )
            finish(row, half, slice(cell, cell + 8), value)

    over_block(visit)


def of_block(ref):
    return lambda row, half, cut: ref[row, half, cut, :]


def of_near(ref):
    return lambda row, half, cut: ref[row + 4, half, cut.start + 8 : cut.stop + 8, :]


def of_wide(ref):
    return lambda row, half, cut: ref[row + 8, half, cut.start + 8 : cut.stop + 8, :]


def injected(maps, index, field):
    def near(row, half, cut):
        hits = maps[row, half, cut, 0:128]
        seen = maps[row, half, cut, 128 * index : 128 * index + 128]
        return hits * field[row, half, cut, :] - seen

    return near


def fill_wide(wide, block, halo):
    below, above, left, right, left_corners, right_corners = halo
    wide[0:8, :, 8 : 8 + CELLS, :] = below[...]
    wide[8 : 8 + ROWS, :, 8 : 8 + CELLS, :] = block[...]
    wide[8 + ROWS : 16 + ROWS, :, 8 : 8 + CELLS, :] = above[...]
    for cells, side, corners in (
        (slice(0, 8), left, left_corners),
        (slice(8 + CELLS, SPAN), right, right_corners),
    ):
        wide[4:8, :, cells, :] = corners[0:4]
        wide[8 : 8 + ROWS, :, cells, :] = side[...]
        wide[8 + ROWS : 12 + ROWS, :, cells, :] = corners[4:8]


WIDE_EDGES = [region(8, CELLS)] * 2 + [region(ROWS, 8)] * 2


def write_wide_edges(block, edges):
    low, high, low_cells, high_cells = edges
    low[...] = block[0:8]
    high[...] = block[ROWS - 8 : ROWS]
    low_cells[...] = block[:, :, 0:8, :]
    high_cells[...] = block[:, :, CELLS - 8 : CELLS, :]


def rim_body(below, above, low, high):
    for out, cut in ((low, slice(0, 8)), (high, slice(CELLS - 8, CELLS))):
        out[0:4] = below[4:8, :, cut, :]
        out[4:8] = above[0:4, :, cut, :]


def swap_wide_edges(edges):
    low, high, low_cells, high_cells = edges
    below, above = send_group(high, 1), send_group(low, -1)
    left, right = send_cells(high_cells, 1), send_cells(low_cells, -1)
    low_corners, high_corners = call(rim_body, [region(8, 8)] * 2, 0, (below, above))
    return below, above, left, right, send_cells(high_corners, 1), send_cells(low_corners, -1)


def cut_body(chunks, *refs, margins):
    count = len(margins)
    slabs, pieces = refs[:count], refs[count:]
    for turn in range(4):
        chunk = chunks[turn]
        first = pl.multiple_of(chunk * CELLS, CELLS)
        before = pl.multiple_of(jnp.maximum(first - 8, 0), 8)
        after = pl.multiple_of(jnp.minimum(first + CELLS, NY - 8), 8)
        at = 0
        for slab, margin in zip(slabs, margins):
            if margin:
                pieces[turn][:, at : at + 8, :] = jnp.where(chunk > 0, slab[:, pl.ds(before, 8), :], 0.0)
                at += 8
            pieces[turn][:, at : at + CELLS, :] = slab[:, pl.ds(first, CELLS), :]
            at += CELLS
            if margin:
                pieces[turn][:, at : at + 8, :] = jnp.where(chunk < 3, slab[:, pl.ds(after, 8), :], 0.0)
                at += 8


def cut_pieces(slabs, margins, chunks):
    width = sum(SPAN if margin else CELLS for margin in margins)
    pieces = call(functools.partial(cut_body, margins=margins), [shape(4, width, NZ)] * 4, 1, (chunks, *slabs))
    return pieces


def place_pieces(slots, pieces, outs):
    for turn in range(4):
        slot = pl.multiple_of(slots[turn] * 4, 4)
        at = 0
        for out in outs:
            width = out.shape[2]
            for half in (0, 1):
                out[pl.ds(slot, 4), half] = pieces[turn][:, at : at + width, 128 * half : 128 * half + 128]
            at += width


def gather_body(slots, *refs, depths):
    pieces, outs = refs[:4], refs[4:]
    low, high = outs[-2:]
    place_pieces(slots, pieces, outs[:-2])
    at = 0
    core = slice(8, 8 + CELLS)
    for out, depth in zip(outs, depths):
        if depth == 8:
            low[:, :, at : at + SPAN, :] = out[0:4]
            high[:, :, at : at + SPAN, :] = out[ROWS - 4 : ROWS]
            at += SPAN
            low[:, :, at : at + CELLS, :] = out[4:8, :, core, :]
            high[:, :, at : at + CELLS, :] = out[ROWS - 8 : ROWS - 4, :, core, :]
            at += CELLS
        elif depth == 4:
            low[:, :, at : at + CELLS, :] = out[0:4, :, core, :]
            high[:, :, at : at + CELLS, :] = out[ROWS - 4 : ROWS, :, core, :]
            at += CELLS


def gather_blocks(pieces, slots, depths):
    outs = [region(ROWS, SPAN if depth else CELLS) for depth in depths]
    packed = sum({8: SPAN + CELLS, 4: CELLS, 0: 0}[depth] for depth in depths)
    outs += [region(4, packed)] * 2
    return call(functools.partial(gather_body, depths=depths), outs, 1, (slots, *pieces))


def stack_wide(out, below, middle, above, at):
    core = slice(8, 8 + CELLS)
    end = at + SPAN + CELLS
    out[0:4, :, core, :] = below[:, :, at + SPAN : end, :]
    out[4:8] = below[:, :, at : at + SPAN, :]
    out[8 : 8 + ROWS] = middle[...]
    out[8 + ROWS : 12 + ROWS] = above[:, :, at : at + SPAN, :]
    out[12 + ROWS : 16 + ROWS, :, core, :] = above[:, :, at + SPAN : end, :]


def stack_near(out, below, middle, above, at):
    core = slice(8, 8 + CELLS)
    out[0:4, :, core, :] = below[:, :, at : at + CELLS, :]
    out[4 : 4 + ROWS] = middle[...]
    out[4 + ROWS : 8 + ROWS, :, core, :] = above[:, :, at : at + CELLS, :]


def fields_body(now, old, adjoint, below, above, wide, old_near, adjoint_near):
    stack_wide(wide, below, now, above, 0)
    stack_near(old_near, below, old, above, SPAN + CELLS)
    stack_near(adjoint_near, below, adjoint, above, SPAN + 2 * CELLS)


def model_body(log_mass, speed, below, above, speed_sq, s0, s1, s2, twice, wide, speed_near):
    stack_wide(wide, below, log_mass, above, 0)
    stack_near(speed_near, below, speed, above, SPAN + CELLS)
    twice[...] = 2.0 / speed[:, :, 8 : 8 + CELLS, :]
    lane = lanes()

    def visit(row, cell):
        stencil = Stencil(wide, row + 4, cell, lane)
        cut = slice(cell, cell + 8)
        for half in (0, 1):
            value = speed_near[row, half, cut, :]
            scale = time_step_sq * value * value
            speed_sq[row, half, cut, :] = lap_coeffs[1] * scale
            scale = (diff_coeffs[0] * diff_coeffs[0]) * scale
            for direction, out in enumerate((s0, s1, s2)):
                out[row, half, cut, :] = scale * stencil.derivative(direction, half)

    over_near(visit)


def forward_body(place, amount, wide, old, speed_sq, s0, s1, s2, near, new, *edges):
    model = (speed_sq, s0, s1, s2)
    lane = lanes()
    near_step(wide, old, model, lane, near)
    add_source(place, amount[0], 0, near)

    def finish(row, half, cut, value):
        new[row, half, cut, :] = value

    block_step(near, of_wide(wide), model, lane, finish)
    add_source(place, amount[1], 5, new)
    write_wide_edges(new, edges)


def write_pieces(slots, block, pieces, at):
    for turn in range(4):
        slot = pl.multiple_of(slots[turn] * 4, 4)
        for half in (0, 1):
            pieces[turn][:, at : at + CELLS, 128 * half : 128 * half + 128] = block[pl.ds(slot, 4), half]


def turn_body(place, amount, block, *refs):
    halo, refs = refs[:6], refs[6:]
    old, speed_sq, s0, s1, s2, adjoint, later, maps, near, new, adjoint_new, summed = refs[:12]
    edges, wide = refs[12:16], refs[16]
    model = (speed_sq, s0, s1, s2)
    lane = lanes()
    fill_wide(wide, block, halo)
    near_step(wide, old, model, lane, near)
    add_source(place, amount[2], 0, near)

    def finish(row, half, cut, value):
        new[row, half, cut, :] = value

    block_step(near, of_block(block), model, lane, finish)
    add_source(place, amount[3], 5, new)

    def finish_adjoint(row, half, cut, value):
        hits = of_near(maps)(row, half, cut)
        ahead = new[row, half, cut, :]
        value = value + (hits[:, 0:128] * ahead - hits[:, 4 * 128 : 5 * 128])
        adjoint_new[row, half, cut, :] = value
        summed[row, half, cut, :] = value * (
            ahead - 2.0 * of_near(near)(row, half, cut) + block[row, half, cut, :]
        )

    block_step(adjoint, of_block(later), model, lane, finish_adjoint)
    write_wide_edges(adjoint_new, edges)


def adjoint_body(block, *refs):
    halo, refs = refs[:6], refs[6:]
    old, speed_sq, s0, s1, s2, maps, u3, u2, u1, u0, sums = refs[:11]
    near, new, summed, low, high, low_cells, high_cells, wide = refs[11:]
    model = (speed_sq, s0, s1, s2)
    lane = lanes()
    fill_wide(wide, block, halo)
    near_step(wide, old, model, lane, near, injected(maps, 3, u3))

    def finish(row, half, cut, value):
        hits = of_near(maps)(row, half, cut)
        third = of_near(u3)(row, half, cut)
        second = u2[row, half, cut, :]
        first = of_near(u1)(row, half, cut)
        zeroth = of_wide(u0)(row, half, cut)
        value = value + (hits[:, 0:128] * second - hits[:, 2 * 128 : 3 * 128])
        new[row, half, cut, :] = value
        total = sums[row, half, cut, :]
        total = total + of_near(near)(row, half, cut) * (third - 2.0 * second + first)
        summed[row, half, cut, :] = total + value * (second - 2.0 * first + zeroth)

    block_step(near, of_block(block), model, lane, finish)
    low[...] = new[0:4]
    high[...] = new[ROWS - 4 : ROWS]
    low_cells[...] = new[:, :, 0:8, :]
    high_cells[...] = new[:, :, CELLS - 8 : CELLS, :]


def last_body(
    slots, model_slots, block, below, above, left, right, old, speed_sq, s0, s1, s2, maps,
    u1, u0, u_before, sums, twice, u4, p0, p1, p2, p3, q0, q1, q2, q3, near, new, image,
):
    near[0:4, :, 8 : 8 + CELLS, :] = below[...]
    near[4 : 4 + ROWS, :, 8 : 8 + CELLS, :] = block[...]
    near[4 + ROWS : 8 + ROWS, :, 8 : 8 + CELLS, :] = above[...]
    near[4 : 4 + ROWS, :, 0:8, :] = left[...]
    near[4 : 4 + ROWS, :, 8 + CELLS : SPAN, :] = right[...]
    lane = lanes()

    def finish(row, half, cut, value):
        hits = of_near(maps)(row, half, cut)
        first = of_near(u1)(row, half, cut)
        value = value + (hits[:, 0:128] * first - hits[:, 128:256])
        new[row, half, cut, :] = value
        curvature = first - 2.0 * of_wide(u0)(row, half, cut) + of_near(u_before)(row, half, cut)
        image[row, half, cut, :] = twice[row, half, cut, :] * (sums[row, half, cut, :] + value * curvature)

    block_step(near, of_near(old), (speed_sq, s0, s1, s2), lane, finish)
    write_pieces(model_slots, image, (p0, p1, p2, p3), 0)
    write_pieces(slots, new, (q0, q1, q2, q3), 0)
    write_pieces(slots, u4, (q0, q1, q2, q3), CELLS)


def spread_body(chunks, p0, p1, p2, p3, *outs):
    for turn, piece in enumerate((p0, p1, p2, p3)):
        first = pl.multiple_of(chunks[turn] * CELLS, CELLS)
        for index, out in enumerate(outs):
            out[:, pl.ds(first, CELLS), :] = piece[:, CELLS * index : CELLS * index + CELLS, :]


def sent_pieces(pieces):
    return [pieces[0]] + [send_y(pieces[turn], turn) for turn in (1, 2, 3)]


def to_slabs(pieces, chunks, count):
    return call(spread_body, [shape(4, NY, NZ)] * count, 1, (chunks, *pieces))


def on_device(
    velocity,
    density,
    aperture_start,
    source_cell,
    receiver_cells,
    wavelet,
    observed,
    forward_old,
    forward_now,
    adjoint_later,
    adjoint_now,
):
    shot = lax.axis_index("shot")
    sub = lax.axis_index("sub")
    core = shot % 2
    x_hi = sub // 16
    x = 2 * x_hi + shot // 2
    z = (sub // 4) % 4
    y = sub % 4
    group = sub // 4
    start = aperture_start[0]
    partner = send_core(aperture_start)

    def wanted(first_slab):
        upper = first_slab // 4 + (y < first_slab % 4).astype(jnp.int32)
        block = jnp.clip(x_hi + (upper - z + 3) // 4, 0, 7)
        position = 2 * (block % 2) + block // 4
        return (block // 2) % 2, (position - x) % 4, upper % 4

    own_core, own_step, turn_by = wanted(start)
    turns = jnp.arange(4, dtype=jnp.int32)
    chunks_out = (y + turns) % 4
    chunks_in = (y - turns) % 4
    slots_in = (y - turns - start % 4) % 4
    slots_out = (y + turns - start % 4) % 4

    pieces = cut_pieces(
        [forward_now[0], forward_old[0], adjoint_now[0], adjoint_later[0]],
        (True, True, True, False),
        chunks_out,
    )
    pair_core, pair_step, _ = wanted(partner[0])

    def gathered(slab, *others):
        from_below = send_x(slab, 1)
        from_above = send_x(slab, -1)
        passing = from_below[0:2], from_above[2:4]
        if others:
            first, second, from_below, from_above, *others = lax.optimization_barrier(
                (*passing, from_below, from_above, *others)
            )
            passing = first, second
        far = jnp.concatenate([send_x(passing[0], 1), send_x(passing[1], -1)])

        def pick(step):
            return jnp.where(
                step < 2, jnp.where(step == 0, slab, from_above), jnp.where(step == 2, far, from_below)
            )

        other = send_core(pick(pair_step))
        return jnp.where(own_core == core, pick(own_step), other), *others

    def turned(arrays, steps, then=tuple):
        def branch(count):
            return lambda *values: then([send_z(value, count) if count else value for value in values])

        return lax.switch(steps, [branch(count) for count in (0, 1, 2, -1)], *arrays)

    log_slab, *pieces = gathered(jnp.log(density), *pieces)
    (speed_slab,) = gathered(velocity)
    pieces = sent_pieces(pieces)

    def local_place(cells, rows_more, cells_more):
        rows = cells // (NY * NZ) - group * ROWS + rows_more
        columns = (cells // NZ) % NY - y * CELLS + cells_more
        inside = (rows >= 0) & (rows < ROWS + 2 * rows_more)
        inside = inside & (columns >= 0) & (columns < CELLS + 2 * cells_more)
        return inside, rows, (cells // 128) % 2, columns, cells % 128

    inside, rows, half, columns, lane = local_place(receiver_cells[0], 4, 8)
    line = jnp.where(inside, (rows * 2 + half) * SPAN + columns, -1)
    lines = (ROWS + 8) * 2 * SPAN
    on_line = (jnp.arange(lines, dtype=jnp.int32)[:, None] == line[None, :]).astype(F32)
    weights = jnp.concatenate([jnp.ones_like(observed[0, :1]), observed[0]])
    hit = lane[:, None, None] == jnp.arange(128, dtype=jnp.int32)[None, None, :]
    at_lane = jnp.where(hit, weights.T[:, :, None], 0.0).reshape(-1, 5 * 128)
    maps = jnp.dot(on_line, at_lane, precision=lax.Precision.HIGHEST)
    maps = maps.reshape(ROWS + 8, 2, SPAN, 5 * 128)

    def source_place(rows_more, cells_more):
        inside, rows, half, columns, lane = local_place(source_cell[0], rows_more, cells_more)
        rows = jnp.clip(rows, 0, ROWS + 2 * rows_more - 1)
        return [inside.astype(jnp.int32), rows, half, columns, lane]

    place = jnp.stack(source_place(4, 8) + source_place(0, 0))
    amount = wavelet[0]

    log_slab, speed_slab = lax.optimization_barrier((log_slab, speed_slab))
    model_pieces = turned(
        (log_slab, speed_slab),
        (4 - turn_by) % 4,
        lambda slabs: tuple(cut_pieces(slabs, (True, True), chunks_out)),
    )
    rest = lax.optimization_barrier((*model_pieces, *pieces))
    model_pieces, pieces = sent_pieces(rest[:4]), rest[4:]
    now, old, adjoint, a_later, side_low, side_high = gather_blocks(pieces, chunks_in, (8, 4, 4, 0))
    below, above = send_group(side_high, 1), send_group(side_low, -1)
    u_wide, old_near, a_near = call(
        fields_body, [WIDE, NEAR, NEAR], 0, (now, old, adjoint, below, above)
    )
    log_mass, speed, side_low, side_high = gather_blocks(model_pieces, slots_in, (8, 4))
    below, above = send_group(side_high, 1), send_group(side_low, -1)
    below, above, maps = lax.optimization_barrier((below, above, maps))
    *model, twice = call(
        model_body, [NEAR] * 4 + [BLOCK], 0, (log_mass, speed, below, above), (WIDE, NEAR)
    )

    u1, u2, *edges = call(
        forward_body, [NEAR, BLOCK] + WIDE_EDGES, 2, (place, amount, u_wide, old_near, *model)
    )
    halo = swap_wide_edges(edges)
    u3, u4, a3, sums, *edges = call(
        turn_body,
        [NEAR, BLOCK, BLOCK, BLOCK] + WIDE_EDGES,
        2,
        (place, amount, u2, *halo, u1, *model, a_near, a_later, maps),
        (WIDE,),
    )
    halo = swap_wide_edges(edges)
    a2, a1, sums, side_low, side_high, low_cells, high_cells = call(
        adjoint_body,
        [NEAR, BLOCK, BLOCK] + [region(4, CELLS)] * 2 + [region(ROWS, 8)] * 2,
        0,
        (a3, *halo, a_near, *model, maps, u3, u2, u1, u_wide, sums),
        (WIDE,),
    )
    halo = (
        send_group(side_high, 1),
        send_group(side_low, -1),
        send_cells(high_cells, 1),
        send_cells(low_cells, -1),
    )
    pieces = call(
        last_body,
        [shape(4, CELLS, NZ)] * 4 + [shape(4, 2 * CELLS, NZ)] * 4,
        2,
        (chunks_out, slots_out, a1, *halo, a2, *model, maps, u1, u_wide, old_near, sums, twice, u4),
        (NEAR, BLOCK, BLOCK),
    )
    pieces = lax.optimization_barrier((*sent_pieces(pieces[:4]), *pieces[4:]))
    (image,) = to_slabs(pieces[:4], chunks_in, 1)

    def both(first_half, second_half):
        return jnp.concatenate([first_half, second_half])

    (image,) = turned((image,), turn_by)
    image, *pieces = lax.optimization_barrier((image, *pieces[4:]))
    other = send_core(image)

    def share(step):
        mine = jnp.where((own_core == core) & (own_step == step), image, 0.0)
        return mine + jnp.where((pair_core == core) & (pair_step == step), other, 0.0)

    far = share(2)
    passing_up = send_x(far[0:2], 1)
    passing_down = send_x(far[2:4], -1)
    passing_up, passing_down, *pieces = lax.optimization_barrier(
        (passing_up, passing_down, *sent_pieces(pieces))
    )
    adjoint_first, forward_last = to_slabs(pieces, chunks_in, 2)
    up = share(1)
    down = share(3)
    up = send_x(both(up[0:2] + passing_up, up[2:4]), 1)
    down = send_x(both(down[0:2], down[2:4] + passing_down), -1)
    gradient = share(0) + up + down
    return (gradient, forward_last[None], adjoint_first[None])


def solution(mesh):
    placed = (
        P(("shot", "sub"), None, None),
        P(("shot", "sub"), None, None),
        P("shot"),
        P("shot"),
        P("shot", None),
        P("shot", None),
        P("shot", None, None),
        P("shot", "sub", None, None),
        P("shot", "sub", None, None),
        P("shot", "sub", None, None),
        P("shot", "sub", None, None),
    )
    return jax.shard_map(
        on_device,
        mesh=mesh,
        in_specs=placed,
        out_specs=(
            P(("shot", "sub"), None, None),
            P("shot", "sub", None, None),
            P("shot", "sub", None, None),
        ),
        check_vma=False,
    )
```
